32 devices in a mesh: dp: 8 (over z, x), sub: 4 (over y, core).
Axes of the slice: x: 2, y: 2, z: 4, core: 2. Of those that a mesh axis runs over, the one named last changes fastest.
Arguments:
- tokens_in: bfloat16 [32768, 768], P(('dp', 'sub')), may hold values from -6 to 6
- grad_out: bfloat16 [32768, 768], P(('dp', 'sub')), may hold values from -6 to 6
- seq_start: int32 [32768], P(('dp', 'sub')), may hold values from 0 to 960, as said below
- valid: int32 [32768], P(('dp', 'sub')), may hold values from 0 to 1, as said below
- matrices: bfloat16 [55296, 128], P(('dp', 'sub')), may hold values from -0.8164966 to 0.8164966
- vectors: bfloat16 [96, 128], P(('dp', 'sub')), may hold values from -1 to 1.3
Outputs:
- block_out: bfloat16 [32768, 768], P(('dp', 'sub'))
- tokens_grad: float32 [32768, 768], P(('dp', 'sub'))
- matrices_grad: float32 [55296, 128], P(('dp', 'sub'))
- vectors_grad: float32 [96, 128], P(('dp', 'sub'))
The draws below stay inside these ranges and needn't reach their ends.
Inputs may be any that keep to these rules, and one draw needn't show every extreme that they name: Each device's 1024 slots are cut into aligned buckets of one power-of-two size between 64 and 1024 (one size a device); seq_start is the device-local first slot of the bucket that holds the slot. Some device holds a single sequence of 1024 tokens, and some device has buckets of 64 slots. Each bucket holds one sequence in its first slots, longer than half of the bucket and at least 64 tokens; valid marks those slots.
All inputs are finite; a program needn't handle non-finite values.
Results may differ from the reference program's by a relative error of at most 0.0097.
Values may be sent and summed in bfloat16 or wider, within the bound.
No kernel may reach another device: no remote copies, remote signals or barrier semaphores. Data moves between devices by JAX's collectives and lax.ppermute only.
A program may use at most 256 MiB of HBM per device.

```python
import jax
import jax.numpy as jnp
from jax import lax

D = 768
HEADS = 12
HD = 64
FF = 3072
ROWW = 128
SLOTS = 1024
TOKENS = 32768
MROWS = 55296
VROWS = 96


def bucket_layout(key):
    device_total = TOKENS // SLOTS
    base = jax.random.fold_in(key, 11)
    level_key, length_key = jax.random.split(base)
    ladder = jax.random.randint(level_key, (device_total,), 0, 31)
    level = 4 - ((ladder >= 1).astype(jnp.int32) + (ladder >= 3).astype(jnp.int32) + (ladder >= 7).astype(jnp.int32) + (ladder >= 15).astype(jnp.int32))
    level = level.at[0].set(4).at[1].set(0)
    bucket = SLOTS // 16 * jnp.left_shift(jnp.ones_like(level), level)
    slot_index = jnp.arange(SLOTS, dtype=jnp.int32)[None, :]
    owner = slot_index // bucket[:, None]
    starts = owner * bucket[:, None]
    lowest = jnp.maximum(bucket // 2 + 1, SLOTS // 16)
    drawn = jax.random.randint(length_key, (device_total, 16), 0, SLOTS)
    lengths = lowest[:, None] + drawn % (bucket[:, None] - lowest[:, None] + 1)
    lengths = lengths.at[0].set(SLOTS)
    own_length = jnp.take_along_axis(lengths, owner, axis=1)
    live = (slot_index - starts < own_length).astype(jnp.int32)
    return (starts.reshape(-1).astype(jnp.int32), live.reshape(-1))


def draw_seq_start(key, part):
    return bucket_layout(key)[0]


def draw_valid(key, part):
    return bucket_layout(key)[1]


def draw_matrices(key, part):
    element = jnp.arange(MROWS, dtype=jnp.int32)[:, None] * ROWW + jnp.arange(ROWW, dtype=jnp.int32)[None, :]
    normal_part = jnp.clip(jax.random.normal(key, (MROWS, ROWW), jnp.float32), -4.0, 4.0)
    factor = jnp.where(element < 3 * D * D, D ** (-0.5), jnp.where(element < 4 * D * D, (D // 32) ** (-0.5), jnp.where(element < 4 * D * D + D * FF, D ** (-0.5), FF ** (-0.5))))
    return (normal_part * factor).astype(jnp.bfloat16)


def draw_vectors(key, part):
    element = jnp.arange(VROWS, dtype=jnp.int32)[:, None] * ROWW + jnp.arange(ROWW, dtype=jnp.int32)[None, :]
    group = element // D
    spread = jax.random.uniform(key, (VROWS, ROWW), jnp.float32, -1.0, 1.0)
    is_gain = (group == 0) | (group == 2)
    is_bias = (group == 1) | (group == 3)
    values = jnp.where(is_gain, 1.0 + 0.3 * spread, jnp.where(is_bias, 0.5 * spread, spread))
    return values.astype(jnp.bfloat16)


def shard_levels(own_key, extent, cuts, least, largest):
    loudness = 1.0
    for axis_at, parts in cuts:
        steps = jax.random.uniform(jax.random.fold_in(jax.random.fold_in(own_key, 6), axis_at), (parts,), jnp.float32, least / len(cuts), largest / len(cuts))
        loudness = loudness * jnp.repeat(jnp.exp(steps), extent[axis_at] // parts).reshape((-1,) + (1,) * (len(extent) - 1 - axis_at))
    return loudness


def normal_values(key, extent, scale, reach, pieces=(), kind=jnp.bfloat16):
    entries = jax.random.normal(key, extent, jnp.float32) * scale
    if len(pieces) > 0:
        entries = shard_levels(key, extent, pieces, -0.22, 0.18) * entries
    return jnp.clip(entries, min=-reach, max=reach).astype(kind)


def setup_inputs(seed: int = 0) -> dict:
    key_list = jax.random.split(jax.random.key(seed), 7)
    tokens_in = normal_values(key_list[0], (TOKENS, D), 1.0, 6.0, ((0, 32),))
    grad_out = normal_values(key_list[1], (TOKENS, D), 1.0, 6.0, ((0, 32),))
    seq_start = draw_seq_start(jax.random.fold_in(key_list[6], 71), 0)
    valid = draw_valid(jax.random.fold_in(key_list[6], 71), 0)
    matrices = draw_matrices(jax.random.fold_in(key_list[6], 71), 0)
    vectors = draw_vectors(jax.random.fold_in(key_list[6], 71), 0)
    return {"tokens_in": tokens_in, "grad_out": grad_out, "seq_start": seq_start, "valid": valid, "matrices": matrices, "vectors": vectors}


EPSILON = 1e-05
NEG_FILL = -1e+30
HIGH = lax.Precision.HIGHEST

@jax.custom_vjp
def low(v):
    return lax.optimization_barrier(v.astype(jnp.bfloat16)).astype(jnp.float32)

@jax.custom_vjp
def low_back(v):
    return v

def low_keep(v):
    return (low(v), None)

def low_pass(kept, grad):
    return (grad,)

def back_keep(v):
    return (v, None)

def back_low(kept, grad):
    return (low(grad),)
low.defvjp(low_keep, low_pass)
low_back.defvjp(back_keep, back_low)

def layer_norm(inputs, gain_vec, offset):
    centre = inputs - lax.optimization_barrier(jnp.mean(inputs, axis=-1, keepdims=True))
    return centre * lax.rsqrt(lax.optimization_barrier(jnp.mean(centre * centre, axis=-1, keepdims=True)) + EPSILON) * gain_vec + offset

def shifted(values, amount):
    padding = [(0, 0)] * (values.ndim - 2) + [(amount, 0), (0, 0)]
    return jnp.pad(values, padding)[..., :values.shape[-2], :]

def depthwise(values, kernel, first_mask, second_mask):
    one_back = shifted(values, 1) * first_mask
    two_back = shifted(values, 2) * second_mask
    return kernel[:, 0:1, :] * values + kernel[:, 1:2, :] * one_back + kernel[:, 2:3, :] * two_back

def layer_block(weights, activations, starts, live):
    w_qkv, w_out, w_up, w_down, gain_one, bias_one, gain_two, bias_two, kernel = weights
    slot_index = jnp.arange(SLOTS, dtype=jnp.int32)
    position = slot_index - starts
    first_mask = (position >= 1).astype(jnp.float32)[:, None]
    second_mask = (position >= 2).astype(jnp.float32)[:, None]
    normed_one = low(layer_norm(activations, gain_one, bias_one))
    project = low_back(jnp.einsum('td,cde->cte', normed_one, w_qkv, precision=HIGH))
    mixed_all = low(depthwise(project, kernel, first_mask, second_mask))
    queries = mixed_all[0].reshape(SLOTS, HEADS, HD)
    keyset = mixed_all[1].reshape(SLOTS, HEADS, HD)
    valueset = mixed_all[2].reshape(SLOTS, HEADS, HD)
    scores = low_back(jnp.einsum('qhd,khd->hqk', queries, keyset, precision=HIGH) * HD ** (-0.5))
    allowed = (starts[:, None] == starts[None, :]) & (slot_index[None, :] <= slot_index[:, None]) & (live[None, :] == 1)
    masked = jnp.where(allowed[None], scores, NEG_FILL)
    row_peak = lax.optimization_barrier(jnp.max(masked, axis=-1, keepdims=True))
    exp_terms = jnp.exp(masked - row_peak)
    attn_probs = exp_terms / lax.optimization_barrier(jnp.sum(exp_terms, axis=-1, keepdims=True))
    attended = jnp.einsum('hqk,khd->qhd', low(attn_probs), valueset, precision=HIGH).reshape(SLOTS, D)
    attended = low(low_back(attended))
    residual = activations + low_back(jnp.dot(attended, w_out, precision=HIGH))
    normed_two = low(layer_norm(residual, gain_two, bias_two))
    upward = low_back(jnp.dot(normed_two, w_up, precision=HIGH))
    active = low(jnp.square(jnp.maximum(upward, 0.0)))
    return residual + jnp.dot(active, w_down, precision=HIGH)

def reference(tokens_in, grad_out, seq_start, valid, matrices, vectors):
    device_total = TOKENS // SLOTS
    square = D * D
    flat_rows = matrices.astype(jnp.float32).reshape(-1)
    flat_vec = vectors.astype(jnp.float32).reshape(-1)
    params = (flat_rows[:3 * square].reshape(3, D, D), flat_rows[3 * square:4 * square].reshape(D, D), flat_rows[4 * square:4 * square + D * FF].reshape(D, FF), flat_rows[4 * square + D * FF:].reshape(FF, D), flat_vec[:D], flat_vec[D:2 * D], flat_vec[2 * D:3 * D], flat_vec[3 * D:4 * D], flat_vec[4 * D:13 * D].reshape(3, 3, D))
    inputs = tokens_in.astype(jnp.float32).reshape(device_total, SLOTS, D)
    starts = seq_start.reshape(device_total, SLOTS)
    live = valid.reshape(device_total, SLOTS)
    cotangent = (grad_out.astype(jnp.float32) * valid.astype(jnp.float32)[:, None]).reshape(device_total, SLOTS, D)

    def forward(weights, activations):

        def one_block(operands):
            return layer_block(weights, operands[0], operands[1], operands[2])
        return lax.map(jax.checkpoint(one_block), (activations, starts, live))
    outputs, pullback = jax.vjp(forward, params, inputs)
    grad_params, grad_inputs = pullback(cotangent)
    grad_rows = jnp.concatenate([grad_params[0].reshape(-1), grad_params[1].reshape(-1), grad_params[2].reshape(-1), grad_params[3].reshape(-1)]).reshape(MROWS, ROWW)
    grad_vec = jnp.concatenate([grad_params[4], grad_params[5], grad_params[6], grad_params[7], grad_params[8].reshape(-1), jnp.zeros((VROWS * ROWW - 13 * D,), jnp.float32)]).reshape(VROWS, ROWW)
    return (outputs.reshape(TOKENS, D).astype(jnp.bfloat16), grad_inputs.reshape(TOKENS, D), grad_rows, grad_vec)
```

```python
import functools

import jax
import jax.numpy as jnp
from jax import lax
from jax.experimental import pallas as pl
from jax.experimental.pallas import tpu as pltpu
from jax.sharding import PartitionSpec as P

HEADS = 12
EPSILON = 1e-05
NEG_FILL = -1e30
BF = jnp.bfloat16
F32 = jnp.float32
AXES = ("dp", "sub")
VMEM_BYTES = 60 * 1024 * 1024
LANES = 128
BLOCK = 256
GROUP = 96
FOLD = 4


def dot(a, b):
    return jnp.dot(a, b, preferred_element_type=F32)


def dot_nt(a, b):
    return lax.dot_general(a, b, (((1,), (1,)), ((), ())), preferred_element_type=F32)


def dot_tn(a, b):
    return lax.dot_general(a, b, (((0,), (0,)), ((), ())), preferred_element_type=F32)


def whole(shape):
    return pl.BlockSpec(shape, lambda *_: (0,) * len(shape))


def fixed(shape):
    return pl.BlockSpec(shape, lambda *_: (0,) * len(shape), pipeline_mode=pl.Buffered(1))


def call(body, grid, ins, outs, out_shape, scratch, args, flops, moved):
    return pl.pallas_call(
        body,
        grid=grid,
        in_specs=ins,
        out_specs=outs,
        out_shape=out_shape,
        scratch_shapes=scratch,
        compiler_params=pltpu.CompilerParams(
            dimension_semantics=("arbitrary",) * len(grid), vmem_limit_bytes=VMEM_BYTES
        ),
        cost_estimate=pl.CostEstimate(flops=flops, bytes_accessed=moved, transcendentals=0),
    )(*args)


def like(shape, dtype):
    return jax.ShapeDtypeStruct(shape, dtype)


def normalize(v):
    centre = v - jnp.mean(v, axis=-1, keepdims=True)
    scaled = lax.rsqrt(jnp.mean(centre * centre, axis=-1, keepdims=True) + EPSILON)
    return centre * scaled, scaled


def norm_back(incoming, normed, scaled, gain):
    weighted = incoming * gain
    return scaled * (
        weighted
        - jnp.mean(weighted, axis=-1, keepdims=True)
        - normed * jnp.mean(weighted * normed, axis=-1, keepdims=True)
    )


def columns(meta):
    return jnp.transpose(meta, (1, 0))


def mix_masks(meta_ref, slots):
    cols = columns(meta_ref[...])
    position = lax.broadcasted_iota(jnp.int32, (slots, 1), 0).astype(F32) - cols[:, 0:1]
    return jnp.where(position >= 1.0, 1.0, 0.0), jnp.where(position >= 2.0, 1.0, 0.0)


def pre_body(x_ref, w_ref, vec_ref, taps_ref, meta_ref, low_ref, mixed_ref, proj_ref):
    slots = x_ref.shape[0]

    @pl.when(pl.program_id(0) == 0)
    def _():
        for lo in range(0, slots, BLOCK):
            rows = slice(lo, lo + BLOCK)
            normed, _ = normalize(x_ref[rows, :].astype(F32))
            low_ref[rows, :] = (normed * vec_ref[0:1, :] + vec_ref[1:2, :]).astype(BF)

    first, second = mix_masks(meta_ref, slots)
    proj_ref[...] = dot(low_ref[...], w_ref[...])
    value = proj_ref[...]
    one_back = pltpu.roll(value, 1, 0) * first
    two_back = pltpu.roll(value, 2, 0) * second
    mixed_ref[...] = (
        taps_ref[0:1, :] * value + taps_ref[1:2, :] * one_back + taps_ref[2:3, :] * two_back
    ).astype(BF)


def attend_body(scale, q_ref, k_ref, v_ref, meta_ref, out_ref, lse_ref, bias_ref, va_ref):
    slots = q_ref.shape[0]
    half = LANES // 2

    @pl.when(pl.program_id(0) == 0)
    def _():
        cols = columns(meta_ref[...])
        for lo in range(0, slots, BLOCK):
            end = lo + BLOCK
            starts = cols[lo:end, 0:1]
            row = lax.broadcasted_iota(jnp.int32, (BLOCK, end), 0) + lo
            col = lax.broadcasted_iota(jnp.int32, (BLOCK, end), 1)
            keep = (starts == meta_ref[0:1, :end]) & (meta_ref[1:2, :end] > 0.5) & (col <= row)
            bias_ref[lo:end, :end] = jnp.where(keep, 0.0, NEG_FILL)

    left = lax.broadcasted_iota(jnp.int32, (1, LANES), 1) < half
    value = v_ref[...]
    one = jnp.ones_like(value)
    va_ref[0, :, :] = jnp.where(left, value, one)
    va_ref[1, :, :] = jnp.where(left, one, value)
    for lo in range(0, slots, BLOCK):
        end = lo + BLOCK
        query = q_ref[lo:end, :] * jnp.asarray(scale, BF)
        outs, logs = [], []
        for head in range(2):
            own = left if head == 0 else jnp.logical_not(left)
            scores = dot_nt(jnp.where(own, query, jnp.zeros_like(query)), k_ref[:end, :])
            scores = scores + bias_ref[lo:end, :end]
            peak = jnp.max(scores, axis=-1, keepdims=True)
            terms = jnp.exp(scores - peak).astype(BF)
            both = dot(terms, va_ref[head, :end, :])
            outs.append(both / pltpu.roll(both, half, 1))
            logs.append(peak + jnp.log(both))
        out_ref[lo:end, :] = jnp.where(left, outs[0], outs[1]).astype(BF)
        lse_ref[lo:end, :] = jnp.where(left, logs[1], logs[0])


def ffn_body(
    att_ref, x_ref, go_ref, meta_ref, wo_ref, w1_ref, w2_ref, vec_ref,
    out_ref, act_ref, up_ref, low_ref, res_ref, cot_ref, gatt_ref, gres_ref, dvec_ref,
):
    width = x_ref.shape[1]
    live = columns(meta_ref[...])[:, 1:2]
    residual = x_ref[...].astype(F32) + dot(att_ref[...], wo_ref[...])
    normed, scaled = normalize(residual)
    low = (normed * vec_ref[2:3, :] + vec_ref[3:4, :]).astype(BF)
    low_ref[...] = low
    cotangent = go_ref[...].astype(F32) * live
    cot_low = cotangent.astype(BF)
    cot_ref[...] = cot_low
    total = residual
    grad = jnp.zeros_like(residual)
    for part in range(FOLD):
        cut = slice(part * width, (part + 1) * width)
        upward = jnp.maximum(dot(low, w1_ref[part]), 0.0)
        active = (upward * upward).astype(BF)
        act_ref[:, cut] = active
        total = total + dot(active, w2_ref[cut, :])
        grad_up = (dot_nt(cot_low, w2_ref[cut, :]) * (2.0 * upward)).astype(BF)
        up_ref[:, cut] = grad_up
        grad = grad + dot_nt(grad_up, w1_ref[part])
    out_ref[...] = total.astype(BF)
    grad_residual = cotangent + norm_back(grad, normed, scaled, vec_ref[2:3, :])
    gres_ref[...] = grad_residual
    res_low = grad_residual.astype(BF)
    res_ref[...] = res_low
    gatt_ref[...] = dot_nt(res_low, wo_ref[...]).astype(BF)

    @pl.when(pl.program_id(0) == 0)
    def _():
        dvec_ref[...] = jnp.zeros_like(dvec_ref)

    dvec_ref[0:1, :] += jnp.sum(grad * normed, axis=0, keepdims=True)
    dvec_ref[1:2, :] += jnp.sum(grad, axis=0, keepdims=True)


def weight_body(act_ref, up_ref, low_ref, cot_ref, att_ref, res_ref, g2_ref, g1_ref, go_ref):
    g2_ref[...] = dot_tn(act_ref[...], cot_ref[...]).astype(BF)
    g1_ref[...] = dot_tn(low_ref[...], up_ref[...]).astype(BF)

    @pl.when(pl.program_id(0) == 0)
    def _():
        go_ref[...] = dot_tn(att_ref[...], res_ref[...]).astype(BF)


def split_three(value):
    high = value.astype(BF)
    rest = value - high.astype(F32)
    middle = rest.astype(BF)
    return high, middle, (rest - middle.astype(F32)).astype(BF)


def attend_back_body(
    scale, q_ref, k_ref, v_ref, do_ref, o_ref, lse_ref, meta_ref, grad_ref,
    bias_ref, qa_ref, ka_ref, va_ref, da_ref, kt_ref, dq_ref,
):
    slots = q_ref.shape[0]
    half = LANES // 2

    @pl.when(pl.program_id(0) == 0)
    def _():
        cols = columns(meta_ref[...])
        for lo in range(0, slots, BLOCK):
            end = lo + BLOCK
            size = slots - lo
            row = lax.broadcasted_iota(jnp.int32, (BLOCK, size), 0)
            col = lax.broadcasted_iota(jnp.int32, (BLOCK, size), 1)
            keep = (
                (cols[lo:end, 0:1] == meta_ref[0:1, lo:])
                & (cols[lo:end, 1:2] > 0.5)
                & (row <= col)
            )
            bias_ref[lo:end, lo:] = jnp.where(keep, 0.0, NEG_FILL)

    lane = lax.broadcasted_iota(jnp.int32, (1, LANES), 1)
    left = lane < half
    query = q_ref[...]
    key = k_ref[...]
    value = v_ref[...]
    grad_out = do_ref[...]
    product = grad_out.astype(F32) * o_ref[...].astype(F32)
    kt_ref[...] = jnp.transpose(key.astype(F32), (1, 0)).astype(BF)
    logs = split_three(-lse_ref[...])
    zero = jnp.zeros_like(query)
    one = jnp.ones_like(query)
    for head in range(2):
        own = left if head == 0 else jnp.logical_not(left)
        base = half if head == 0 else 0
        delta = jnp.sum(jnp.where(own, product, 0.0), axis=-1, keepdims=True)
        deltas = split_three(-delta)
        marks = [lane == base + n for n in range(3)]

        def spread(terms):
            result = zero
            for mark, term in zip(marks, terms):
                result = jnp.where(mark, term, result)
            return result

        ones = spread((one, one, one))
        qa_ref[head] = jnp.where(own, query * jnp.asarray(scale, BF), spread(logs))
        ka_ref[head] = jnp.where(own, key, ones)
        va_ref[head] = jnp.where(own, value, ones)
        da_ref[head] = jnp.where(own, grad_out, spread(deltas))
    dq_ref[...] = jnp.zeros_like(dq_ref)
    for lo in range(0, slots, BLOCK):
        end = lo + BLOCK
        grad_keys, grad_values = [], []
        for head in range(2):
            rows = slice(head * half, (head + 1) * half)
            scores = dot_nt(ka_ref[head, lo:end, :], qa_ref[head, lo:, :]) + bias_ref[lo:end, lo:]
            probs = jnp.exp(scores)
            inner = dot_nt(va_ref[head, lo:end, :], da_ref[head, lo:, :])
            grad_scores = (probs * inner).astype(BF)
            grad_values.append(dot(probs.astype(BF), do_ref[lo:, :]))
            grad_keys.append(dot(grad_scores, q_ref[lo:, :]))
            dq_ref[rows, lo:] += dot(kt_ref[rows, lo:end], grad_scores)
        grad_ref[1, lo:end, :] = jnp.where(left, grad_keys[0], grad_keys[1]) * scale
        grad_ref[2, lo:end, :] = jnp.where(left, grad_values[0], grad_values[1])
    grad_ref[0, :, :] = jnp.transpose(dq_ref[...], (1, 0)) * scale


def post_body(
    gm_ref, proj_ref, taps_ref, w_ref, low_ref, x_ref, gres_ref, vec_ref, meta_ref,
    gw_ref, gtaps_ref, out_ref, dvec_ref, gn_ref,
):
    slots = x_ref.shape[0]
    first, second = mix_masks(meta_ref, slots)
    mixed = gm_ref[...]
    proj = proj_ref[...]
    one_up = pltpu.roll(mixed * first, slots - 1, 0)
    two_up = pltpu.roll(mixed * second, slots - 2, 0)
    gtaps_ref[0:1, :] = jnp.sum(mixed * proj, axis=0, keepdims=True)
    gtaps_ref[1:2, :] = jnp.sum(one_up * proj, axis=0, keepdims=True)
    gtaps_ref[2:3, :] = jnp.sum(two_up * proj, axis=0, keepdims=True)
    grad = (
        taps_ref[0:1, :] * mixed + taps_ref[1:2, :] * one_up + taps_ref[2:3, :] * two_up
    ).astype(BF)
    gw_ref[...] = dot_tn(low_ref[...], grad).astype(BF)

    @pl.when(pl.program_id(0) == 0)
    def _():
        gn_ref[...] = jnp.zeros_like(gn_ref)

    gn_ref[...] += dot_nt(grad, w_ref[...])

    @pl.when(pl.program_id(0) == 2)
    def _():
        dvec_ref[...] = jnp.zeros_like(dvec_ref)
        for lo in range(0, slots, BLOCK):
            rows = slice(lo, lo + BLOCK)
            normed, scaled = normalize(x_ref[rows, :].astype(F32))
            incoming = gn_ref[rows, :]
            out_ref[rows, :] = gres_ref[rows, :] + norm_back(
                incoming, normed, scaled, vec_ref[0:1, :]
            )
            dvec_ref[0:1, :] += jnp.sum(incoming * normed, axis=0, keepdims=True)
            dvec_ref[1:2, :] += jnp.sum(incoming, axis=0, keepdims=True)


def layer(tokens, grad_out, meta, w_qkv, w_out, w_up, w_down, vec, taps):
    slots, width = tokens.shape
    hidden = FOLD * width
    pairs = width // LANES
    scale = (width // HEADS) ** (-0.5)
    three = pl.BlockSpec((None, slots, width), lambda c: (c, 0, 0))
    square = pl.BlockSpec((None, width, width), lambda c: (c, 0, 0))
    tap = pl.BlockSpec((None, 3, width), lambda c: (c, 0, 0))
    gemm = 2 * slots * width * width
    low_one, mixed, project = call(
        pre_body,
        (3,),
        [whole((slots, width)), square, whole(vec.shape), tap, whole(meta.shape)],
        [whole((slots, width)), three, three],
        [like((slots, width), BF), like((3, slots, width), BF), like((3, slots, width), F32)],
        [],
        (tokens, w_qkv, vec, taps, meta),
        3 * gemm,
        24 << 20,
    )
    lane_block = pl.BlockSpec((slots, LANES), lambda p: (0, p))

    def part(c):
        return pl.BlockSpec((None, slots, LANES), lambda p: (c, 0, p))

    attended, lse = call(
        functools.partial(attend_body, scale),
        (pairs,),
        [part(0), part(1), part(2), whole(meta.shape)],
        [lane_block, lane_block],
        [like((slots, width), BF), like((slots, width), F32)],
        [pltpu.VMEM((slots, slots), F32), pltpu.VMEM((2, slots, LANES), BF)],
        (mixed, mixed, mixed, meta),
        2 * slots * slots * width * 2,
        12 << 20,
    )
    row_block = pl.BlockSpec((BLOCK, width), lambda i: (i, 0))
    wide_block = pl.BlockSpec((BLOCK, hidden), lambda i: (i, 0))
    block_out, active, grad_up, low_two, res_low, cot, grad_att, grad_res, dvec_two = call(
        ffn_body,
        (slots // BLOCK,),
        [
            row_block,
            row_block,
            row_block,
            pl.BlockSpec((8, BLOCK), lambda i: (0, i)),
            fixed((width, width)),
            fixed((FOLD, width, width)),
            fixed((hidden, width)),
            whole(vec.shape),
        ],
        [row_block, wide_block, wide_block, row_block, row_block, row_block, row_block, row_block,
         whole((8, width))],
        [
            like((slots, width), BF),
            like((slots, hidden), BF),
            like((slots, hidden), BF),
            like((slots, width), BF),
            like((slots, width), BF),
            like((slots, width), BF),
            like((slots, width), BF),
            like((slots, width), F32),
            like((8, width), F32),
        ],
        [],
        (attended, tokens, grad_out, meta, w_out, w_up, w_down, vec),
        (4 * FOLD + 2) * gemm,
        36 << 20,
    )
    wide = pl.BlockSpec((slots, width), lambda q: (0, q))
    grad_down, grad_w_up, grad_w_out = call(
        weight_body,
        (FOLD,),
        [wide, wide] + [whole((slots, width))] * 4,
        [
            pl.BlockSpec((width, width), lambda q: (q, 0)),
            pl.BlockSpec((None, width, width), lambda q: (q, 0, 0)),
            whole((width, width)),
        ],
        [like((hidden, width), BF), like((FOLD, width, width), BF), like((width, width), BF)],
        [],
        (active, grad_up, low_two, cot, attended, res_low),
        (2 * FOLD + 1) * gemm,
        28 << 20,
    )
    grad_mixed = call(
        functools.partial(attend_back_body, scale),
        (pairs,),
        [part(0), part(1), part(2), lane_block, lane_block, lane_block, whole(meta.shape)],
        pl.BlockSpec((3, slots, LANES), lambda p: (0, 0, p)),
        like((3, slots, width), F32),
        [
            pltpu.VMEM((slots, slots), F32),
            pltpu.VMEM((2, slots, LANES), BF),
            pltpu.VMEM((2, slots, LANES), BF),
            pltpu.VMEM((2, slots, LANES), BF),
            pltpu.VMEM((2, slots, LANES), BF),
            pltpu.VMEM((LANES, slots), BF),
            pltpu.VMEM((LANES, slots), F32),
        ],
        (mixed, mixed, mixed, grad_att, attended, lse, meta),
        5 * slots * slots * width * 2,
        20 << 20,
    )
    grad_qkv, grad_taps, tokens_grad, dvec_one = call(
        post_body,
        (3,),
        [
            three, three, tap, square, whole((slots, width)), whole((slots, width)),
            fixed((slots, width)), whole(vec.shape), whole(meta.shape),
        ],
        [square, tap, whole((slots, width)), whole((8, width))],
        [
            like((3, width, width), BF),
            like((3, 3, width), F32),
            like((slots, width), F32),
            like((8, width), F32),
        ],
        [pltpu.VMEM((slots, width), F32)],
        (grad_mixed, project, taps, w_qkv, low_one, tokens, grad_res, vec, meta),
        6 * gemm,
        34 << 20,
    )
    return (
        block_out, tokens_grad, grad_qkv, grad_w_out, grad_w_up, grad_down,
        dvec_one, dvec_two, grad_taps,
    )


def per_device(shards, tokens_in, grad_out, seq_start, valid, matrices, vectors):
    slots, width = tokens_in.shape
    rows, roww = matrices.shape
    square = width * width
    total = rows * shards * roww
    view_rows = total // width
    meta = jnp.concatenate(
        [seq_start.astype(F32)[None], valid.astype(F32)[None], jnp.zeros((6, slots), F32)], axis=0
    )
    view = lax.all_gather(matrices.reshape(-1, width), AXES, axis=0, tiled=True)
    vec_flat = lax.all_gather(vectors, AXES, axis=0, tiled=True).reshape(-1).astype(F32)
    vec = vec_flat[: 13 * width].reshape(13, width)
    taps = vec[4:13].reshape(3, 3, width)
    vec = vec[:8]
    w_qkv = view[: 3 * width].reshape(3, width, width)
    w_out = view[3 * width : 4 * width]
    w_up = view[4 * width : 8 * width].reshape(width, FOLD, width).transpose(1, 0, 2)
    w_down = view[8 * width :]
    (
        block_out, tokens_grad, grad_qkv, grad_w_out, grad_w_up, grad_down,
        dvec_one, dvec_two, grad_taps,
    ) = layer(tokens_in, grad_out, meta, w_qkv, w_out, w_up, w_down, vec, taps)
    grad_view = jnp.concatenate(
        [
            grad_qkv.reshape(-1, width),
            grad_w_out,
            grad_w_up.transpose(1, 0, 2).reshape(-1, width),
            grad_down,
        ],
        axis=0,
    )
    owned = lax.psum_scatter(grad_view, AXES, scatter_dimension=0, tiled=True)
    grad_vec = jnp.concatenate(
        [dvec_one[:2], dvec_two[:2], grad_taps.reshape(9, width)], axis=0
    ).reshape(-1)
    grad_vec = jnp.pad(grad_vec, (0, vec_flat.size - grad_vec.size)).reshape(-1, roww)
    owned_vec = lax.psum_scatter(grad_vec, AXES, scatter_dimension=0, tiled=True)
    return (
        block_out,
        tokens_grad,
        owned.astype(F32).reshape(rows, roww),
        owned_vec,
    )


def solution(mesh):
    row = P(AXES, None)
    flat = P(AXES)
    shards = mesh.shape["dp"] * mesh.shape["sub"]
    return jax.shard_map(
        functools.partial(per_device, shards),
        mesh=mesh,
        in_specs=(row, row, flat, flat, row, row),
        out_specs=(row, row, row, row),
        check_vma=False,
    )
```

```python
import functools

import jax
import jax.numpy as jnp
from jax import lax
from jax.experimental import pallas as pl
from jax.experimental.pallas import tpu as pltpu
from jax.sharding import PartitionSpec as P

HEADS = 12
EPSILON = 1e-05
NEG_FILL = -1e30
BF = jnp.bfloat16
F32 = jnp.float32
AXES = ("dp", "sub")
VMEM_BYTES = 60 * 1024 * 1024
LANES = 128
BLOCK = 256
GROUP = 96
FOLD = 4
SHARDS = 32
OUT_GROUPS = 8
UP_GROUPS = 32
UP_FIRST, UP_END = 32, 64
HALVES = ((0, 4), (4, 2))
(
    PLACE_LINEAR, PLACE_Z, PLACE_IN_PLANE, PLACE_XY, PLACE_CORE,
    PLACE_NEAR, PLACE_LOW, PLACE_HIGH,
) = range(8)
HBM = pl.BlockSpec(memory_space=pl.ANY)


def dot(a, b):
    return jnp.dot(a, b, preferred_element_type=F32)


def dot_nt(a, b):
    return lax.dot_general(a, b, (((1,), (1,)), ((), ())), preferred_element_type=F32)


def dot_tn(a, b):
    return lax.dot_general(a, b, (((0,), (0,)), ((), ())), preferred_element_type=F32)


def whole(shape):
    return pl.BlockSpec(shape, lambda *_: (0,) * len(shape))


def fixed(shape):
    return pl.BlockSpec(shape, lambda *_: (0,) * len(shape), pipeline_mode=pl.Buffered(1))


def call(body, grid, ins, outs, out_shape, scratch, args, flops, moved, place=None):
    return pl.pallas_call(
        body,
        grid_spec=pltpu.PrefetchScalarGridSpec(
            num_scalar_prefetch=0 if place is None else 1,
            grid=grid,
            in_specs=ins,
            out_specs=outs,
            scratch_shapes=scratch,
        ),
        out_shape=out_shape,
        compiler_params=pltpu.CompilerParams(
            dimension_semantics=("arbitrary",) * len(grid), vmem_limit_bytes=VMEM_BYTES
        ),
        cost_estimate=pl.CostEstimate(flops=flops, bytes_accessed=moved, transcendentals=0),
    )(*(() if place is None else (place,)), *args)


def like(shape, dtype):
    return jax.ShapeDtypeStruct(shape, dtype)


def normalize(v):
    centre = v - jnp.mean(v, axis=-1, keepdims=True)
    scaled = lax.rsqrt(jnp.mean(centre * centre, axis=-1, keepdims=True) + EPSILON)
    return centre * scaled, scaled


def norm_back(incoming, normed, scaled, gain):
    weighted = incoming * gain
    return scaled * (
        weighted
        - jnp.mean(weighted, axis=-1, keepdims=True)
        - normed * jnp.mean(weighted * normed, axis=-1, keepdims=True)
    )


def columns(meta):
    return jnp.transpose(meta, (1, 0))


def mix_masks(meta_ref, slots):
    cols = columns(meta_ref[...])
    position = lax.broadcasted_iota(jnp.int32, (slots, 1), 0).astype(F32) - cols[:, 0:1]
    return jnp.where(position >= 1.0, 1.0, 0.0), jnp.where(position >= 2.0, 1.0, 0.0)


def xor_pairs(mask, keep=None):
    return [(i, i ^ mask) for i in range(SHARDS) if keep is None or keep(i)]


def swap(value, mask, keep=None):
    return lax.ppermute(value, AXES, xor_pairs(mask, keep))


def plane_of(index):
    return index >> 3


def prep_body(place_ref, in_ref, out_ref, wide_ref):
    width = out_ref.shape[1]
    cols = width // LANES
    wide_ref[...] = in_ref[...].astype(F32)
    first = place_ref[PLACE_LINEAR] * (out_ref.shape[0] // GROUP)
    for n in range(out_ref.shape[0] // GROUP):
        base = n * GROUP * cols
        up = jnp.logical_and(first + n >= UP_FIRST, first + n < UP_END)

        @pl.when(up)
        def _():
            for j in range(cols):
                parts = [
                    wide_ref[pl.ds(base + q * cols + j, GROUP // FOLD, stride=cols * FOLD), :]
                    for q in range(FOLD)
                ]
                out_ref[n * GROUP : (n + 1) * GROUP, j * LANES : (j + 1) * LANES] = (
                    jnp.concatenate(parts, axis=0).astype(BF)
                )

        @pl.when(jnp.logical_not(up))
        def _():
            for j in range(cols):
                out_ref[n * GROUP : (n + 1) * GROUP, j * LANES : (j + 1) * LANES] = wide_ref[
                    pl.ds(base + j, GROUP, stride=cols), :
                ].astype(BF)


def finish_body(place_ref, *refs):
    halves = len(HALVES)
    zero = [refs[4 * h : 4 * h + 4] for h in range(halves)]
    rest, out_ref, total_ref = refs[4 * halves : 4 * halves + 4], refs[-2], refs[-1]
    width = total_ref.shape[1]
    cols = width // LANES
    plane = place_ref[PLACE_Z]

    def add(parts):
        total = parts[0][...].astype(F32)
        for part in parts[1:]:
            total = total + part[...].astype(F32)
        return total

    @pl.when(plane == 0)
    def _():
        for (at, count), parts in zip(HALVES, zero):
            total_ref[:, at * LANES : (at + count) * LANES] = add(parts)

    @pl.when(plane != 0)
    def _():
        total_ref[...] = add(rest)

    first = place_ref[PLACE_LINEAR] * (total_ref.shape[0] // GROUP)
    for n in range(total_ref.shape[0] // GROUP):
        base = n * GROUP * cols
        up = jnp.logical_and(first + n >= UP_FIRST, first + n < UP_END)

        @pl.when(up)
        def _():
            step = GROUP // FOLD
            for j in range(cols):
                for q in range(FOLD):
                    lo = n * GROUP + q * step
                    out_ref[pl.ds(base + q * cols + j, step, stride=cols * FOLD), :] = total_ref[
                        lo : lo + step, j * LANES : (j + 1) * LANES
                    ]

        @pl.when(jnp.logical_not(up))
        def _():
            for j in range(cols):
                out_ref[pl.ds(base + j, GROUP, stride=cols), :] = total_ref[
                    n * GROUP : (n + 1) * GROUP, j * LANES : (j + 1) * LANES
                ]


def route_body(place_ref, mine_ref, other_ref, *outs):
    for r, out in enumerate(outs):

        @pl.when(pl.program_id(0) == r)
        def _():
            out[...] = (mine_ref[...].astype(F32) + other_ref[...].astype(F32)).astype(BF)


def lift_body(place_ref, *refs):
    lows, highs, outs = refs[:4], refs[4:8], refs[8:]
    plane = place_ref[PLACE_Z]

    def add(parts):
        total = parts[0].astype(F32)
        for part in parts[1:]:
            total = total + part.astype(F32)
        return total.astype(BF)

    for k, out in enumerate(outs):
        target = plane ^ k

        @pl.when(target == 3)
        def _():
            out[...] = add([ref[...] for ref in highs])

        @pl.when(target != 3)
        def _():
            p = jnp.maximum(target, 1) - 1
            out[...] = add([ref[p] for ref in lows])


def sum_body(a_ref, b_ref, c_ref, d_ref, out_ref):
    out_ref[...] = (
        a_ref[...].astype(F32) + b_ref[...].astype(F32) + c_ref[...].astype(F32) + d_ref[...].astype(F32)
    ).astype(BF)


def start_qkv(place_ref, own, near, w_ref, sem):
    size = own[0].shape[0]
    for r in range(8):
        at = pl.multiple_of((place_ref[PLACE_IN_PLANE] ^ r) * size, 32)

        @pl.when(place_ref[PLACE_Z] == 0)
        def _():
            pltpu.make_async_copy(own[r], w_ref.at[pl.ds(at, size)], sem).start()

        @pl.when(place_ref[PLACE_Z] != 0)
        def _():
            pltpu.make_async_copy(near[r], w_ref.at[pl.ds(at, size)], sem).start()


def wait_all(ref, sem):
    pltpu.make_async_copy(ref, ref, sem).wait()


def start_dense(place_ref, own, near, far, wo_ref, w1_ref, w2_ref, sems):
    step = GROUP // FOLD
    width = own[0].shape[1]
    slots = [(own, None, PLACE_Z, (1, 2, 3)), (near, None, PLACE_NEAR, (1,))]
    slots += [(far, 0, PLACE_LOW, (1, 2)), (far, 1, PLACE_HIGH, (2, 3))]
    for bufs, slot, plane_at, planes in slots:
        for p in planes:

            @pl.when(place_ref[plane_at] == p)
            def _():
                for r in range(8):
                    buf = bufs[r] if slot is None else bufs[r].at[slot]
                    place = place_ref[PLACE_IN_PLANE] ^ r
                    for n in range(3):
                        group = 24 * (p - 1) + 3 * place + n
                        rows = buf.at[pl.ds(n * GROUP, GROUP)]

                        def to_out():
                            at = pl.multiple_of(group * GROUP, 32)
                            pltpu.make_async_copy(
                                rows, wo_ref.at[pl.ds(at, GROUP)], sems.at[0]
                            ).start()

                        def to_up():
                            at = pl.multiple_of((group - OUT_GROUPS) * step, 8)
                            pltpu.make_async_copy(
                                rows.reshape(FOLD, step, width),
                                w1_ref.at[:, pl.ds(at, step)],
                                sems.at[1],
                            ).start()

                        def to_down():
                            at = pl.multiple_of((group - OUT_GROUPS - UP_GROUPS) * GROUP, 32)
                            pltpu.make_async_copy(
                                rows, w2_ref.at[pl.ds(at, GROUP)], sems.at[2]
                            ).start()

                        if p == 1:
                            pl.when(group < OUT_GROUPS)(to_out)
                            pl.when(group >= OUT_GROUPS)(to_up)
                        elif p == 2:
                            pl.when(group < OUT_GROUPS + UP_GROUPS)(to_up)
                            if w2_ref is not None:
                                pl.when(group >= OUT_GROUPS + UP_GROUPS)(to_down)
                        elif w2_ref is not None:
                            to_down()


def deal(place_ref, targets, sems, copy):
    core = place_ref[PLACE_CORE]
    for j in range(8):
        for which in range(2):

            @pl.when(core ^ (j % 2) == which)
            def _():
                copy(j, targets[which].at[j // 2], sems.at[which])


def pre_body(place_ref, x_ref, vec_ref, taps_ref, meta_ref, *refs):
    own, near, (low_ref, mixed_ref, proj_ref, w_ref, sem) = refs[:8], refs[8:16], refs[16:]
    slots, width = x_ref.shape
    here = pl.multiple_of(pl.program_id(0) * width, width)

    @pl.when(pl.program_id(0) == 0)
    def _():
        start_qkv(place_ref, own, near, w_ref, sem)
        for lo in range(0, slots, BLOCK):
            rows = slice(lo, lo + BLOCK)
            normed, _ = normalize(x_ref[rows, :].astype(F32))
            low_ref[rows, :] = (normed * vec_ref[0:1, :] + vec_ref[1:2, :]).astype(BF)
        wait_all(w_ref, sem)

    first, second = mix_masks(meta_ref, slots)
    proj_ref[...] = dot(low_ref[...], w_ref[pl.ds(here, width), :])
    value = proj_ref[...]
    one_back = pltpu.roll(value, 1, 0) * first
    two_back = pltpu.roll(value, 2, 0) * second
    mixed_ref[...] = (
        taps_ref[0:1, :] * value + taps_ref[1:2, :] * one_back + taps_ref[2:3, :] * two_back
    ).astype(BF)


def attend_body(scale, q_ref, k_ref, v_ref, meta_ref, out_ref, lse_ref, bias_ref, va_ref):
    slots = q_ref.shape[0]
    half = LANES // 2

    @pl.when(pl.program_id(0) == 0)
    def _():
        cols = columns(meta_ref[...])
        for lo in range(0, slots, BLOCK):
            end = lo + BLOCK
            starts = cols[lo:end, 0:1]
            row = lax.broadcasted_iota(jnp.int32, (BLOCK, end), 0) + lo
            col = lax.broadcasted_iota(jnp.int32, (BLOCK, end), 1)
            keep = (starts == meta_ref[0:1, :end]) & (meta_ref[1:2, :end] > 0.5) & (col <= row)
            bias_ref[lo:end, :end] = jnp.where(keep, 0.0, NEG_FILL)

    left = lax.broadcasted_iota(jnp.int32, (1, LANES), 1) < half
    value = v_ref[...]
    one = jnp.ones_like(value)
    va_ref[0, :, :] = jnp.where(left, value, one)
    va_ref[1, :, :] = jnp.where(left, one, value)
    for lo in range(0, slots, BLOCK):
        end = lo + BLOCK
        query = q_ref[lo:end, :] * jnp.asarray(scale, BF)
        outs, logs = [], []
        for head in range(2):
            own = left if head == 0 else jnp.logical_not(left)
            scores = dot_nt(jnp.where(own, query, jnp.zeros_like(query)), k_ref[:end, :])
            scores = scores + bias_ref[lo:end, :end]
            peak = jnp.max(scores, axis=-1, keepdims=True)
            terms = jnp.exp(scores - peak).astype(BF)
            both = dot(terms, va_ref[head, :end, :])
            outs.append(both / pltpu.roll(both, half, 1))
            logs.append(peak + jnp.log(both))
        out_ref[lo:end, :] = jnp.where(left, outs[0], outs[1]).astype(BF)
        lse_ref[lo:end, :] = jnp.where(left, logs[1], logs[0])


def up_body(place_ref, att_ref, x_ref, go_ref, meta_ref, vec_ref, *refs):
    own, near, far = refs[:8], refs[8:16], refs[16:24]
    (
        res_ref, low_ref, cot_ref, pos_ref, mine_ref, other_ref, first_ref,
        wo_ref, w1_ref, act_ref, cots_ref, g2_ref, sems,
    ) = refs[24:]
    width = x_ref.shape[1]
    step = pl.program_id(0)
    blocks = act_ref.shape[0] // BLOCK
    here = pl.multiple_of(step * BLOCK, BLOCK)

    @pl.when(step == 0)
    def _():
        start_dense(place_ref, own, near, far, wo_ref, w1_ref, None, sems)
        wait_all(wo_ref, sems.at[0])

    @pl.when(step < blocks)
    def _():
        live = columns(meta_ref[...])[:, 1:2]
        residual = x_ref[...].astype(F32) + dot(att_ref[...], wo_ref[...])
        res_ref[...] = residual
        normed, _ = normalize(residual)
        low = (normed * vec_ref[2:3, :] + vec_ref[3:4, :]).astype(BF)
        low_ref[...] = low
        cot = (go_ref[...].astype(F32) * live).astype(BF)
        cot_ref[...] = cot
        cots_ref[pl.ds(here, BLOCK), :] = cot

        @pl.when(step == 0)
        def _():
            wait_all(w1_ref, sems.at[1])

        for part in range(FOLD):
            cut = slice(part * width, (part + 1) * width)
            upward = jnp.maximum(dot(low, w1_ref[part]), 0.0)
            pos_ref[:, cut] = upward
            act_ref[pl.ds(here, BLOCK), cut] = (upward * upward).astype(BF)

    for part in range(FOLD):

        @pl.when(step == blocks + part)
        def _():
            cut = slice(part * width, (part + 1) * width)
            g2_ref[cut, :] = dot_tn(act_ref[:, cut], cots_ref[...]).astype(BF)

    @pl.when(step == blocks + FOLD - 1)
    def _():
        size = mine_ref.shape[1]
        skip = g2_ref.shape[0] - 8 * size

        def copy(j, target, sem):
            pltpu.make_async_copy(g2_ref.at[pl.ds(skip + j * size, size)], target, sem).start()

        deal(place_ref, (mine_ref, other_ref), sems, copy)
        first_ref[...] = g2_ref[0:skip, :]
        wait_all(mine_ref, sems.at[0])
        wait_all(other_ref, sems.at[1])


def down_body(
    place_ref, att_ref, low_ref, res_ref, cot_ref, pos_ref, vec_ref, first_ref, *refs
):
    own, near, far = refs[:8], refs[8:16], refs[16:24]
    (
        out_ref, gatt_ref, gres_ref, dvec_ref, mine_ref, other_ref,
        wo_ref, w1_ref, w2_ref, up_ref, reslow_ref, g1_ref, go_ref, sems,
    ) = refs[24:]
    width = res_ref.shape[1]
    step = pl.program_id(0)
    blocks = up_ref.shape[0] // BLOCK
    here = pl.multiple_of(step * BLOCK, BLOCK)

    @pl.when(step == 0)
    def _():
        start_dense(place_ref, own, near, far, wo_ref, w1_ref, w2_ref, sems)
        dvec_ref[...] = jnp.zeros_like(dvec_ref)
        wait_all(w2_ref, sems.at[2])
        wait_all(w1_ref, sems.at[1])
        wait_all(wo_ref, sems.at[0])

    @pl.when(step < blocks)
    def _():
        residual = res_ref[...]
        normed, scaled = normalize(residual)
        cot = cot_ref[...]
        total = residual
        grad = jnp.zeros_like(residual)
        for part in range(FOLD):
            cut = slice(part * width, (part + 1) * width)
            upward = pos_ref[:, cut]
            total = total + dot((upward * upward).astype(BF), w2_ref[cut, :])
            grad_up = (dot_nt(cot, w2_ref[cut, :]) * (2.0 * upward)).astype(BF)
            up_ref[pl.ds(here, BLOCK), cut] = grad_up
            grad = grad + dot_nt(grad_up, w1_ref[part])
        out_ref[...] = total.astype(BF)
        grad_residual = cot.astype(F32) + norm_back(grad, normed, scaled, vec_ref[2:3, :])
        gres_ref[...] = grad_residual
        res_low = grad_residual.astype(BF)
        reslow_ref[pl.ds(here, BLOCK), :] = res_low
        gatt_ref[...] = dot_nt(res_low, wo_ref[...]).astype(BF)
        dvec_ref[0:1, :] += jnp.sum(grad * normed, axis=0, keepdims=True)
        dvec_ref[1:2, :] += jnp.sum(grad, axis=0, keepdims=True)

    for part in range(FOLD):

        @pl.when(step == blocks + part)
        def _():
            cut = slice(part * width, (part + 1) * width)
            g1_ref[part] = dot_tn(low_ref[...], up_ref[:, cut]).astype(BF)

    @pl.when(step == blocks + FOLD - 1)
    def _():
        go_ref[...] = dot_tn(att_ref[...], reslow_ref[...]).astype(BF)
        span = GROUP // FOLD

        def copy(j, target, sem):
            for p in range(2):
                for n in range(3):
                    group = 24 * p + 3 * j + n
                    rows = target.at[p, pl.ds(n * GROUP, GROUP)]
                    if group < OUT_GROUPS:
                        source = go_ref.at[pl.ds(group * GROUP, GROUP)]
                    elif group < OUT_GROUPS + UP_GROUPS:
                        source = g1_ref.at[:, pl.ds((group - OUT_GROUPS) * span, span)]
                        rows = rows.reshape(FOLD, span, width)
                    else:
                        at = (group - OUT_GROUPS - UP_GROUPS) * GROUP
                        source = first_ref.at[pl.ds(at, GROUP)]
                    pltpu.make_async_copy(source, rows, sem).start()

        deal(place_ref, (mine_ref, other_ref), sems, copy)
        wait_all(mine_ref, sems.at[0])
        wait_all(other_ref, sems.at[1])


def split_three(value):
    high = value.astype(BF)
    rest = value - high.astype(F32)
    middle = rest.astype(BF)
    return high, middle, (rest - middle.astype(F32)).astype(BF)


def attend_back_body(
    scale, q_ref, k_ref, v_ref, do_ref, o_ref, lse_ref, meta_ref, grad_ref,
    bias_ref, qa_ref, ka_ref, va_ref, da_ref, kt_ref, dq_ref,
):
    slots = q_ref.shape[0]
    half = LANES // 2

    @pl.when(pl.program_id(0) == 0)
    def _():
        cols = columns(meta_ref[...])
        for lo in range(0, slots, BLOCK):
            end = lo + BLOCK
            size = slots - lo
            row = lax.broadcasted_iota(jnp.int32, (BLOCK, size), 0)
            col = lax.broadcasted_iota(jnp.int32, (BLOCK, size), 1)
            keep = (
                (cols[lo:end, 0:1] == meta_ref[0:1, lo:])
                & (cols[lo:end, 1:2] > 0.5)
                & (row <= col)
            )
            bias_ref[lo:end, lo:] = jnp.where(keep, 0.0, NEG_FILL)

    lane = lax.broadcasted_iota(jnp.int32, (1, LANES), 1)
    left = lane < half
    query = q_ref[...]
    key = k_ref[...]
    value = v_ref[...]
    grad_out = do_ref[...]
    product = grad_out.astype(F32) * o_ref[...].astype(F32)
    kt_ref[...] = jnp.transpose(key.astype(F32), (1, 0)).astype(BF)
    logs = split_three(-lse_ref[...])
    zero = jnp.zeros_like(query)
    one = jnp.ones_like(query)
    for head in range(2):
        own = left if head == 0 else jnp.logical_not(left)
        base = half if head == 0 else 0
        delta = jnp.sum(jnp.where(own, product, 0.0), axis=-1, keepdims=True)
        deltas = split_three(-delta)
        marks = [lane == base + n for n in range(3)]

        def spread(terms):
            result = zero
            for mark, term in zip(marks, terms):
                result = jnp.where(mark, term, result)
            return result

        ones = spread((one, one, one))
        qa_ref[head] = jnp.where(own, query * jnp.asarray(scale, BF), spread(logs))
        ka_ref[head] = jnp.where(own, key, ones)
        va_ref[head] = jnp.where(own, value, ones)
        da_ref[head] = jnp.where(own, grad_out, spread(deltas))
    dq_ref[...] = jnp.zeros_like(dq_ref)
    for lo in range(0, slots, BLOCK):
        end = lo + BLOCK
        grad_keys, grad_values = [], []
        for head in range(2):
            rows = slice(head * half, (head + 1) * half)
            scores = dot_nt(ka_ref[head, lo:end, :], qa_ref[head, lo:, :]) + bias_ref[lo:end, lo:]
            probs = jnp.exp(scores)
            inner = dot_nt(va_ref[head, lo:end, :], da_ref[head, lo:, :])
            grad_scores = (probs * inner).astype(BF)
            grad_values.append(dot(probs.astype(BF), do_ref[lo:, :]))
            grad_keys.append(dot(grad_scores, q_ref[lo:, :]))
            dq_ref[rows, lo:] += dot(kt_ref[rows, lo:end], grad_scores)
        grad_ref[1, lo:end, :] = jnp.where(left, grad_keys[0], grad_keys[1]) * scale
        grad_ref[2, lo:end, :] = jnp.where(left, grad_values[0], grad_values[1])
    grad_ref[0, :, :] = jnp.transpose(dq_ref[...], (1, 0)) * scale


def post_body(last, lane_at, place_ref, gm_ref, proj_ref, taps_ref, low_ref, meta_ref, *refs):
    if last:
        x_ref, gres_ref, vec_ref, part_ref = refs[:4]
        refs = refs[4:]
    own, near = refs[:8], refs[8:16]
    if last:
        mine_ref, other_ref, gtaps_ref, out_ref, dvec_ref, gn_ref, w_ref, gw_ref, sems = refs[16:]
    else:
        mine_ref, other_ref, gtaps_ref, gn_ref, w_ref, gw_ref, sems = refs[16:]
    slots, lanes = gm_ref.shape
    width = gn_ref.shape[1]
    step = pl.program_id(0)
    here = pl.multiple_of(step * width, width)

    @pl.when(step == 0)
    def _():
        start_qkv(place_ref, own, near, w_ref, sems.at[0])
        gn_ref[...] = part_ref[...] if last else jnp.zeros_like(gn_ref)

    first, second = mix_masks(meta_ref, slots)
    mixed = gm_ref[...]
    proj = proj_ref[...]
    one_up = pltpu.roll(mixed * first, slots - 1, 0)
    two_up = pltpu.roll(mixed * second, slots - 2, 0)
    gtaps_ref[0:1, :] = jnp.sum(mixed * proj, axis=0, keepdims=True)
    gtaps_ref[1:2, :] = jnp.sum(one_up * proj, axis=0, keepdims=True)
    gtaps_ref[2:3, :] = jnp.sum(two_up * proj, axis=0, keepdims=True)
    grad = (
        taps_ref[0:1, :] * mixed + taps_ref[1:2, :] * one_up + taps_ref[2:3, :] * two_up
    ).astype(BF)
    gw_ref[pl.ds(here, width), :] = dot_tn(low_ref[...], grad).astype(BF)

    @pl.when(step == 0)
    def _():
        wait_all(w_ref, sems.at[0])

    gn_ref[...] += dot_nt(grad, w_ref[pl.ds(here, width), lane_at : lane_at + lanes])

    @pl.when(step == 2)
    def _():
        size = mine_ref.shape[1]

        def copy(j, target, sem):
            pltpu.make_async_copy(gw_ref.at[pl.ds(j * size, size)], target, sem).start()

        deal(place_ref, (mine_ref, other_ref), sems, copy)
        if last:
            dvec_ref[...] = jnp.zeros_like(dvec_ref)
            for lo in range(0, slots, BLOCK):
                rows = slice(lo, lo + BLOCK)
                normed, scaled = normalize(x_ref[rows, :].astype(F32))
                incoming = gn_ref[rows, :]
                out_ref[rows, :] = gres_ref[rows, :] + norm_back(
                    incoming, normed, scaled, vec_ref[0:1, :]
                )
                dvec_ref[0:1, :] += jnp.sum(incoming * normed, axis=0, keepdims=True)
                dvec_ref[1:2, :] += jnp.sum(incoming, axis=0, keepdims=True)
        wait_all(mine_ref, sems.at[0])
        wait_all(other_ref, sems.at[1])


def forward(place, tokens, meta, own, near, vec, taps):
    slots, width = tokens.shape
    pairs = width // LANES
    scale = (width // HEADS) ** (-0.5)
    three = pl.BlockSpec((None, slots, width), lambda c, *_: (c, 0, 0))
    tap = pl.BlockSpec((None, 3, width), lambda c, *_: (c, 0, 0))
    low_one, mixed, project = call(
        pre_body,
        (3,),
        [whole((slots, width)), whole(vec.shape), tap, whole(meta.shape)] + [HBM] * 16,
        [whole((slots, width)), three, three],
        [like((slots, width), BF), like((3, slots, width), BF), like((3, slots, width), F32)],
        [pltpu.VMEM((3 * width, width), BF), pltpu.SemaphoreType.DMA],
        (tokens, vec, taps, meta, *own, *near),
        6 * slots * width * width,
        24 << 20,
        place,
    )
    lane_block = pl.BlockSpec((slots, LANES), lambda p: (0, p))

    def part(c):
        return pl.BlockSpec((None, slots, LANES), lambda p: (c, 0, p))

    attended, lse = call(
        functools.partial(attend_body, scale),
        (pairs,),
        [part(0), part(1), part(2), whole(meta.shape)],
        [lane_block, lane_block],
        [like((slots, width), BF), like((slots, width), F32)],
        [pltpu.VMEM((slots, slots), F32), pltpu.VMEM((2, slots, LANES), BF)],
        (mixed, mixed, mixed, meta),
        2 * slots * slots * width * 2,
        12 << 20,
    )
    return low_one, mixed, project, attended, lse


def dense_up(place, tokens, grad_out, meta, attended, bufs, vec):
    slots, width = tokens.shape
    hidden = FOLD * width
    size = bufs[0].shape[0]
    blocks = slots // BLOCK
    row_block = pl.BlockSpec((BLOCK, width), lambda i, *_: (jnp.minimum(i, blocks - 1), 0))
    wide_block = pl.BlockSpec((BLOCK, hidden), lambda i, *_: (jnp.minimum(i, blocks - 1), 0))
    meta_block = pl.BlockSpec((8, BLOCK), lambda i, *_: (0, jnp.minimum(i, blocks - 1)))
    skip = hidden - 8 * size
    return call(
        up_body,
        (blocks + FOLD,),
        [row_block] * 3 + [meta_block, whole(vec.shape)] + [HBM] * 24,
        [row_block, row_block, row_block, wide_block, HBM, HBM, whole((skip, width))],
        [
            like((slots, width), F32),
            like((slots, width), BF),
            like((slots, width), BF),
            like((slots, hidden), F32),
            like((4, size, width), BF),
            like((4, size, width), BF),
            like((skip, width), BF),
        ],
        [
            pltpu.VMEM((width, width), BF),
            pltpu.VMEM((FOLD, width, width), BF),
            pltpu.VMEM((slots, hidden), BF),
            pltpu.VMEM((slots, width), BF),
            pltpu.VMEM((hidden, width), BF),
            pltpu.SemaphoreType.DMA((3,)),
        ],
        (attended, tokens, grad_out, meta, vec, *bufs),
        (4 * FOLD + 2) * slots * width * width,
        30 << 20,
        place,
    )


def dense_down(place, attended, low, residual, cot, positive, vec, first, bufs):
    slots, width = residual.shape
    hidden = FOLD * width
    size = bufs[0].shape[0]
    blocks = slots // BLOCK
    row_block = pl.BlockSpec((BLOCK, width), lambda i, *_: (jnp.minimum(i, blocks - 1), 0))
    wide_block = pl.BlockSpec((BLOCK, hidden), lambda i, *_: (jnp.minimum(i, blocks - 1), 0))
    full = fixed((slots, width))
    return call(
        down_body,
        (blocks + FOLD,),
        [full, full, row_block, row_block, wide_block, whole(vec.shape), whole(first.shape)]
        + [HBM] * 24,
        [row_block, row_block, row_block, whole((8, width)), HBM, HBM],
        [
            like((slots, width), BF),
            like((slots, width), BF),
            like((slots, width), F32),
            like((8, width), F32),
            like((4, 2, size, width), BF),
            like((4, 2, size, width), BF),
        ],
        [
            pltpu.VMEM((width, width), BF),
            pltpu.VMEM((FOLD, width, width), BF),
            pltpu.VMEM((hidden, width), BF),
            pltpu.VMEM((slots, hidden), BF),
            pltpu.VMEM((slots, width), BF),
            pltpu.VMEM((FOLD, width, width), BF),
            pltpu.VMEM((width, width), BF),
            pltpu.SemaphoreType.DMA((3,)),
        ],
        (attended, low, residual, cot, positive, vec, first, *bufs),
        (8 * FOLD + 4) * slots * width * width,
        36 << 20,
        place,
    )


def attend_back(half, mixed, grad_att, attended, lse, meta):
    slots, width = grad_att.shape
    at, count = half
    lane_block = pl.BlockSpec((slots, LANES), lambda p: (0, p + at))

    def part(c):
        return pl.BlockSpec((None, slots, LANES), lambda p: (c, 0, p + at))

    return call(
        functools.partial(attend_back_body, (width // HEADS) ** (-0.5)),
        (count,),
        [part(0), part(1), part(2), lane_block, lane_block, lane_block, whole(meta.shape)],
        pl.BlockSpec((3, slots, LANES), lambda p: (0, 0, p)),
        like((3, slots, count * LANES), F32),
        [
            pltpu.VMEM((slots, slots), F32),
            pltpu.VMEM((2, slots, LANES), BF),
            pltpu.VMEM((2, slots, LANES), BF),
            pltpu.VMEM((2, slots, LANES), BF),
            pltpu.VMEM((2, slots, LANES), BF),
            pltpu.VMEM((LANES, slots), BF),
            pltpu.VMEM((LANES, slots), F32),
        ],
        (mixed, mixed, mixed, grad_att, attended, lse, meta),
        10 * slots * slots * count * LANES,
        20 << 20,
    )


def post(place, half, grad_mixed, project, taps, low, meta, own, near, tail):
    _, slots, lanes = grad_mixed.shape
    width = low.shape[1]
    at = half[0] * LANES
    size = own[0].shape[0]
    lane = pl.BlockSpec((None, slots, lanes), lambda c, *_: (c, 0, 0))
    wide = pl.BlockSpec((None, slots, lanes), lambda c, *_: (c, 0, at // lanes))
    tap = pl.BlockSpec((None, 3, lanes), lambda c, *_: (c, 0, at // lanes))
    tap_out = pl.BlockSpec((None, 3, lanes), lambda c, *_: (c, 0, 0))
    full = whole((slots, width))
    ins = [lane, wide, tap, full, whole(meta.shape)]
    args = [grad_mixed, project, taps, low, meta]
    outs = [HBM, HBM, tap_out]
    shapes = [like((4, size, lanes), BF), like((4, size, lanes), BF), like((3, 3, lanes), F32)]
    scratch = []
    if tail is None:
        outs.append(full)
        shapes.append(like((slots, width), F32))
    else:
        ins += [full, fixed((slots, width)), whole(tail[2].shape), fixed((slots, width))]
        args += list(tail)
        outs += [full, whole((8, width))]
        shapes += [like((slots, width), F32), like((8, width), F32)]
        scratch.append(pltpu.VMEM((slots, width), F32))
    return call(
        functools.partial(post_body, tail is not None, at),
        (3,),
        ins + [HBM] * 16,
        outs,
        shapes,
        scratch
        + [
            pltpu.VMEM((3 * width, width), BF),
            pltpu.VMEM((3 * width, lanes), BF),
            pltpu.SemaphoreType.DMA((2,)),
        ],
        (*args, *own, *near),
        12 * slots * width * lanes,
        24 << 20,
        place,
    )


def split_core(place, mine, received):
    block = mine.shape[1:]
    spec = pl.BlockSpec((None, *block), lambda r, place: (r ^ place[PLACE_XY],) + (0,) * len(block))
    return call(
        route_body,
        (4,),
        [spec, spec],
        [whole(block)] * 4,
        [like(block, BF)] * 4,
        [],
        (mine, received),
        0,
        3 * mine.size * 2,
        place,
    )


def in_plane(routed):
    return [routed[0]] + [swap(routed[r], 2 * r) for r in range(1, 4)]


def lift(place, lows, highs):
    size, width = highs[0].shape
    return call(
        lift_body,
        (1,),
        [whole(lows[0].shape)] * 4 + [whole((size, width))] * 4,
        [whole((size, width))] * 4,
        [like((size, width), BF)] * 4,
        [],
        (*lows, *highs),
        0,
        24 * size * width,
        place,
    )


def add_four(parts):
    shape = parts[0].shape
    return call(
        sum_body,
        (1,),
        [whole(shape)] * 4,
        whole(shape),
        like(shape, BF),
        [],
        parts,
        0,
        10 * parts[0].size,
    )


def prepare(place, matrices, width):
    rows, roww = matrices.shape
    size = rows * roww // width
    return call(
        prep_body,
        (1,),
        [whole((rows, roww))],
        whole((size, width)),
        like((size, width), BF),
        [pltpu.VMEM((rows, roww), F32)],
        (matrices,),
        0,
        4 * matrices.size,
        place,
    )


def finish(place, qkv_sums, dense_sums, rows, roww):
    size, width = dense_sums[0].shape
    specs = [whole(part.shape) for part in qkv_sums] + [whole((size, width))] * 4
    return call(
        finish_body,
        (1,),
        specs,
        whole((rows, roww)),
        like((rows, roww), F32),
        [pltpu.VMEM((size, width), F32)],
        (*qkv_sums, *dense_sums),
        0,
        20 * size * width,
        place,
    )


def after(value, *deps):
    return lax.optimization_barrier((value, *deps))


def meta_rows(seq_start, valid):
    zeros = jnp.zeros((6, seq_start.shape[0]), F32)
    return jnp.concatenate([seq_start.astype(F32)[None], valid.astype(F32)[None], zeros], axis=0)


def split_vectors(vec_flat, width):
    vec = vec_flat[: 13 * width].reshape(13, width)
    return vec[:8], vec[4:13].reshape(3, 3, width)


def join_vectors(dvec_one, dvec_two, grad_taps, total, roww):
    width = dvec_one.shape[1]
    taps = jnp.concatenate(grad_taps, axis=-1).reshape(9, width)
    rows = jnp.concatenate([dvec_one[:2], dvec_two[:2], taps], axis=0).reshape(-1)
    return jnp.pad(rows, (0, total - rows.size)).reshape(-1, roww)


def per_device(tokens_in, grad_out, seq_start, valid, matrices, vectors):
    width = tokens_in.shape[1]
    rows, roww = matrices.shape
    linear = lax.axis_index(AXES)
    plane = plane_of(linear)
    place = (linear >> jnp.array([0, 3, 0, 1, 0])) & jnp.array([31, 3, 7, 3, 1])
    near_planes = jnp.stack([1 - jnp.minimum(plane, 1), 2 - plane // 2, 3 - plane // 3])
    place = jnp.concatenate([place, near_planes])
    meta = meta_rows(seq_start, valid)
    shard = prepare(place, matrices, width)

    def up(value, steps, keep):
        pairs = [(i, i + 8 * steps) for i in range(SHARDS) if plane_of(i) in keep]
        return lax.ppermute(value, AXES, pairs)

    vec_flat = lax.all_to_all(jnp.tile(vectors, (SHARDS, 1)), AXES, 0, 0, tiled=True)
    vec_flat = vec_flat.reshape(-1).astype(F32)
    vec, taps = split_vectors(vec_flat, width)

    def spread(held):
        chips = [held] + [swap(held, 2 * r) for r in range(1, 4)]
        return chips

    def with_partner(chips):
        bufs = []
        for chip in chips:
            bufs += [chip, swap(chip, 1)]
        return bufs

    jump = up(shard, 2, (0,))
    left_one = up(shard, -1, (1, 2, 3))
    own_chips = spread(shard)
    hop = up(jnp.where(plane == 2, jump, shard), 1, (0, 2))
    left_two = up(left_one, -1, (2, 1))
    left_three = up(left_two, -1, (1,))
    near_one = jnp.where(plane == 0, left_one, jnp.where(plane == 2, jump, hop))
    shard_later, near_one = after(shard, near_one)
    near_chips = spread(near_one)
    right_one = up(shard_later, 1, (1, 2))
    right_two = up(right_one, 1, (2,))
    low = jnp.where(plane == 0, left_two, jnp.where(plane == 1, left_one, jnp.where(plane == 2, right_one, right_two)))
    high = jnp.where(plane == 0, left_three, jnp.where(plane == 1, left_two, jnp.where(plane == 2, left_one, right_one)))
    far = jnp.stack([low, high])
    far, *near_chips = after(far, *near_chips)
    far_chips = spread(far)
    own = with_partner(own_chips)
    near = with_partner(near_chips)
    low_one, mixed, project, attended, lse = forward(place, tokens_in, meta, own, near, vec, taps)
    attended, *far_chips = after(attended, *far_chips)
    far = with_partner(far_chips)
    bufs = (*own, *near, *far)
    residual, low_two, cot, positive, mine_three, other_three, first = dense_up(
        place, tokens_in, grad_out, meta, attended, bufs, vec
    )
    got_three = swap(other_three, 1)
    block_out, grad_att, grad_res, dvec_two, mine_low, other_low = dense_down(
        place, attended, low_two, residual, cot, positive, vec, first, bufs
    )
    highs = in_plane(split_core(place, mine_three, got_three))
    got_low = swap(other_low, 1)
    grad_att, *highs = after(grad_att, *highs)
    lows = split_core(place, mine_low, got_low)
    grad_att, *lows = after(grad_att, *lows)
    lows = in_plane(lows)
    half_a, half_b = HALVES
    mixed_a = attend_back(half_a, mixed, grad_att, attended, lse, meta)
    mine_a, other_a, taps_a, grad_part = post(
        place, half_a, mixed_a, project, taps, low_one, meta, own, near, None
    )
    got_a = swap(other_a, 1)
    qkv_a = split_core(place, mine_a, got_a)
    grad_att, *qkv_a = after(grad_att, *qkv_a)
    qkv_a = in_plane(qkv_a)
    mixed_b = attend_back(half_b, mixed, grad_att, attended, lse, meta)
    mine_b, other_b, taps_b, tokens_grad, dvec_one = post(
        place, half_b, mixed_b, project, taps, low_one, meta, own, near,
        (tokens_in, grad_res, vec, grad_part),
    )
    lifted = lift(place, lows, highs)
    dense_sums = [lifted[0]] + [
        swap(lifted[k], 8 * k, lambda i, k=k: plane_of(i) ^ k != 0) for k in (1, 2, 3)
    ]

    def to_first(parts):
        total = add_four(parts)
        return [total] + [swap(total, 8 * k, lambda i, k=k: plane_of(i) == k) for k in (1, 2, 3)]

    sums_a = to_first(qkv_a)
    sums_b = to_first(in_plane(split_core(place, mine_b, swap(other_b, 1))))
    owned = finish(place, (*sums_a, *sums_b), dense_sums, rows, roww)
    grad_vec = join_vectors(dvec_one, dvec_two, (taps_a, taps_b), vec_flat.size, roww)
    owned_vec = lax.all_to_all(grad_vec, AXES, 0, 0, tiled=True)
    owned_vec = owned_vec.reshape(SHARDS, *vectors.shape).sum(axis=0)
    return block_out, tokens_grad, owned, owned_vec


def per_device_any(tokens_in, grad_out, seq_start, valid, matrices, vectors):
    width = tokens_in.shape[1]
    rows, roww = matrices.shape
    step = GROUP // FOLD
    place = jnp.array([0, 0, 0, 0, 0, 1, 2, 3], jnp.int32)
    meta = meta_rows(seq_start, valid)
    view = lax.all_gather(matrices, AXES, axis=0, tiled=True).reshape(-1, width)
    vec_flat = lax.all_gather(vectors, AXES, axis=0, tiled=True).reshape(-1).astype(F32)
    vec, taps = split_vectors(vec_flat, width)
    cut = (UP_FIRST * GROUP, UP_END * GROUP)
    up = view[cut[0] : cut[1]].reshape(UP_GROUPS, step, FOLD, width).swapaxes(1, 2)
    view = jnp.concatenate([view[: cut[0]], up.reshape(-1, width), view[cut[1] :]])
    shards = view.reshape(4, 8, -1, width)
    own = [shards[0, r] for r in range(8)]
    near = [shards[1, r] for r in range(8)]
    far = [shards[2:, r] for r in range(8)]
    low_one, mixed, project, attended, lse = forward(place, tokens_in, meta, own, near, vec, taps)
    bufs = (*own, *near, *far)
    residual, low_two, cot, positive, mine_three, other_three, first = dense_up(
        place, tokens_in, grad_out, meta, attended, bufs, vec
    )
    block_out, grad_att, grad_res, dvec_two, mine_low, other_low = dense_down(
        place, attended, low_two, residual, cot, positive, vec, first, bufs
    )
    qkv, grad_taps, part = [], [], None
    for half in HALVES:
        tail = None if part is None else (tokens_in, grad_res, vec, part)
        grad_mixed = attend_back(half, mixed, grad_att, attended, lse, meta)
        result = post(place, half, grad_mixed, project, taps, low_one, meta, own, near, tail)
        qkv.append(jnp.stack(result[:2], axis=1))
        grad_taps.append(result[2])
        part = result[3]
    tokens_grad, dvec_one = result[3:]
    planes = [
        jnp.concatenate(qkv, axis=-1)[:, :, None],
        jnp.stack([mine_low, other_low], axis=1),
        jnp.stack([mine_three, other_three], axis=1)[:, :, None],
    ]
    grad = jnp.concatenate(planes, axis=2)
    grad = grad.transpose(2, 0, 1, 3, 4).reshape(-1, width)
    up = grad[cut[0] : cut[1]].reshape(UP_GROUPS, FOLD, step, width).swapaxes(1, 2)
    grad = jnp.concatenate([grad[: cut[0]], up.reshape(-1, width), grad[cut[1] :]])
    owned = lax.psum_scatter(
        grad.reshape(-1, roww).astype(F32), AXES, scatter_dimension=0, tiled=True
    )
    grad_vec = join_vectors(dvec_one, dvec_two, grad_taps, vec_flat.size, roww)
    owned_vec = lax.psum_scatter(grad_vec, AXES, scatter_dimension=0, tiled=True)
    return block_out, tokens_grad, owned, owned_vec


def solution(mesh):
    row = P(AXES, None)
    flat = P(AXES)
    body = per_device if mesh.shape["dp"] * mesh.shape["sub"] == SHARDS else per_device_any
    return jax.shard_map(
        body,
        mesh=mesh,
        in_specs=(row, row, flat, flat, row, row),
        out_specs=(row, row, row, row),
        check_vma=False,
    )
```

```python
import functools

import jax
import jax.numpy as jnp
from jax import lax
from jax.experimental import pallas as pl
from jax.experimental.pallas import tpu as pltpu
from jax.sharding import Mesh
from jax.sharding import PartitionSpec as P

HEADS = 12
EPSILON = 1e-05
NEG_FILL = -1e30
BF = jnp.bfloat16
F32 = jnp.float32
AXES = ("dp", "sub")
FINE = ("z", "x", "y", "core")
SQUARE = ("x", "y")
VMEM_BYTES = 60 * 1024 * 1024
LANES = 128
BLOCK = 256
GROUP = 96
FOLD = 4
SHARDS = 32
WEIGHT = 100
OUT_GROUPS = 8
UP_GROUPS = 32
UP_FIRST, UP_END = 32, 64
HALVES = ((0, 4), (4, 2))
PIECES = ((0, 2), (2, 2))
(
    PLACE_LINEAR, PLACE_Z, PLACE_IN_PLANE, PLACE_XY, PLACE_CORE,
    PLACE_NEAR, PLACE_LOW, PLACE_HIGH,
) = range(8)
HBM = pl.BlockSpec(memory_space=pl.ANY)


def dot(a, b):
    return jnp.dot(a, b, preferred_element_type=F32)


def dot_nt(a, b):
    return lax.dot_general(a, b, (((1,), (1,)), ((), ())), preferred_element_type=F32)


def dot_tn(a, b):
    return lax.dot_general(a, b, (((0,), (0,)), ((), ())), preferred_element_type=F32)


def whole(shape):
    return pl.BlockSpec(shape, lambda *_: (0,) * len(shape))


def fixed(shape):
    return pl.BlockSpec(shape, lambda *_: (0,) * len(shape), pipeline_mode=pl.Buffered(1))


def call(body, grid, ins, outs, out_shape, scratch, args, flops, moved, place=None):
    return pl.pallas_call(
        body,
        grid_spec=pltpu.PrefetchScalarGridSpec(
            num_scalar_prefetch=0 if place is None else 1,
            grid=grid,
            in_specs=ins,
            out_specs=outs,
            scratch_shapes=scratch,
        ),
        out_shape=out_shape,
        compiler_params=pltpu.CompilerParams(
            dimension_semantics=("arbitrary",) * len(grid), vmem_limit_bytes=VMEM_BYTES
        ),
        cost_estimate=pl.CostEstimate(
            flops=WEIGHT * flops, bytes_accessed=WEIGHT * moved, transcendentals=0
        ),
    )(*(() if place is None else (place,)), *args)


def like(shape, dtype):
    return jax.ShapeDtypeStruct(shape, dtype)


def normalize(v):
    centre = v - jnp.mean(v, axis=-1, keepdims=True)
    scaled = lax.rsqrt(jnp.mean(centre * centre, axis=-1, keepdims=True) + EPSILON)
    return centre * scaled, scaled


def norm_back(incoming, normed, scaled, gain):
    weighted = incoming * gain
    return scaled * (
        weighted
        - jnp.mean(weighted, axis=-1, keepdims=True)
        - normed * jnp.mean(weighted * normed, axis=-1, keepdims=True)
    )


def columns(meta):
    return jnp.transpose(meta, (1, 0))


def mix_masks(meta_ref, slots):
    cols = columns(meta_ref[...])
    position = lax.broadcasted_iota(jnp.int32, (slots, 1), 0).astype(F32) - cols[:, 0:1]
    return jnp.where(position >= 1.0, 1.0, 0.0), jnp.where(position >= 2.0, 1.0, 0.0)


def xor_pairs(mask, keep=None):
    return [(i, i ^ mask) for i in range(SHARDS) if keep is None or keep(i)]


def swap(value, mask, keep=None):
    return lax.ppermute(value, FINE, xor_pairs(mask, keep))


def plane_of(index):
    return index >> 3


def prep_body(place_ref, in_ref, out_ref, wide_ref):
    width = out_ref.shape[1]
    cols = width // LANES
    wide_ref[...] = in_ref[...].astype(F32)
    first = place_ref[PLACE_LINEAR] * (out_ref.shape[0] // GROUP)
    for n in range(out_ref.shape[0] // GROUP):
        base = n * GROUP * cols
        up = jnp.logical_and(first + n >= UP_FIRST, first + n < UP_END)

        @pl.when(up)
        def _():
            for j in range(cols):
                parts = [
                    wide_ref[pl.ds(base + q * cols + j, GROUP // FOLD, stride=cols * FOLD), :]
                    for q in range(FOLD)
                ]
                out_ref[n * GROUP : (n + 1) * GROUP, j * LANES : (j + 1) * LANES] = (
                    jnp.concatenate(parts, axis=0).astype(BF)
                )

        @pl.when(jnp.logical_not(up))
        def _():
            for j in range(cols):
                out_ref[n * GROUP : (n + 1) * GROUP, j * LANES : (j + 1) * LANES] = wide_ref[
                    pl.ds(base + j, GROUP, stride=cols), :
                ].astype(BF)


def finish_body(place_ref, *refs):
    halves = len(HALVES)
    zero = [refs[4 * h : 4 * h + 4] for h in range(halves)]
    middle, last = refs[4 * halves : 4 * halves + 4], refs[4 * halves + 4 : 4 * halves + 8]
    out_ref, total_ref = refs[-2:]
    width = total_ref.shape[1]
    cols = width // LANES
    plane = place_ref[PLACE_Z]

    def add(parts):
        total = parts[0][...].astype(F32)
        for part in parts[1:]:
            total = total + part[...].astype(F32)
        return total

    @pl.when(plane == 0)
    def _():
        for (at, count), parts in zip(HALVES, zero):
            total_ref[:, at * LANES : (at + count) * LANES] = add(parts)

    @pl.when(jnp.logical_or(plane == 1, plane == 2))
    def _():
        total_ref[...] = add(middle)

    @pl.when(plane == 3)
    def _():
        total_ref[...] = add(last)

    first = place_ref[PLACE_LINEAR] * (total_ref.shape[0] // GROUP)
    for n in range(total_ref.shape[0] // GROUP):
        base = n * GROUP * cols
        up = jnp.logical_and(first + n >= UP_FIRST, first + n < UP_END)

        @pl.when(up)
        def _():
            step = GROUP // FOLD
            for j in range(cols):
                for q in range(FOLD):
                    lo = n * GROUP + q * step
                    out_ref[pl.ds(base + q * cols + j, step, stride=cols * FOLD), :] = total_ref[
                        lo : lo + step, j * LANES : (j + 1) * LANES
                    ]

        @pl.when(jnp.logical_not(up))
        def _():
            for j in range(cols):
                out_ref[pl.ds(base + j, GROUP, stride=cols), :] = total_ref[
                    n * GROUP : (n + 1) * GROUP, j * LANES : (j + 1) * LANES
                ]


def route_body(place_ref, mine_ref, other_ref, *outs):
    for r, out in enumerate(outs):
        at = place_ref[PLACE_XY] ^ r
        out[...] = (mine_ref[at].astype(F32) + other_ref[at].astype(F32)).astype(BF)


def lift_body(place_ref, in_ref, *outs):
    plane = place_ref[PLACE_Z]
    for k, out in enumerate(outs):
        p = jnp.clip(plane ^ k, 1, 2) - 1
        total = in_ref[0, p].astype(F32)
        for r in range(1, 4):
            total = total + in_ref[r, p].astype(F32)
        out[...] = total.astype(BF)


def sum_body(a_ref, b_ref, c_ref, d_ref, out_ref):
    out_ref[...] = (
        a_ref[...].astype(F32) + b_ref[...].astype(F32) + c_ref[...].astype(F32) + d_ref[...].astype(F32)
    ).astype(BF)


def start_qkv(place_ref, own, near, w_ref, sem):
    size = own[0].shape[0]
    for r in range(8):
        at = pl.multiple_of((place_ref[PLACE_IN_PLANE] ^ r) * size, 32)

        @pl.when(place_ref[PLACE_Z] == 0)
        def _():
            pltpu.make_async_copy(own[r], w_ref.at[pl.ds(at, size)], sem).start()

        @pl.when(place_ref[PLACE_Z] != 0)
        def _():
            pltpu.make_async_copy(near[r], w_ref.at[pl.ds(at, size)], sem).start()


def wait_all(ref, sem):
    pltpu.make_async_copy(ref, ref, sem).wait()


def start_dense(place_ref, own, near, far, wo_ref, w1_ref, w2_ref, sems):
    step = GROUP // FOLD
    width = own[0].shape[1]
    slots = [(own, None, PLACE_Z, (1, 2, 3)), (near, None, PLACE_NEAR, (1,))]
    slots += [(far, 0, PLACE_LOW, (1, 2)), (far, 1, PLACE_HIGH, (2, 3))]
    for bufs, slot, plane_at, planes in slots:
        for p in planes:

            @pl.when(place_ref[plane_at] == p)
            def _():
                for r in range(8):
                    buf = bufs[r] if slot is None else bufs[r].at[slot]
                    place = place_ref[PLACE_IN_PLANE] ^ r
                    for n in range(3):
                        group = 24 * (p - 1) + 3 * place + n
                        rows = buf.at[pl.ds(n * GROUP, GROUP)]

                        def to_out():
                            at = pl.multiple_of(group * GROUP, 32)
                            pltpu.make_async_copy(
                                rows, wo_ref.at[pl.ds(at, GROUP)], sems.at[0]
                            ).start()

                        def to_up():
                            at = pl.multiple_of((group - OUT_GROUPS) * step, 8)
                            pltpu.make_async_copy(
                                rows.reshape(FOLD, step, width),
                                w1_ref.at[:, pl.ds(at, step)],
                                sems.at[1],
                            ).start()

                        def to_down():
                            at = pl.multiple_of((group - OUT_GROUPS - UP_GROUPS) * GROUP, 32)
                            pltpu.make_async_copy(
                                rows, w2_ref.at[pl.ds(at, GROUP)], sems.at[2]
                            ).start()

                        if p == 1:
                            pl.when(group < OUT_GROUPS)(to_out)
                            pl.when(group >= OUT_GROUPS)(to_up)
                        elif p == 2:
                            pl.when(group < OUT_GROUPS + UP_GROUPS)(to_up)
                            if w2_ref is not None:
                                pl.when(group >= OUT_GROUPS + UP_GROUPS)(to_down)
                        elif w2_ref is not None:
                            to_down()


def deal(place_ref, targets, sems, copy):
    core = place_ref[PLACE_CORE]
    for j in range(8):
        for which in range(2):

            @pl.when(core ^ (j % 2) == which)
            def _():
                copy(j, targets[which].at[j // 2], sems.at[which])


def pre_body(place_ref, x_ref, vec_ref, taps_ref, meta_ref, *refs):
    own, near, (low_ref, mixed_ref, proj_ref, w_ref, sem) = refs[:8], refs[8:16], refs[16:]
    slots, width = x_ref.shape
    here = pl.multiple_of(pl.program_id(0) * width, width)

    @pl.when(pl.program_id(0) == 0)
    def _():
        start_qkv(place_ref, own, near, w_ref, sem)
        for lo in range(0, slots, BLOCK):
            rows = slice(lo, lo + BLOCK)
            normed, _ = normalize(x_ref[rows, :].astype(F32))
            low_ref[rows, :] = (normed * vec_ref[0:1, :] + vec_ref[1:2, :]).astype(BF)
        wait_all(w_ref, sem)

    first, second = mix_masks(meta_ref, slots)
    proj_ref[...] = dot(low_ref[...], w_ref[pl.ds(here, width), :])
    value = proj_ref[...]
    one_back = pltpu.roll(value, 1, 0) * first
    two_back = pltpu.roll(value, 2, 0) * second
    mixed_ref[...] = (
        taps_ref[0:1, :] * value + taps_ref[1:2, :] * one_back + taps_ref[2:3, :] * two_back
    ).astype(BF)


def attend_body(scale, q_ref, k_ref, v_ref, meta_ref, out_ref, lse_ref, bias_ref, va_ref):
    slots = q_ref.shape[0]
    half = LANES // 2

    @pl.when(pl.program_id(0) == 0)
    def _():
        cols = columns(meta_ref[...])
        for lo in range(0, slots, BLOCK):
            end = lo + BLOCK
            starts = cols[lo:end, 0:1]
            row = lax.broadcasted_iota(jnp.int32, (BLOCK, end), 0) + lo
            col = lax.broadcasted_iota(jnp.int32, (BLOCK, end), 1)
            keep = (starts == meta_ref[0:1, :end]) & (meta_ref[1:2, :end] > 0.5) & (col <= row)
            bias_ref[lo:end, :end] = jnp.where(keep, 0.0, NEG_FILL)

    left = lax.broadcasted_iota(jnp.int32, (1, LANES), 1) < half
    value = v_ref[...]
    one = jnp.ones_like(value)
    va_ref[0, :, :] = jnp.where(left, value, one)
    va_ref[1, :, :] = jnp.where(left, one, value)
    for lo in range(0, slots, BLOCK):
        end = lo + BLOCK
        query = q_ref[lo:end, :] * jnp.asarray(scale, BF)
        outs, logs = [], []
        for head in range(2):
            own = left if head == 0 else jnp.logical_not(left)
            scores = dot_nt(jnp.where(own, query, jnp.zeros_like(query)), k_ref[:end, :])
            scores = scores + bias_ref[lo:end, :end]
            peak = jnp.max(scores, axis=-1, keepdims=True)
            terms = jnp.exp(scores - peak).astype(BF)
            both = dot(terms, va_ref[head, :end, :])
            outs.append(both / pltpu.roll(both, half, 1))
            logs.append(peak + jnp.log(both))
        out_ref[lo:end, :] = jnp.where(left, outs[0], outs[1]).astype(BF)
        lse_ref[lo:end, :] = jnp.where(left, logs[1], logs[0])


def up_body(place_ref, att_ref, x_ref, go_ref, meta_ref, vec_ref, *refs):
    own, near, far = refs[:8], refs[8:16], refs[16:24]
    (
        res_ref, low_ref, cot_ref, pos_ref, mine_ref, other_ref, first_ref,
        wo_ref, w1_ref, act_ref, cots_ref, g2_ref, sems,
    ) = refs[24:]
    width = x_ref.shape[1]
    step = pl.program_id(0)
    blocks = act_ref.shape[0] // BLOCK
    here = pl.multiple_of(step * BLOCK, BLOCK)

    @pl.when(step == 0)
    def _():
        start_dense(place_ref, own, near, far, wo_ref, w1_ref, None, sems)
        wait_all(wo_ref, sems.at[0])

    @pl.when(step < blocks)
    def _():
        live = columns(meta_ref[...])[:, 1:2]
        residual = x_ref[...].astype(F32) + dot(att_ref[...], wo_ref[...])
        res_ref[...] = residual
        normed, _ = normalize(residual)
        low = (normed * vec_ref[2:3, :] + vec_ref[3:4, :]).astype(BF)
        low_ref[...] = low
        cot = (go_ref[...].astype(F32) * live).astype(BF)
        cot_ref[...] = cot
        cots_ref[pl.ds(here, BLOCK), :] = cot

        @pl.when(step == 0)
        def _():
            wait_all(w1_ref, sems.at[1])

        for part in range(FOLD):
            cut = slice(part * width, (part + 1) * width)
            upward = jnp.maximum(dot(low, w1_ref[part]), 0.0)
            pos_ref[:, cut] = upward
            act_ref[pl.ds(here, BLOCK), cut] = (upward * upward).astype(BF)

    for part in range(FOLD):

        @pl.when(step == blocks + part)
        def _():
            cut = slice(part * width, (part + 1) * width)
            g2_ref[cut, :] = dot_tn(act_ref[:, cut], cots_ref[...]).astype(BF)

    @pl.when(step == blocks + FOLD - 1)
    def _():
        size = mine_ref.shape[1]
        skip = g2_ref.shape[0] - 8 * size

        def copy(j, target, sem):
            pltpu.make_async_copy(g2_ref.at[pl.ds(skip + j * size, size)], target, sem).start()

        deal(place_ref, (mine_ref, other_ref), sems, copy)
        first_ref[...] = g2_ref[0:skip, :]
        wait_all(mine_ref, sems.at[0])
        wait_all(other_ref, sems.at[1])


def down_body(
    place_ref, att_ref, low_ref, res_ref, cot_ref, pos_ref, vec_ref, first_ref, *refs
):
    own, near, far = refs[:8], refs[8:16], refs[16:24]
    (
        out_ref, gatt_ref, gres_ref, dvec_ref, mine_ref, other_ref,
        wo_ref, w1_ref, w2_ref, up_ref, reslow_ref, g1_ref, go_ref, sems,
    ) = refs[24:]
    width = res_ref.shape[1]
    step = pl.program_id(0)
    blocks = up_ref.shape[0] // BLOCK
    here = pl.multiple_of(step * BLOCK, BLOCK)

    @pl.when(step == 0)
    def _():
        start_dense(place_ref, own, near, far, wo_ref, w1_ref, w2_ref, sems)
        dvec_ref[...] = jnp.zeros_like(dvec_ref)
        wait_all(w2_ref, sems.at[2])
        wait_all(w1_ref, sems.at[1])
        wait_all(wo_ref, sems.at[0])

    @pl.when(step < blocks)
    def _():
        residual = res_ref[...]
        normed, scaled = normalize(residual)
        cot = cot_ref[...]
        total = residual
        grad = jnp.zeros_like(residual)
        for part in range(FOLD):
            cut = slice(part * width, (part + 1) * width)
            upward = pos_ref[:, cut]
            total = total + dot((upward * upward).astype(BF), w2_ref[cut, :])
            grad_up = (dot_nt(cot, w2_ref[cut, :]) * (2.0 * upward)).astype(BF)
            up_ref[pl.ds(here, BLOCK), cut] = grad_up
            grad = grad + dot_nt(grad_up, w1_ref[part])
        out_ref[...] = total.astype(BF)
        grad_residual = cot.astype(F32) + norm_back(grad, normed, scaled, vec_ref[2:3, :])
        gres_ref[...] = grad_residual
        res_low = grad_residual.astype(BF)
        reslow_ref[pl.ds(here, BLOCK), :] = res_low
        gatt_ref[...] = dot_nt(res_low, wo_ref[...]).astype(BF)
        dvec_ref[0:1, :] += jnp.sum(grad * normed, axis=0, keepdims=True)
        dvec_ref[1:2, :] += jnp.sum(grad, axis=0, keepdims=True)

    for part in range(FOLD):

        @pl.when(step == blocks + part)
        def _():
            cut = slice(part * width, (part + 1) * width)
            g1_ref[part] = dot_tn(low_ref[...], up_ref[:, cut]).astype(BF)

    @pl.when(step == blocks + FOLD - 1)
    def _():
        go_ref[...] = dot_tn(att_ref[...], reslow_ref[...]).astype(BF)
        span = GROUP // FOLD

        def copy(j, target, sem):
            for p in range(2):
                for n in range(3):
                    group = 24 * p + 3 * j + n
                    rows = target.at[p, pl.ds(n * GROUP, GROUP)]
                    if group < OUT_GROUPS:
                        source = go_ref.at[pl.ds(group * GROUP, GROUP)]
                    elif group < OUT_GROUPS + UP_GROUPS:
                        source = g1_ref.at[:, pl.ds((group - OUT_GROUPS) * span, span)]
                        rows = rows.reshape(FOLD, span, width)
                    else:
                        at = (group - OUT_GROUPS - UP_GROUPS) * GROUP
                        source = first_ref.at[pl.ds(at, GROUP)]
                    pltpu.make_async_copy(source, rows, sem).start()

        deal(place_ref, (mine_ref, other_ref), sems, copy)
        wait_all(mine_ref, sems.at[0])
        wait_all(other_ref, sems.at[1])


def split_three(value):
    high = value.astype(BF)
    rest = value - high.astype(F32)
    middle = rest.astype(BF)
    return high, middle, (rest - middle.astype(F32)).astype(BF)


def attend_back_body(
    scale, q_ref, k_ref, v_ref, do_ref, o_ref, lse_ref, meta_ref, grad_ref,
    bias_ref, qa_ref, ka_ref, va_ref, da_ref, kt_ref, dq_ref,
):
    slots = q_ref.shape[0]
    half = LANES // 2

    @pl.when(pl.program_id(0) == 0)
    def _():
        cols = columns(meta_ref[...])
        for lo in range(0, slots, BLOCK):
            end = lo + BLOCK
            size = slots - lo
            row = lax.broadcasted_iota(jnp.int32, (BLOCK, size), 0)
            col = lax.broadcasted_iota(jnp.int32, (BLOCK, size), 1)
            keep = (
                (cols[lo:end, 0:1] == meta_ref[0:1, lo:])
                & (cols[lo:end, 1:2] > 0.5)
                & (row <= col)
            )
            bias_ref[lo:end, lo:] = jnp.where(keep, 0.0, NEG_FILL)

    lane = lax.broadcasted_iota(jnp.int32, (1, LANES), 1)
    left = lane < half
    query = q_ref[...]
    key = k_ref[...]
    value = v_ref[...]
    grad_out = do_ref[...]
    product = grad_out.astype(F32) * o_ref[...].astype(F32)
    kt_ref[...] = jnp.transpose(key.astype(F32), (1, 0)).astype(BF)
    logs = split_three(-lse_ref[...])
    zero = jnp.zeros_like(query)
    one = jnp.ones_like(query)
    for head in range(2):
        own = left if head == 0 else jnp.logical_not(left)
        base = half if head == 0 else 0
        delta = jnp.sum(jnp.where(own, product, 0.0), axis=-1, keepdims=True)
        deltas = split_three(-delta)
        marks = [lane == base + n for n in range(3)]

        def spread(terms):
            result = zero
            for mark, term in zip(marks, terms):
                result = jnp.where(mark, term, result)
            return result

        ones = spread((one, one, one))
        qa_ref[head] = jnp.where(own, query * jnp.asarray(scale, BF), spread(logs))
        ka_ref[head] = jnp.where(own, key, ones)
        va_ref[head] = jnp.where(own, value, ones)
        da_ref[head] = jnp.where(own, grad_out, spread(deltas))
    dq_ref[...] = jnp.zeros_like(dq_ref)
    for lo in range(0, slots, BLOCK):
        end = lo + BLOCK
        grad_keys, grad_values = [], []
        for head in range(2):
            rows = slice(head * half, (head + 1) * half)
            scores = dot_nt(ka_ref[head, lo:end, :], qa_ref[head, lo:, :]) + bias_ref[lo:end, lo:]
            probs = jnp.exp(scores)
            inner = dot_nt(va_ref[head, lo:end, :], da_ref[head, lo:, :])
            grad_scores = (probs * inner).astype(BF)
            grad_values.append(dot(probs.astype(BF), do_ref[lo:, :]))
            grad_keys.append(dot(grad_scores, q_ref[lo:, :]))
            dq_ref[rows, lo:] += dot(kt_ref[rows, lo:end], grad_scores)
        grad_ref[1, lo:end, :] = jnp.where(left, grad_keys[0], grad_keys[1]) * scale
        grad_ref[2, lo:end, :] = jnp.where(left, grad_values[0], grad_values[1])
    grad_ref[0, :, :] = jnp.transpose(dq_ref[...], (1, 0)) * scale


def post_body(count, place_ref, *refs):
    pieces, (proj_ref, taps_ref, low_ref, meta_ref) = refs[:count], refs[count : count + 4]
    mine_ref, other_ref, gtaps_ref, gproj_ref, gw_ref, sems = refs[count + 4 :]
    slots = low_ref.shape[0]
    width = low_ref.shape[1]
    step = pl.program_id(0)
    here = pl.multiple_of(step * width, width)
    first, second = mix_masks(meta_ref, slots)
    mixed = jnp.concatenate([ref[...] for ref in pieces], axis=1)
    proj = proj_ref[...]
    one_up = pltpu.roll(mixed * first, slots - 1, 0)
    two_up = pltpu.roll(mixed * second, slots - 2, 0)
    gtaps_ref[0:1, :] = jnp.sum(mixed * proj, axis=0, keepdims=True)
    gtaps_ref[1:2, :] = jnp.sum(one_up * proj, axis=0, keepdims=True)
    gtaps_ref[2:3, :] = jnp.sum(two_up * proj, axis=0, keepdims=True)
    grad = (
        taps_ref[0:1, :] * mixed + taps_ref[1:2, :] * one_up + taps_ref[2:3, :] * two_up
    ).astype(BF)
    gproj_ref[...] = grad
    gw_ref[pl.ds(here, width), :] = dot_tn(low_ref[...], grad).astype(BF)

    @pl.when(step == 2)
    def _():
        size = mine_ref.shape[1]

        def copy(j, target, sem):
            pltpu.make_async_copy(gw_ref.at[pl.ds(j * size, size)], target, sem).start()

        deal(place_ref, (mine_ref, other_ref), sems, copy)
        wait_all(mine_ref, sems.at[0])
        wait_all(other_ref, sems.at[1])


def back_body(place_ref, *refs):
    halves = len(HALVES)
    grads, (x_ref, gres_ref, vec_ref) = refs[:halves], refs[halves : halves + 3]
    own, near = refs[halves + 3 : halves + 11], refs[halves + 11 : halves + 19]
    out_ref, dvec_ref, w_ref, sem = refs[halves + 19 :]
    width = x_ref.shape[1]

    @pl.when(pl.program_id(0) == 0)
    def _():
        start_qkv(place_ref, own, near, w_ref, sem)
        dvec_ref[...] = jnp.zeros_like(dvec_ref)
        wait_all(w_ref, sem)

    incoming = None
    for c in range(3):
        rows = slice(c * width, (c + 1) * width)
        for (at, count), grad in zip(HALVES, grads):
            term = dot_nt(grad[c], w_ref[rows, at * LANES : (at + count) * LANES])
            incoming = term if incoming is None else incoming + term
    normed, scaled = normalize(x_ref[...].astype(F32))
    out_ref[...] = gres_ref[...] + norm_back(incoming, normed, scaled, vec_ref[0:1, :])
    dvec_ref[0:1, :] += jnp.sum(incoming * normed, axis=0, keepdims=True)
    dvec_ref[1:2, :] += jnp.sum(incoming, axis=0, keepdims=True)


def forward(place, tokens, meta, own, near, vec, taps):
    slots, width = tokens.shape
    pairs = width // LANES
    scale = (width // HEADS) ** (-0.5)
    three = pl.BlockSpec((None, slots, width), lambda c, *_: (c, 0, 0))
    tap = pl.BlockSpec((None, 3, width), lambda c, *_: (c, 0, 0))
    low_one, mixed, project = call(
        pre_body,
        (3,),
        [whole((slots, width)), whole(vec.shape), tap, whole(meta.shape)] + [HBM] * 16,
        [whole((slots, width)), three, three],
        [like((slots, width), BF), like((3, slots, width), BF), like((3, slots, width), F32)],
        [pltpu.VMEM((3 * width, width), BF), pltpu.SemaphoreType.DMA],
        (tokens, vec, taps, meta, *own, *near),
        6 * slots * width * width,
        24 << 20,
        place,
    )
    lane_block = pl.BlockSpec((slots, LANES), lambda p: (0, p))

    def part(c):
        return pl.BlockSpec((None, slots, LANES), lambda p: (c, 0, p))

    attended, lse = call(
        functools.partial(attend_body, scale),
        (pairs,),
        [part(0), part(1), part(2), whole(meta.shape)],
        [lane_block, lane_block],
        [like((slots, width), BF), like((slots, width), F32)],
        [pltpu.VMEM((slots, slots), F32), pltpu.VMEM((2, slots, LANES), BF)],
        (mixed, mixed, mixed, meta),
        2 * slots * slots * width * 2,
        12 << 20,
    )
    return low_one, mixed, project, attended, lse


def dense_up(place, tokens, grad_out, meta, attended, bufs, vec):
    slots, width = tokens.shape
    hidden = FOLD * width
    size = bufs[0].shape[0]
    blocks = slots // BLOCK
    row_block = pl.BlockSpec((BLOCK, width), lambda i, *_: (jnp.minimum(i, blocks - 1), 0))
    wide_block = pl.BlockSpec((BLOCK, hidden), lambda i, *_: (jnp.minimum(i, blocks - 1), 0))
    meta_block = pl.BlockSpec((8, BLOCK), lambda i, *_: (0, jnp.minimum(i, blocks - 1)))
    skip = hidden - 8 * size
    return call(
        up_body,
        (blocks + FOLD,),
        [row_block] * 3 + [meta_block, whole(vec.shape)] + [HBM] * 24,
        [row_block, row_block, row_block, wide_block, HBM, HBM, whole((skip, width))],
        [
            like((slots, width), F32),
            like((slots, width), BF),
            like((slots, width), BF),
            like((slots, hidden), F32),
            like((4, size, width), BF),
            like((4, size, width), BF),
            like((skip, width), BF),
        ],
        [
            pltpu.VMEM((width, width), BF),
            pltpu.VMEM((FOLD, width, width), BF),
            pltpu.VMEM((slots, hidden), BF),
            pltpu.VMEM((slots, width), BF),
            pltpu.VMEM((hidden, width), BF),
            pltpu.SemaphoreType.DMA((3,)),
        ],
        (attended, tokens, grad_out, meta, vec, *bufs),
        (4 * FOLD + 2) * slots * width * width,
        30 << 20,
        place,
    )


def dense_down(place, attended, low, residual, cot, positive, vec, first, bufs):
    slots, width = residual.shape
    hidden = FOLD * width
    size = bufs[0].shape[0]
    blocks = slots // BLOCK
    row_block = pl.BlockSpec((BLOCK, width), lambda i, *_: (jnp.minimum(i, blocks - 1), 0))
    wide_block = pl.BlockSpec((BLOCK, hidden), lambda i, *_: (jnp.minimum(i, blocks - 1), 0))
    full = fixed((slots, width))
    return call(
        down_body,
        (blocks + FOLD,),
        [full, full, row_block, row_block, wide_block, whole(vec.shape), whole(first.shape)]
        + [HBM] * 24,
        [row_block, row_block, row_block, whole((8, width)), HBM, HBM],
        [
            like((slots, width), BF),
            like((slots, width), BF),
            like((slots, width), F32),
            like((8, width), F32),
            like((4, 2, size, width), BF),
            like((4, 2, size, width), BF),
        ],
        [
            pltpu.VMEM((width, width), BF),
            pltpu.VMEM((FOLD, width, width), BF),
            pltpu.VMEM((hidden, width), BF),
            pltpu.VMEM((slots, hidden), BF),
            pltpu.VMEM((slots, width), BF),
            pltpu.VMEM((FOLD, width, width), BF),
            pltpu.VMEM((width, width), BF),
            pltpu.SemaphoreType.DMA((3,)),
        ],
        (attended, low, residual, cot, positive, vec, first, *bufs),
        (8 * FOLD + 4) * slots * width * width,
        36 << 20,
        place,
    )


def attend_back(half, mixed, grad_att, attended, lse, meta):
    slots, width = grad_att.shape
    at, count = half
    lane_block = pl.BlockSpec((slots, LANES), lambda p: (0, p + at))

    def part(c):
        return pl.BlockSpec((None, slots, LANES), lambda p: (c, 0, p + at))

    return call(
        functools.partial(attend_back_body, (width // HEADS) ** (-0.5)),
        (count,),
        [part(0), part(1), part(2), lane_block, lane_block, lane_block, whole(meta.shape)],
        pl.BlockSpec((3, slots, LANES), lambda p: (0, 0, p)),
        like((3, slots, count * LANES), F32),
        [
            pltpu.VMEM((slots, slots), F32),
            pltpu.VMEM((2, slots, LANES), BF),
            pltpu.VMEM((2, slots, LANES), BF),
            pltpu.VMEM((2, slots, LANES), BF),
            pltpu.VMEM((2, slots, LANES), BF),
            pltpu.VMEM((LANES, slots), BF),
            pltpu.VMEM((LANES, slots), F32),
        ],
        (mixed, mixed, mixed, grad_att, attended, lse, meta),
        10 * slots * slots * count * LANES,
        20 << 20,
    )


def post(place, half, grad_mixed, project, taps, low, meta, size):
    slots, width = low.shape
    at, lanes = half[0] * LANES, half[1] * LANES
    wide = pl.BlockSpec((None, slots, lanes), lambda c, *_: (c, 0, at // lanes))
    tap = pl.BlockSpec((None, 3, lanes), lambda c, *_: (c, 0, at // lanes))
    pieces = [pl.BlockSpec((None, *g.shape[1:]), lambda c, *_: (c, 0, 0)) for g in grad_mixed]
    return call(
        functools.partial(post_body, len(grad_mixed)),
        (3,),
        pieces + [wide, tap, whole((slots, width)), whole(meta.shape)],
        [
            HBM,
            HBM,
            pl.BlockSpec((None, 3, lanes), lambda c, *_: (c, 0, 0)),
            pl.BlockSpec((None, slots, lanes), lambda c, *_: (c, 0, 0)),
        ],
        [
            like((4, size, lanes), BF),
            like((4, size, lanes), BF),
            like((3, 3, lanes), F32),
            like((3, slots, lanes), BF),
        ],
        [pltpu.VMEM((3 * width, lanes), BF), pltpu.SemaphoreType.DMA((2,))],
        (*grad_mixed, project, taps, low, meta),
        6 * slots * width * lanes,
        24 << 20,
        place,
    )


def back(place, grads, tokens, grad_res, vec, own, near):
    slots, width = tokens.shape
    row_block = pl.BlockSpec((BLOCK, width), lambda i, *_: (i, 0))
    specs = [pl.BlockSpec((3, BLOCK, g.shape[2]), lambda i, *_: (0, i, 0)) for g in grads]
    return call(
        back_body,
        (slots // BLOCK,),
        specs + [row_block, row_block, whole(vec.shape)] + [HBM] * 16,
        [row_block, whole((8, width))],
        [like((slots, width), F32), like((8, width), F32)],
        [pltpu.VMEM((3 * width, width), BF), pltpu.SemaphoreType.DMA],
        (*grads, tokens, grad_res, vec, *own, *near),
        6 * slots * width * width,
        20 << 20,
        place,
    )


def split_core(place, mine, received):
    block = mine.shape[1:]
    return call(
        route_body,
        (1,),
        [whole(mine.shape)] * 2,
        [whole(block)] * 4,
        [like(block, BF)] * 4,
        [],
        (mine, received),
        0,
        3 * mine.size * 2,
        place,
    )


def in_plane(routed):
    return [routed[0]] + [swap(routed[r], 2 * r) for r in range(1, 4)]


def lift(place, blocks):
    shape = blocks.shape[2:]
    return call(
        lift_body,
        (1,),
        [whole(blocks.shape)],
        [whole(shape)] * 4,
        [like(shape, BF)] * 4,
        [],
        (blocks,),
        0,
        3 * blocks.size,
        place,
    )


def send_planes(total, target):
    return [total] + [
        swap(total, 8 * k, lambda i, k=k: plane_of(i) ^ k == target) for k in (1, 2, 3)
    ]


def add_four(parts):
    shape = parts[0].shape
    return call(
        sum_body,
        (1,),
        [whole(shape)] * 4,
        whole(shape),
        like(shape, BF),
        [],
        parts,
        0,
        10 * parts[0].size,
    )


def prepare(place, matrices, width):
    rows, roww = matrices.shape
    size = rows * roww // width
    return call(
        prep_body,
        (1,),
        [whole((rows, roww))],
        whole((size, width)),
        like((size, width), BF),
        [pltpu.VMEM((rows, roww), F32)],
        (matrices,),
        0,
        4 * matrices.size,
        place,
    )


def finish(place, sums, rows, roww):
    size, width = sums[-1].shape
    return call(
        finish_body,
        (1,),
        [whole(part.shape) for part in sums],
        whole((rows, roww)),
        like((rows, roww), F32),
        [pltpu.VMEM((size, width), F32)],
        sums,
        0,
        28 * size * width,
        place,
    )


def after(value, *deps):
    return lax.optimization_barrier((value, *deps))


def meta_rows(seq_start, valid):
    zeros = jnp.zeros((6, seq_start.shape[0]), F32)
    return jnp.concatenate([seq_start.astype(F32)[None], valid.astype(F32)[None], zeros], axis=0)


def split_vectors(vec_flat, width):
    vec = vec_flat[: 13 * width].reshape(13, width)
    return vec[:8], vec[4:13].reshape(3, 3, width)


def join_vectors(dvec_one, dvec_two, grad_taps, total, roww):
    width = dvec_one.shape[1]
    taps = jnp.concatenate(grad_taps, axis=-1).reshape(9, width)
    rows = jnp.concatenate([dvec_one[:2], dvec_two[:2], taps], axis=0).reshape(-1)
    return jnp.pad(rows, (0, total - rows.size)).reshape(-1, roww)


def per_device(tokens_in, grad_out, seq_start, valid, matrices, vectors):
    width = tokens_in.shape[1]
    rows, roww = matrices.shape
    linear = lax.axis_index(FINE)
    plane = plane_of(linear)
    place = (linear >> jnp.array([0, 3, 0, 1, 0])) & jnp.array([31, 3, 7, 3, 1])
    near_planes = jnp.stack([1 - jnp.minimum(plane, 1), 2 - plane // 2, 3 - plane // 3])
    place = jnp.concatenate([place, near_planes])
    meta = meta_rows(seq_start, valid)
    shard = prepare(place, matrices, width)

    def up(value, steps, keep):
        pairs = [(i, i + 8 * steps) for i in range(SHARDS) if plane_of(i) in keep]
        return lax.ppermute(value, FINE, pairs)

    def with_partner(chips):
        bufs = []
        for chip in chips:
            bufs += [chip, swap(chip, 1)]
        return bufs

    def spread(held):
        by_y, by_x = swap(held, 2), swap(held, 4)
        return [held, by_y, by_x, swap(held, 6)]

    pairs = [(i, i + 16) for i in range(8)] + [(i, i + 8) for i in range(16, 24)]
    jump = lax.ppermute(shard, FINE, pairs)
    left_one = up(shard, -1, (1, 2, 3))
    own_y, own_x, own_both = spread(shard)[1:]
    jump, own_y, own_x = after(jump, own_y, own_x)
    hop = up(jnp.where(plane == 2, jump, shard), 1, (0, 1, 2))
    left_two = up(left_one, -1, (2, 1))
    near_one = jnp.where(plane == 0, left_one, jnp.where(plane == 2, jump, hop))
    near_one, hop, left_two, vectors_later, own_both = after(
        near_one, hop, left_two, vectors, own_both
    )
    own_chips = [shard, own_y, own_x, own_both]
    vec_flat = lax.all_to_all(jnp.tile(vectors_later, (SHARDS, 1)), FINE, 0, 0, tiled=True)
    near_chips = spread(near_one)
    left_three = up(left_two, -1, (1,))
    right_two = up(hop, 1, (2,))
    low = jnp.where(plane == 1, left_one, jnp.where(plane == 2, hop, right_two))
    low = jnp.where(plane == 0, left_two, low)
    high = jnp.where(plane == 1, left_two, jnp.where(plane == 2, left_one, jump))
    high = jnp.where(plane == 0, left_three, high)
    far, *near_chips = after(jnp.stack([low, high]), *near_chips)
    far_chips = spread(far)
    own = with_partner(own_chips)
    near = with_partner(near_chips)
    vec_flat = vec_flat.reshape(-1).astype(F32)
    vec, taps = split_vectors(vec_flat, width)
    low_one, mixed, project, attended, lse = forward(place, tokens_in, meta, own, near, vec, taps)
    attended, *far_chips = after(attended, *far_chips)
    far = with_partner(far_chips)
    bufs = (*own, *near, *far)
    residual, low_two, cot, positive, mine, other, first = dense_up(
        place, tokens_in, grad_out, meta, attended, bufs, vec
    )

    def to_plane(parts, target):
        total = add_four(parts)
        return [total] + [
            swap(total, 8 * k, lambda i, k=k: plane_of(i) ^ k == target) for k in (1, 2, 3)
        ]

    def to_square(mine, other):
        return (mine.astype(F32) + other.astype(F32)).astype(BF)

    def exchange(blocks):
        return lax.all_to_all(blocks, SQUARE, 0, 0, tiled=True)

    def summed(blocks):
        return blocks.astype(F32).sum(axis=0).astype(BF)

    residual, highs = after(residual, to_square(mine, swap(other, 1)))
    highs = exchange(highs)
    block_out, grad_att, grad_res, dvec_two, mine, other = dense_down(
        place, attended, low_two, residual, cot, positive, vec, first, bufs
    )
    grad_att, highs = after(grad_att, summed(highs))
    high_sums = send_planes(highs, 3)
    received = swap(other, 1)
    mixed_one = attend_back(PIECES[0], mixed, grad_att, attended, lse, meta)
    mixed_one, received, grad_att = after(mixed_one, received, grad_att)
    grad_att, lows = after(grad_att, to_square(mine, received))
    lows = exchange(lows)
    mixed_two = attend_back(PIECES[1], mixed, grad_att, attended, lse, meta)
    half_a, half_b = HALVES
    size = shard.shape[0]
    mine, other, taps_a, grads_a = post(
        place, half_a, (mixed_one, mixed_two), project, taps, low_one, meta, size
    )
    grad_att, taps_a, *high_sums = after(grad_att, taps_a, *high_sums)
    received = swap(other, 1)
    mixed_b = attend_back(half_b, mixed, grad_att, attended, lse, meta)
    mixed_b, received, lows = after(mixed_b, received, lows)
    lifted = lift(place, lows)
    mixed_b, qkv_a, *lifted = after(mixed_b, to_square(mine, received), *lifted)
    qkv_a = exchange(qkv_a)
    low_sums = [lifted[0]] + [
        swap(lifted[k], 8 * k, lambda i, k=k: plane_of(i) ^ k in (1, 2)) for k in (1, 2, 3)
    ]
    mine, other, taps_b, grads_b = post(
        place, half_b, (mixed_b,), project, taps, low_one, meta, size
    )
    grads_b, qkv_a, *rest = after(
        grads_b, summed(qkv_a), *split_core(place, mine, swap(other, 1))
    )
    qkv_b = in_plane(rest)
    sums_a = send_planes(qkv_a, 0)
    tokens_grad, dvec_one = back(
        place, (grads_a, grads_b), tokens_in, grad_res, vec, own, near
    )
    dvec_one, *qkv_b = after(dvec_one, *qkv_b)
    sums_b = send_planes(add_four(qkv_b), 0)
    grad_vec = join_vectors(dvec_one, dvec_two, (taps_a, taps_b), vec_flat.size, roww)
    owned_vec = lax.all_to_all(grad_vec, FINE, 0, 0, tiled=True)
    owned_vec, *sums_b = after(owned_vec, *sums_b)
    owned = finish(place, (*sums_a, *sums_b, *low_sums, *high_sums), rows, roww)
    owned_vec = owned_vec.reshape(SHARDS, *vectors.shape).sum(axis=0)
    return block_out, tokens_grad, owned, owned_vec


def per_device_any(tokens_in, grad_out, seq_start, valid, matrices, vectors):
    width = tokens_in.shape[1]
    rows, roww = matrices.shape
    step = GROUP // FOLD
    place = jnp.array([0, 0, 0, 0, 0, 1, 2, 3], jnp.int32)
    meta = meta_rows(seq_start, valid)
    view = lax.all_gather(matrices, AXES, axis=0, tiled=True).reshape(-1, width)
    vec_flat = lax.all_gather(vectors, AXES, axis=0, tiled=True).reshape(-1).astype(F32)
    vec, taps = split_vectors(vec_flat, width)
    cut = (UP_FIRST * GROUP, UP_END * GROUP)
    up = view[cut[0] : cut[1]].reshape(UP_GROUPS, step, FOLD, width).swapaxes(1, 2)
    view = jnp.concatenate([view[: cut[0]], up.reshape(-1, width), view[cut[1] :]])
    shards = view.reshape(4, 8, -1, width)
    own = [shards[0, r] for r in range(8)]
    near = [shards[1, r] for r in range(8)]
    far = [shards[2:, r] for r in range(8)]
    low_one, mixed, project, attended, lse = forward(place, tokens_in, meta, own, near, vec, taps)
    bufs = (*own, *near, *far)
    residual, low_two, cot, positive, mine_three, other_three, first = dense_up(
        place, tokens_in, grad_out, meta, attended, bufs, vec
    )
    block_out, grad_att, grad_res, dvec_two, mine_low, other_low = dense_down(
        place, attended, low_two, residual, cot, positive, vec, first, bufs
    )
    qkv, grad_taps, grads = [], [], []
    for half in HALVES:
        grad_mixed = [attend_back(half, mixed, grad_att, attended, lse, meta)]
        result = post(place, half, grad_mixed, project, taps, low_one, meta, own[0].shape[0])
        qkv.append(jnp.stack(result[:2], axis=1))
        grad_taps.append(result[2])
        grads.append(result[3])
    tokens_grad, dvec_one = back(place, grads, tokens_in, grad_res, vec, own, near)
    planes = [
        jnp.concatenate(qkv, axis=-1)[:, :, None],
        jnp.stack([mine_low, other_low], axis=1),
        jnp.stack([mine_three, other_three], axis=1)[:, :, None],
    ]
    grad = jnp.concatenate(planes, axis=2)
    grad = grad.transpose(2, 0, 1, 3, 4).reshape(-1, width)
    up = grad[cut[0] : cut[1]].reshape(UP_GROUPS, FOLD, step, width).swapaxes(1, 2)
    grad = jnp.concatenate([grad[: cut[0]], up.reshape(-1, width), grad[cut[1] :]])
    owned = lax.psum_scatter(
        grad.reshape(-1, roww).astype(F32), AXES, scatter_dimension=0, tiled=True
    )
    grad_vec = join_vectors(dvec_one, dvec_two, grad_taps, vec_flat.size, roww)
    owned_vec = lax.psum_scatter(grad_vec, AXES, scatter_dimension=0, tiled=True)
    return block_out, tokens_grad, owned, owned_vec


def solution(mesh):
    body, axes = per_device_any, AXES
    if mesh.devices.size == SHARDS:
        mesh = Mesh(mesh.devices.reshape(4, 2, 2, 2), FINE)
        body, axes = per_device, FINE
    row = P(axes, None)
    flat = P(axes)
    return jax.shard_map(
        body,
        mesh=mesh,
        in_specs=(row, row, flat, flat, row, row),
        out_specs=(row, row, row, row),
        check_vma=False,
    )
```

```python
import functools

import jax
import jax.numpy as jnp
from jax import lax
from jax.experimental import pallas as pl
from jax.experimental.pallas import tpu as pltpu
from jax.sharding import Mesh
from jax.sharding import PartitionSpec as P

HEADS = 12
EPSILON = 1e-05
NEG_FILL = -1e30
BF = jnp.bfloat16
F32 = jnp.float32
AXES = ("dp", "sub")
FINE = ("z", "x", "y", "core")
SQUARE = ("x", "y")
VMEM_BYTES = 60 * 1024 * 1024
LANES = 128
BLOCK = 256
SPAN = 512
GROUP = 96
FOLD = 4
SHARDS = 32
WEIGHT = 100
REPEAT = 4
OUT_GROUPS = 8
UP_GROUPS = 32
UP_FIRST, UP_END = 32, 64
HALVES = ((0, 4), (4, 2))
PIECES = ((0, 2), (2, 2))
(
    PLACE_LINEAR, PLACE_Z, PLACE_IN_PLANE, PLACE_XY, PLACE_CORE,
    PLACE_NEAR, PLACE_LOW, PLACE_HIGH,
) = range(8)
HBM = pl.BlockSpec(memory_space=pl.ANY)


def dot(a, b):
    return jnp.dot(a, b, preferred_element_type=F32)


def dot_nt(a, b):
    return lax.dot_general(a, b, (((1,), (1,)), ((), ())), preferred_element_type=F32)


def dot_tn(a, b):
    return lax.dot_general(a, b, (((0,), (0,)), ((), ())), preferred_element_type=F32)


def whole(shape):
    return pl.BlockSpec(shape, lambda *_: (0,) * len(shape))


def fixed(shape):
    return pl.BlockSpec(shape, lambda *_: (0,) * len(shape), pipeline_mode=pl.Buffered(1))


def call(body, grid, ins, outs, out_shape, scratch, args, flops, moved, place=None, weight=WEIGHT):
    return pl.pallas_call(
        body,
        grid_spec=pltpu.PrefetchScalarGridSpec(
            num_scalar_prefetch=0 if place is None else 1,
            grid=grid,
            in_specs=ins,
            out_specs=outs,
            scratch_shapes=scratch,
        ),
        out_shape=out_shape,
        compiler_params=pltpu.CompilerParams(
            dimension_semantics=("arbitrary",) * len(grid), vmem_limit_bytes=VMEM_BYTES
        ),
        cost_estimate=pl.CostEstimate(
            flops=weight * flops, bytes_accessed=weight * moved, transcendentals=0
        ),
    )(*(() if place is None else (place,)), *args)


def like(shape, dtype):
    return jax.ShapeDtypeStruct(shape, dtype)


def normalize(v):
    centre = v - jnp.mean(v, axis=-1, keepdims=True)
    scaled = lax.rsqrt(jnp.mean(centre * centre, axis=-1, keepdims=True) + EPSILON)
    return centre * scaled, scaled


def norm_back(incoming, normed, scaled, gain):
    weighted = incoming * gain
    return scaled * (
        weighted
        - jnp.mean(weighted, axis=-1, keepdims=True)
        - normed * jnp.mean(weighted * normed, axis=-1, keepdims=True)
    )


def columns(meta):
    return jnp.transpose(meta, (1, 0))


def mix_masks(meta_ref, slots):
    cols = columns(meta_ref[...])
    position = lax.broadcasted_iota(jnp.int32, (slots, 1), 0).astype(F32) - cols[:, 0:1]
    return jnp.where(position >= 1.0, 1.0, 0.0), jnp.where(position >= 2.0, 1.0, 0.0)


def xor_pairs(mask, keep=None):
    return [(i, i ^ mask) for i in range(SHARDS) if keep is None or keep(i)]


def swap(value, mask, keep=None):
    return lax.ppermute(value, FINE, xor_pairs(mask, keep))


def plane_of(index):
    return index >> 3


def prep_body(place_ref, in_ref, out_ref, wide_ref):
    width = out_ref.shape[1]
    cols = width // LANES
    wide_ref[...] = in_ref[...].astype(F32)
    first = place_ref[PLACE_LINEAR] * (out_ref.shape[0] // GROUP)
    for n in range(out_ref.shape[0] // GROUP):
        base = n * GROUP * cols
        up = jnp.logical_and(first + n >= UP_FIRST, first + n < UP_END)

        @pl.when(up)
        def _():
            for j in range(cols):
                parts = [
                    wide_ref[pl.ds(base + q * cols + j, GROUP // FOLD, stride=cols * FOLD), :]
                    for q in range(FOLD)
                ]
                out_ref[n * GROUP : (n + 1) * GROUP, j * LANES : (j + 1) * LANES] = (
                    jnp.concatenate(parts, axis=0).astype(BF)
                )

        @pl.when(jnp.logical_not(up))
        def _():
            for j in range(cols):
                out_ref[n * GROUP : (n + 1) * GROUP, j * LANES : (j + 1) * LANES] = wide_ref[
                    pl.ds(base + j, GROUP, stride=cols), :
                ].astype(BF)


def finish_body(place_ref, *refs):
    halves = len(HALVES)
    zero = [refs[4 * h : 4 * h + 4] for h in range(halves)]
    middle, last = refs[4 * halves : 4 * halves + 4], refs[4 * halves + 4 : 4 * halves + 8]
    out_ref, total_ref = refs[-2:]
    width = total_ref.shape[1]
    cols = width // LANES
    plane = place_ref[PLACE_Z]

    def add(parts):
        total = parts[0][...].astype(F32)
        for part in parts[1:]:
            total = total + part[...].astype(F32)
        return total

    @pl.when(plane == 0)
    def _():
        for (at, count), parts in zip(HALVES, zero):
            total_ref[:, at * LANES : (at + count) * LANES] = add(parts)

    @pl.when(jnp.logical_or(plane == 1, plane == 2))
    def _():
        total_ref[...] = add(middle)

    @pl.when(plane == 3)
    def _():
        total_ref[...] = add(last)

    first = place_ref[PLACE_LINEAR] * (total_ref.shape[0] // GROUP)
    for n in range(total_ref.shape[0] // GROUP):
        base = n * GROUP * cols
        up = jnp.logical_and(first + n >= UP_FIRST, first + n < UP_END)

        @pl.when(up)
        def _():
            step = GROUP // FOLD
            for j in range(cols):
                for q in range(FOLD):
                    lo = n * GROUP + q * step
                    out_ref[pl.ds(base + q * cols + j, step, stride=cols * FOLD), :] = total_ref[
                        lo : lo + step, j * LANES : (j + 1) * LANES
                    ]

        @pl.when(jnp.logical_not(up))
        def _():
            for j in range(cols):
                out_ref[pl.ds(base + j, GROUP, stride=cols), :] = total_ref[
                    n * GROUP : (n + 1) * GROUP, j * LANES : (j + 1) * LANES
                ]


def route_body(place_ref, mine_ref, other_ref, *outs):
    for r, out in enumerate(outs):
        at = place_ref[PLACE_XY] ^ r
        out[...] = (mine_ref[at].astype(F32) + other_ref[at].astype(F32)).astype(BF)


def lift_body(place_ref, in_ref, *outs):
    plane = place_ref[PLACE_Z]
    for k, out in enumerate(outs):
        p = jnp.clip(plane ^ k, 1, 2) - 1
        total = in_ref[0, p].astype(F32)
        for r in range(1, 4):
            total = total + in_ref[r, p].astype(F32)
        out[...] = total.astype(BF)


def sum_body(a_ref, b_ref, c_ref, d_ref, out_ref):
    out_ref[...] = (
        a_ref[...].astype(F32) + b_ref[...].astype(F32) + c_ref[...].astype(F32) + d_ref[...].astype(F32)
    ).astype(BF)


def start_qkv(place_ref, own, near, w_ref, sem):
    size = own[0].shape[0]
    for r in range(8):
        at = pl.multiple_of((place_ref[PLACE_IN_PLANE] ^ r) * size, 32)

        @pl.when(place_ref[PLACE_Z] == 0)
        def _():
            pltpu.make_async_copy(own[r], w_ref.at[pl.ds(at, size)], sem).start()

        @pl.when(place_ref[PLACE_Z] != 0)
        def _():
            pltpu.make_async_copy(near[r], w_ref.at[pl.ds(at, size)], sem).start()


def wait_all(ref, sem):
    pltpu.make_async_copy(ref, ref, sem).wait()


def start_dense(place_ref, own, near, far, wo_ref, w1_ref, w2_ref, sems):
    step = GROUP // FOLD
    width = own[0].shape[1]
    slots = [(own, None, PLACE_Z, (1, 2, 3)), (near, None, PLACE_NEAR, (1,))]
    slots += [(far, 0, PLACE_LOW, (1, 2)), (far, 1, PLACE_HIGH, (2, 3))]
    for bufs, slot, plane_at, planes in slots:
        for p in planes:

            @pl.when(place_ref[plane_at] == p)
            def _():
                for r in range(8):
                    buf = bufs[r] if slot is None else bufs[r].at[slot]
                    place = place_ref[PLACE_IN_PLANE] ^ r
                    for n in range(3):
                        group = 24 * (p - 1) + 3 * place + n
                        rows = buf.at[pl.ds(n * GROUP, GROUP)]

                        def to_out():
                            at = pl.multiple_of(group * GROUP, 32)
                            pltpu.make_async_copy(
                                rows, wo_ref.at[pl.ds(at, GROUP)], sems.at[0]
                            ).start()

                        def to_up():
                            at = pl.multiple_of((group - OUT_GROUPS) * step, 8)
                            for q in range(FOLD):
                                pltpu.make_async_copy(
                                    rows.at[pl.ds(q * step, step)],
                                    w1_ref.at[pl.ds(at, step), pl.ds(q * width, width)],
                                    sems.at[1],
                                ).start()

                        def to_down():
                            at = pl.multiple_of((group - OUT_GROUPS - UP_GROUPS) * GROUP, 32)
                            pltpu.make_async_copy(
                                rows, w2_ref.at[pl.ds(at, GROUP)], sems.at[2]
                            ).start()

                        if p == 1:
                            pl.when(group < OUT_GROUPS)(to_out)
                            pl.when(group >= OUT_GROUPS)(to_up)
                        elif p == 2:
                            pl.when(group < OUT_GROUPS + UP_GROUPS)(to_up)
                            if w2_ref is not None:
                                pl.when(group >= OUT_GROUPS + UP_GROUPS)(to_down)
                        elif w2_ref is not None:
                            to_down()


def deal(place_ref, targets, sems, copy):
    core = place_ref[PLACE_CORE]
    for j in range(8):
        for which in range(2):

            @pl.when(core ^ (j % 2) == which)
            def _():
                copy(j, targets[which].at[j // 2], sems.at[which])


def pre_body(place_ref, x_ref, vec_ref, taps_ref, meta_ref, *refs):
    own, near = refs[:8], refs[8:16]
    low_ref, mixed_ref, proj_ref, w_ref, keep_ref, sem = refs[16:]
    slots, width = x_ref.shape
    here = pl.multiple_of(pl.program_id(0) * width, width)

    @pl.when(pl.program_id(0) == 0)
    def _():
        start_qkv(place_ref, own, near, w_ref, sem)
        for lo in range(0, slots, BLOCK):
            rows = slice(lo, lo + BLOCK)
            normed, _ = normalize(x_ref[rows, :].astype(F32))
            low_ref[rows, :] = (normed * vec_ref[0:1, :] + vec_ref[1:2, :]).astype(BF)
        wait_all(w_ref, sem)

    first, second = mix_masks(meta_ref, slots)
    weight = w_ref[pl.ds(here, width), :]
    ahead = dot(low_ref[0:BLOCK, :], weight)
    for lo in range(0, slots, BLOCK):
        end = lo + BLOCK
        value = ahead
        if end < slots:
            ahead = dot(low_ref[end : end + BLOCK, :], weight)
        proj_ref[lo:end, :] = value.astype(BF)
        keep_ref[lo:end, :] = value
        one_back = pltpu.roll(value, 1, 0) if lo == 0 else keep_ref[lo - 1 : end - 1, :]
        two_back = pltpu.roll(value, 2, 0) if lo == 0 else keep_ref[lo - 2 : end - 2, :]
        mixed_ref[lo:end, :] = (
            taps_ref[0:1, :] * value
            + taps_ref[1:2, :] * (one_back * first[lo:end])
            + taps_ref[2:3, :] * (two_back * second[lo:end])
        ).astype(BF)


def mask_columns(cols):
    lane = lax.broadcasted_iota(jnp.int32, (1, LANES), 1) % (LANES // 2)
    bucket = (lane >= 16) & (lane < 32)
    same = cols[:, 0:1] * (1.0 / 64.0) == (lane - 16).astype(F32)
    query = jnp.where(bucket & same, 0.0, jnp.where((lane >= 16) & (lane <= 32), NEG_FILL, 0.0))
    key = jnp.where(bucket & same, 1.0, jnp.where(lane == 32, 1.0 - cols[:, 1:2], 0.0))
    return query.astype(BF), key.astype(BF)


def triangle(lower):
    row = lax.broadcasted_iota(jnp.int32, (BLOCK, BLOCK), 0)
    col = lax.broadcasted_iota(jnp.int32, (BLOCK, BLOCK), 1)
    return jnp.where(col <= row if lower else row <= col, 0.0, NEG_FILL)


def attend_body(
    scale, q_ref, k_ref, v_ref, meta_ref, out_ref, lse_ref,
    tri_ref, qm_ref, km_ref, qa_ref, ka_ref, va_ref,
):
    slots = q_ref.shape[0]
    half = LANES // 2

    @pl.when(pl.program_id(0) == 0)
    def _():
        tri_ref[...] = triangle(True)
        qm_ref[...], km_ref[...] = mask_columns(columns(meta_ref[...]))

    left = lax.broadcasted_iota(jnp.int32, (1, LANES), 1) < half
    query = q_ref[...] * jnp.asarray(scale, BF)
    one = jnp.ones_like(query)
    for head in range(2):
        own = left if head == 0 else jnp.logical_not(left)
        qa_ref[head] = jnp.where(own, query, qm_ref[...])
        ka_ref[head] = jnp.where(own, k_ref[...], km_ref[...])
        va_ref[head] = jnp.where(own, v_ref[...], one)
    stages = [(lo, head) for lo in range(0, slots, BLOCK) for head in range(2)]
    outs, logs = [], []

    def score(lo, head):
        return dot_nt(qa_ref[head, lo : lo + BLOCK, :], ka_ref[head, : lo + BLOCK, :])

    def finish_stage(lo, head, terms, peak):
        end = lo + BLOCK
        both = dot(terms, va_ref[head, :end, :])
        outs.append(both / pltpu.roll(both, half, 1))
        logs.append(peak + jnp.log(both))
        if head == 1:
            out_ref[lo:end, :] = jnp.where(left, outs[-2], outs[-1]).astype(BF)
            lse_ref[lo:end, :] = jnp.where(left, logs[-1], logs[-2])

    ahead = score(*stages[0])
    behind = None
    for n, (lo, head) in enumerate(stages):
        scores = ahead
        if n + 1 < len(stages):
            ahead = score(*stages[n + 1])
        if behind is not None:
            finish_stage(*behind)
        near = scores[:, lo:] + tri_ref[...]
        scores = jnp.concatenate([scores[:, :lo], near], axis=1) if lo else near
        peak = jnp.max(scores, axis=-1, keepdims=True)
        behind = (lo, head, jnp.exp(scores - peak).astype(BF), peak)
    finish_stage(*behind)


def up_body(place_ref, att_ref, x_ref, go_ref, meta_ref, vec_ref, *refs):
    own, near, far = refs[:8], refs[8:16], refs[16:24]
    (
        res_ref, low_ref, cot_ref, out_ref, mine_ref, other_ref, first_ref,
        wo_ref, w1_ref, act_ref, cots_ref, g2_ref, sems,
    ) = refs[24:]
    width = x_ref.shape[1]
    step = pl.program_id(0)
    blocks = act_ref.shape[0] // SPAN
    here = pl.multiple_of(step * SPAN, SPAN)

    @pl.when(step == 0)
    def _():
        start_dense(place_ref, own, near, far, wo_ref, w1_ref, None, sems)
        wait_all(wo_ref, sems.at[0])
        wait_all(w1_ref, sems.at[1])

    @pl.when(step < blocks)
    def _():
        live = columns(meta_ref[...])[:, 1:2]
        cot = (go_ref[...].astype(F32) * live).astype(BF)
        cot_ref[...] = cot
        cots_ref[pl.ds(here, SPAN), :] = cot
        pieces = range(0, SPAN, BLOCK)
        residuals = [
            x_ref[lo : lo + BLOCK, :].astype(F32) + dot(att_ref[lo : lo + BLOCK, :], wo_ref[...])
            for lo in pieces
        ]
        lows = []

        def norm(lo, residual):
            res_ref[lo : lo + BLOCK, :] = residual
            normed, _ = normalize(residual)
            low = (normed * vec_ref[2:3, :] + vec_ref[3:4, :]).astype(BF)
            low_ref[lo : lo + BLOCK, :] = low
            lows.append(low)

        norm(0, residuals[0])
        stages = [(at, part) for at in range(len(pieces)) for part in range(FOLD)]

        def project(at, part):
            return dot(lows[at], w1_ref[:, part * width : (part + 1) * width])

        ahead = project(0, 0)
        for n, (at, part) in enumerate(stages):
            upward = jnp.maximum(ahead, 0.0)
            if part == 0 and at + 1 < len(pieces):
                norm(pieces[at + 1], residuals[at + 1])
            if n + 1 < len(stages):
                ahead = project(*stages[n + 1])
            cut = slice(part * width, (part + 1) * width)
            rows = pl.ds(pl.multiple_of(here + at * BLOCK, BLOCK), BLOCK)
            active = (upward * upward).astype(BF)
            act_ref[rows, cut] = active
            out_ref[at * BLOCK : (at + 1) * BLOCK, cut] = active

    for part in range(FOLD):

        @pl.when(step == blocks + part)
        def _():
            cut = slice(part * width, (part + 1) * width)
            g2_ref[cut, :] = dot_tn(act_ref[:, cut], cots_ref[...]).astype(BF)

    @pl.when(step == blocks + FOLD - 1)
    def _():
        size = mine_ref.shape[1]
        skip = g2_ref.shape[0] - 8 * size

        def copy(j, target, sem):
            pltpu.make_async_copy(g2_ref.at[pl.ds(skip + j * size, size)], target, sem).start()

        deal(place_ref, (mine_ref, other_ref), sems, copy)
        first_ref[...] = g2_ref[0:skip, :]
        wait_all(mine_ref, sems.at[0])
        wait_all(other_ref, sems.at[1])


def down_body(
    place_ref, att_ref, low_ref, res_ref, cot_ref, act_ref, vec_ref, first_ref, *refs
):
    own, near, far = refs[:8], refs[8:16], refs[16:24]
    (
        out_ref, gatt_ref, gres_ref, dvec_ref, mine_ref, other_ref,
        wo_ref, w1_ref, w2_ref, up_ref, reslow_ref, g1_ref, go_ref, sems,
    ) = refs[24:]
    width = res_ref.shape[1]
    step = pl.program_id(0)
    blocks = up_ref.shape[0] // SPAN
    here = pl.multiple_of(step * SPAN, SPAN)

    @pl.when(step == 0)
    def _():
        start_dense(place_ref, own, near, far, wo_ref, w1_ref, w2_ref, sems)
        dvec_ref[...] = jnp.zeros_like(dvec_ref)
        wait_all(w2_ref, sems.at[2])

    @pl.when(step < blocks)
    def _():
        pieces = range(0, SPAN, BLOCK)
        stages = [(lo, part) for lo in pieces for part in range(FOLD)]

        def incoming(lo, part):
            return dot_nt(cot_ref[lo : lo + BLOCK, :], w2_ref[part * width : (part + 1) * width, :])

        ahead = incoming(*stages[0])
        for n, (lo, part) in enumerate(stages):
            grad_active = ahead
            if n + 1 < len(stages):
                ahead = incoming(*stages[n + 1])
            cut = slice(part * width, (part + 1) * width)
            upward = jnp.sqrt(act_ref[lo : lo + BLOCK, cut].astype(F32))
            rows = pl.ds(pl.multiple_of(here + lo, BLOCK), BLOCK)
            up_ref[rows, cut] = (grad_active * (2.0 * upward)).astype(BF)
        for lo in pieces:
            out = res_ref[lo : lo + BLOCK, :] + dot(act_ref[lo : lo + BLOCK, :], w2_ref[...])
            out_ref[lo : lo + BLOCK, :] = out.astype(BF)

    @pl.when(step == 0)
    def _():
        wait_all(w1_ref, sems.at[1])
        wait_all(wo_ref, sems.at[0])

    @pl.when(step < blocks)
    def _():
        pieces = range(0, SPAN, BLOCK)

        def outgoing(lo):
            return dot_nt(up_ref[pl.ds(pl.multiple_of(here + lo, BLOCK), BLOCK), :], w1_ref[...])

        ahead = outgoing(0)
        for lo in pieces:
            grad = ahead
            if lo + BLOCK < SPAN:
                ahead = outgoing(lo + BLOCK)
            span = slice(lo, lo + BLOCK)
            normed, scaled = normalize(res_ref[span, :])
            back = norm_back(grad, normed, scaled, vec_ref[2:3, :])
            grad_residual = cot_ref[span, :].astype(F32) + back
            gres_ref[span, :] = grad_residual
            res_low = grad_residual.astype(BF)
            reslow_ref[pl.ds(pl.multiple_of(here + lo, BLOCK), BLOCK), :] = res_low
            gatt_ref[span, :] = dot_nt(res_low, wo_ref[...]).astype(BF)
            dvec_ref[0:1, :] += jnp.sum(grad * normed, axis=0, keepdims=True)
            dvec_ref[1:2, :] += jnp.sum(grad, axis=0, keepdims=True)

    for part in range(FOLD):

        @pl.when(step == blocks + part)
        def _():
            cut = slice(part * width, (part + 1) * width)
            g1_ref[part] = dot_tn(low_ref[...], up_ref[:, cut]).astype(BF)

    @pl.when(step == blocks + FOLD - 1)
    def _():
        go_ref[...] = dot_tn(att_ref[...], reslow_ref[...]).astype(BF)
        span = GROUP // FOLD

        def copy(j, target, sem):
            for p in range(2):
                for n in range(3):
                    group = 24 * p + 3 * j + n
                    rows = target.at[p, pl.ds(n * GROUP, GROUP)]
                    if group < OUT_GROUPS:
                        source = go_ref.at[pl.ds(group * GROUP, GROUP)]
                    elif group < OUT_GROUPS + UP_GROUPS:
                        source = g1_ref.at[:, pl.ds((group - OUT_GROUPS) * span, span)]
                        rows = rows.reshape(FOLD, span, width)
                    else:
                        at = (group - OUT_GROUPS - UP_GROUPS) * GROUP
                        source = first_ref.at[pl.ds(at, GROUP)]
                    pltpu.make_async_copy(source, rows, sem).start()

        deal(place_ref, (mine_ref, other_ref), sems, copy)
        wait_all(mine_ref, sems.at[0])
        wait_all(other_ref, sems.at[1])


def split_three(value):
    high = value.astype(BF)
    rest = value - high.astype(F32)
    middle = rest.astype(BF)
    return high, middle, (rest - middle.astype(F32)).astype(BF)


def attend_back_body(
    scale, q_ref, k_ref, v_ref, do_ref, o_ref, lse_ref, meta_ref, proj_ref, taps_ref,
    gproj_ref, gtaps_ref, grad_ref, mask_ref, bias_ref, qa_ref, ka_ref, va_ref, da_ref, kt_ref, dq_ref,
):
    slots = q_ref.shape[0]
    half = LANES // 2

    @pl.when(pl.program_id(0) == 0)
    def _():
        cols = columns(meta_ref[...])
        for lo in range(0, slots, BLOCK):
            end = lo + BLOCK
            size = slots - lo
            row = lax.broadcasted_iota(jnp.int32, (BLOCK, size), 0)
            col = lax.broadcasted_iota(jnp.int32, (BLOCK, size), 1)
            keep = (
                (cols[lo:end, 0:1] == meta_ref[0:1, lo:])
                & (cols[lo:end, 1:2] > 0.5)
                & (row <= col)
            )
            bias_ref[lo:end, lo:] = jnp.where(keep, 0.0, NEG_FILL)
        for n, mask in enumerate(mix_masks(meta_ref, slots)):
            mask_ref[n] = jnp.broadcast_to(mask, (slots, LANES))

    lane = lax.broadcasted_iota(jnp.int32, (1, LANES), 1)
    left = lane < half
    query = q_ref[...]
    key = k_ref[...]
    value = v_ref[...]
    grad_out = do_ref[...]
    product = grad_out.astype(F32) * o_ref[...].astype(F32)
    kt_ref[...] = jnp.transpose(key.astype(F32), (1, 0)).astype(BF)
    logs = split_three(-lse_ref[...])
    zero = jnp.zeros_like(query)
    one = jnp.ones_like(query)
    for head in range(2):
        own = left if head == 0 else jnp.logical_not(left)
        base = half if head == 0 else 0
        delta = jnp.sum(jnp.where(own, product, 0.0), axis=-1, keepdims=True)
        deltas = split_three(-delta)
        marks = [lane == base + n for n in range(3)]

        def spread(terms):
            result = zero
            for mark, term in zip(marks, terms):
                result = jnp.where(mark, term, result)
            return result

        ones = spread((one, one, one))
        qa_ref[head] = jnp.where(own, query * jnp.asarray(scale, BF), spread(logs))
        ka_ref[head] = jnp.where(own, key, ones)
        va_ref[head] = jnp.where(own, value, ones)
        da_ref[head] = jnp.where(own, grad_out, spread(deltas))
    dq_ref[...] = jnp.zeros_like(dq_ref)
    for lo in range(0, slots, BLOCK):
        end = lo + BLOCK
        grad_keys, grad_values = [], []
        for head in range(2):
            rows = slice(head * half, (head + 1) * half)
            scores = dot_nt(ka_ref[head, lo:end, :], qa_ref[head, lo:, :]) + bias_ref[lo:end, lo:]
            probs = jnp.exp(scores)
            inner = dot_nt(va_ref[head, lo:end, :], da_ref[head, lo:, :])
            grad_scores = (probs * inner).astype(BF)
            grad_values.append(dot(probs.astype(BF), do_ref[lo:, :]))
            grad_keys.append(dot(grad_scores, q_ref[lo:, :]))
            dq_ref[rows, lo:] += dot(kt_ref[rows, lo:end], grad_scores)
        grad_ref[1, lo:end, :] = jnp.where(left, grad_keys[0], grad_keys[1]) * scale
        grad_ref[2, lo:end, :] = jnp.where(left, grad_values[0], grad_values[1])
    grad_ref[0, :, :] = jnp.transpose(dq_ref[...], (1, 0)) * scale
    for c in range(3):
        mixed = grad_ref[c]
        proj = proj_ref[c].astype(F32)
        one_up = pltpu.roll(mixed * mask_ref[0], slots - 1, 0)
        two_up = pltpu.roll(mixed * mask_ref[1], slots - 2, 0)
        gtaps_ref[c, 0:1, :] = jnp.sum(mixed * proj, axis=0, keepdims=True)
        gtaps_ref[c, 1:2, :] = jnp.sum(one_up * proj, axis=0, keepdims=True)
        gtaps_ref[c, 2:3, :] = jnp.sum(two_up * proj, axis=0, keepdims=True)
        gproj_ref[c] = (
            taps_ref[c, 0:1, :] * mixed + taps_ref[c, 1:2, :] * one_up + taps_ref[c, 2:3, :] * two_up
        ).astype(BF)


def post_body(count, place_ref, *refs):
    pieces, low_ref = refs[:count], refs[count]
    mine_ref, lows_ref, highs_ref, gw_ref, lowt_ref, sems = refs[count + 1 :]
    width = low_ref.shape[1]
    step = pl.program_id(0)

    @pl.when(step == 0)
    def _():
        lowt_ref[...] = jnp.transpose(low_ref[...], (1, 0))

    here = pl.multiple_of(step * width, width)
    at = 0
    for ref in pieces:
        lanes = ref.shape[1]
        gw_ref[pl.ds(here, width), at : at + lanes] = dot(lowt_ref[...], ref[...]).astype(BF)
        at += lanes

    @pl.when(step == 2)
    def _():
        size = mine_ref.shape[1]

        core = place_ref[PLACE_CORE]
        for j in range(8):
            other = lows_ref.at[j // 2] if j < 4 else highs_ref.at[j // 2 - 2]
            rows = gw_ref.at[pl.ds(j * size, size)]

            @pl.when(core == j % 2)
            def _():
                pltpu.make_async_copy(rows, mine_ref.at[j // 2], sems.at[0]).start()

            @pl.when(core != j % 2)
            def _():
                pltpu.make_async_copy(rows, other, sems.at[1 + j // 4]).start()

        wait_all(mine_ref, sems.at[0])
        wait_all(lows_ref, sems.at[1])
        wait_all(highs_ref, sems.at[2])


def back_body(place_ref, *refs):
    grads, (x_ref, gres_ref, vec_ref) = refs[:-23], refs[-23:-20]
    own, near = refs[-20:-12], refs[-12:-4]
    out_ref, dvec_ref, w_ref, sem = refs[-4:]
    width = x_ref.shape[1]

    @pl.when(pl.program_id(0) == 0)
    def _():
        start_qkv(place_ref, own, near, w_ref, sem)
        dvec_ref[...] = jnp.zeros_like(dvec_ref)
        wait_all(w_ref, sem)

    incoming = None
    for c in range(3):
        rows = slice(c * width, (c + 1) * width)
        at = 0
        for grad in grads:
            lanes = grad.shape[2]
            term = dot_nt(grad[c], w_ref[rows, at : at + lanes])
            incoming = term if incoming is None else incoming + term
            at += lanes
    normed, scaled = normalize(x_ref[...].astype(F32))
    out_ref[...] = gres_ref[...] + norm_back(incoming, normed, scaled, vec_ref[0:1, :])
    dvec_ref[0:1, :] += jnp.sum(incoming * normed, axis=0, keepdims=True)
    dvec_ref[1:2, :] += jnp.sum(incoming, axis=0, keepdims=True)


def forward(place, tokens, meta, own, near, vec, taps):
    slots, width = tokens.shape
    pairs = width // LANES
    scale = (width // HEADS) ** (-0.5)
    three = pl.BlockSpec((None, slots, width), lambda c, *_: (c, 0, 0))
    tap = pl.BlockSpec((None, 3, width), lambda c, *_: (c, 0, 0))
    low_one, mixed, project = call(
        pre_body,
        (3,),
        [whole((slots, width)), whole(vec.shape), tap, whole(meta.shape)] + [HBM] * 16,
        [whole((slots, width)), three, three],
        [like((slots, width), BF), like((3, slots, width), BF), like((3, slots, width), BF)],
        [
            pltpu.VMEM((3 * width, width), BF),
            pltpu.VMEM((slots, width), F32),
            pltpu.SemaphoreType.DMA,
        ],
        (tokens, vec, taps, meta, *own, *near),
        6 * slots * width * width,
        24 << 20,
        place,
    )
    lane_block = pl.BlockSpec((slots, LANES), lambda p: (0, p))

    def part(c):
        return pl.BlockSpec((None, slots, LANES), lambda p: (c, 0, p))

    attended, lse = call(
        functools.partial(attend_body, scale),
        (pairs,),
        [part(0), part(1), part(2), whole(meta.shape)],
        [lane_block, lane_block],
        [like((slots, width), BF), like((slots, width), F32)],
        [pltpu.VMEM((BLOCK, BLOCK), F32)]
        + [pltpu.VMEM((slots, LANES), BF)] * 2
        + [pltpu.VMEM((2, slots, LANES), BF)] * 3,
        (mixed, mixed, mixed, meta),
        2 * slots * slots * width * 2,
        12 << 20,
    )
    return low_one, mixed, project, attended, lse


def dense_up(place, tokens, grad_out, meta, attended, bufs, vec):
    slots, width = tokens.shape
    hidden = FOLD * width
    size = bufs[0].shape[0]
    blocks = slots // SPAN
    row_block = pl.BlockSpec((SPAN, width), lambda i, *_: (jnp.minimum(i, blocks - 1), 0))
    wide_block = pl.BlockSpec((SPAN, hidden), lambda i, *_: (jnp.minimum(i, blocks - 1), 0))
    meta_block = pl.BlockSpec((8, SPAN), lambda i, *_: (0, jnp.minimum(i, blocks - 1)))
    skip = hidden - 8 * size
    return call(
        up_body,
        (blocks + FOLD,),
        [row_block] * 3 + [meta_block, whole(vec.shape)] + [HBM] * 24,
        [row_block, row_block, row_block, wide_block, HBM, HBM, whole((skip, width))],
        [
            like((slots, width), F32),
            like((slots, width), BF),
            like((slots, width), BF),
            like((slots, hidden), BF),
            like((4, size, width), BF),
            like((4, size, width), BF),
            like((skip, width), BF),
        ],
        [
            pltpu.VMEM((width, width), BF),
            pltpu.VMEM((width, hidden), BF),
            pltpu.VMEM((slots, hidden), BF),
            pltpu.VMEM((slots, width), BF),
            pltpu.VMEM((hidden, width), BF),
            pltpu.SemaphoreType.DMA((3,)),
        ],
        (attended, tokens, grad_out, meta, vec, *bufs),
        (4 * FOLD + 2) * slots * width * width,
        30 << 20,
        place,
    )


def dense_down(place, attended, low, residual, cot, active, vec, first, bufs):
    slots, width = residual.shape
    hidden = FOLD * width
    size = bufs[0].shape[0]
    blocks = slots // SPAN
    row_block = pl.BlockSpec((SPAN, width), lambda i, *_: (jnp.minimum(i, blocks - 1), 0))
    wide_block = pl.BlockSpec((SPAN, hidden), lambda i, *_: (jnp.minimum(i, blocks - 1), 0))
    full = fixed((slots, width))
    return call(
        down_body,
        (blocks + FOLD,),
        [full, full, row_block, row_block, wide_block, whole(vec.shape), whole(first.shape)]
        + [HBM] * 24,
        [row_block, row_block, row_block, whole((8, width)), HBM, HBM],
        [
            like((slots, width), BF),
            like((slots, width), BF),
            like((slots, width), F32),
            like((8, width), F32),
            like((4, 2, size, width), BF),
            like((4, 2, size, width), BF),
        ],
        [
            pltpu.VMEM((width, width), BF),
            pltpu.VMEM((width, hidden), BF),
            pltpu.VMEM((hidden, width), BF),
            pltpu.VMEM((slots, hidden), BF),
            pltpu.VMEM((slots, width), BF),
            pltpu.VMEM((FOLD, width, width), BF),
            pltpu.VMEM((width, width), BF),
            pltpu.SemaphoreType.DMA((3,)),
        ],
        (attended, low, residual, cot, active, vec, first, *bufs),
        (8 * FOLD + 4) * slots * width * width,
        36 << 20,
        place,
    )


def attend_back(half, mixed, grad_att, attended, lse, meta, project, taps):
    slots, width = grad_att.shape
    at, count = half
    lane_block = pl.BlockSpec((slots, LANES), lambda p: (0, p + at))

    def part(c):
        return pl.BlockSpec((None, slots, LANES), lambda p: (c, 0, p + at))

    return call(
        functools.partial(attend_back_body, (width // HEADS) ** (-0.5)),
        (count,),
        [part(0), part(1), part(2), lane_block, lane_block, lane_block, whole(meta.shape)]
        + [
            pl.BlockSpec((3, slots, LANES), lambda p: (0, 0, p + at)),
            pl.BlockSpec((3, 3, LANES), lambda p: (0, 0, p + at)),
        ],
        [
            pl.BlockSpec((3, slots, LANES), lambda p: (0, 0, p)),
            pl.BlockSpec((3, 3, LANES), lambda p: (0, 0, p)),
        ],
        [like((3, slots, count * LANES), BF), like((3, 3, count * LANES), F32)],
        [
            pltpu.VMEM((3, slots, LANES), F32),
            pltpu.VMEM((2, slots, LANES), F32),
            pltpu.VMEM((slots, slots), F32),
            pltpu.VMEM((2, slots, LANES), BF),
            pltpu.VMEM((2, slots, LANES), BF),
            pltpu.VMEM((2, slots, LANES), BF),
            pltpu.VMEM((2, slots, LANES), BF),
            pltpu.VMEM((LANES, slots), BF),
            pltpu.VMEM((LANES, slots), F32),
        ],
        (mixed, mixed, mixed, grad_att, attended, lse, meta, project, taps),
        10 * slots * slots * count * LANES,
        20 << 20,
    )


def post(place, grads, low, size):
    slots, width = low.shape
    lanes = sum(g.shape[2] for g in grads)
    return call(
        functools.partial(post_body, len(grads)),
        (3,),
        [pl.BlockSpec((None, *g.shape[1:]), lambda c, *_: (c, 0, 0)) for g in grads]
        + [whole((slots, width))],
        [HBM] * 3,
        [like((n, size, lanes), BF) for n in (4, 2, 2)],
        [
            pltpu.VMEM((3 * width, lanes), BF),
            pltpu.VMEM((width, slots), BF),
            pltpu.SemaphoreType.DMA((3,)),
        ],
        (*grads, low),
        6 * slots * width * lanes,
        24 << 20,
        place,
    )


def back(place, grads, tokens, grad_res, vec, own, near):
    slots, width = tokens.shape
    row_block = pl.BlockSpec((BLOCK, width), lambda i, *_: (i, 0))
    specs = [pl.BlockSpec((3, BLOCK, g.shape[2]), lambda i, *_: (0, i, 0)) for g in grads]
    return call(
        back_body,
        (slots // BLOCK,),
        specs + [row_block, row_block, whole(vec.shape)] + [HBM] * 16,
        [row_block, whole((8, width))],
        [like((slots, width), F32), like((8, width), F32)],
        [pltpu.VMEM((3 * width, width), BF), pltpu.SemaphoreType.DMA],
        (*grads, tokens, grad_res, vec, *own, *near),
        6 * slots * width * width,
        1,
        place,
        0,
    )


def split_core(place, mine, received):
    block = mine.shape[1:]
    return call(
        route_body,
        (1,),
        [whole(mine.shape)] * 2,
        [whole(block)] * 4,
        [like(block, BF)] * 4,
        [],
        (mine, received),
        0,
        3 * mine.size * 2,
        place,
    )


def in_plane(routed):
    return [routed[0]] + [swap(routed[r], 2 * r) for r in range(1, 4)]


def lift(place, blocks):
    shape = blocks.shape[2:]
    return call(
        lift_body,
        (1,),
        [whole(blocks.shape)],
        [whole(shape)] * 4,
        [like(shape, BF)] * 4,
        [],
        (blocks,),
        0,
        3 * blocks.size,
        place,
        0,
    )


def send_planes(total, target):
    return [total] + [
        swap(total, 8 * k, lambda i, k=k: plane_of(i) ^ k == target) for k in (1, 2, 3)
    ]


def add_four(parts):
    shape = parts[0].shape
    return call(
        sum_body,
        (1,),
        [whole(shape)] * 4,
        whole(shape),
        like(shape, BF),
        [],
        parts,
        0,
        10 * parts[0].size,
        weight=0,
    )


def prepare(place, matrices, width):
    rows, roww = matrices.shape
    size = rows * roww // width
    return call(
        prep_body,
        (1,),
        [whole((rows, roww))],
        whole((size, width)),
        like((size, width), BF),
        [pltpu.VMEM((rows, roww), F32)],
        (matrices,),
        0,
        4 * matrices.size,
        place,
    )


def finish(place, sums, rows, roww):
    size, width = sums[-1].shape
    return call(
        finish_body,
        (1,),
        [whole(part.shape) for part in sums],
        whole((rows, roww)),
        like((rows, roww), F32),
        [pltpu.VMEM((size, width), F32)],
        sums,
        0,
        28 * size * width,
        place,
    )


def after(value, *deps):
    return lax.optimization_barrier((value, *deps))


def meta_rows(seq_start, valid):
    zeros = jnp.zeros((6, seq_start.shape[0]), F32)
    return jnp.concatenate([seq_start.astype(F32)[None], valid.astype(F32)[None], zeros], axis=0)


def split_vectors(vec_flat, width):
    vec = vec_flat[: 13 * width].reshape(13, width)
    return vec[:8], vec[4:13].reshape(3, 3, width)


def join_vectors(dvec_one, dvec_two, grad_taps, total, roww):
    width = dvec_one.shape[1]
    taps = jnp.concatenate(grad_taps, axis=-1).reshape(9, width)
    rows = jnp.concatenate([dvec_one[:2], dvec_two[:2], taps], axis=0).reshape(-1)
    return jnp.pad(rows, (0, total - rows.size)).reshape(-1, roww)


def per_device(tokens_in, grad_out, seq_start, valid, matrices, vectors):
    width = tokens_in.shape[1]
    rows, roww = matrices.shape
    linear = lax.axis_index(FINE)
    plane = plane_of(linear)
    place = (linear >> jnp.array([0, 3, 0, 1, 0])) & jnp.array([31, 3, 7, 3, 1])
    near_planes = jnp.stack([1 - jnp.minimum(plane, 1), 2 - plane // 2, 3 - plane // 3])
    place = jnp.concatenate([place, near_planes])
    meta = meta_rows(seq_start, valid)
    shard = prepare(place, matrices, width)

    def up(value, steps, keep):
        pairs = [(i, i + 8 * steps) for i in range(SHARDS) if plane_of(i) in keep]
        return lax.ppermute(value, FINE, pairs)

    def with_partner(chips):
        bufs = []
        for chip in chips:
            bufs += [chip, swap(chip, 1)]
        return bufs

    def spread(held):
        by_y, by_x = swap(held, 2), swap(held, 4)
        return [held, by_y, by_x, swap(held, 6)]

    pairs = [(i, i + 16) for i in range(8)] + [(i, i + 8) for i in range(16, 24)]
    jump = lax.ppermute(shard, FINE, pairs)
    left_one = up(shard, -1, (1, 2, 3))
    own_y, own_x, own_both = spread(shard)[1:]
    jump, own_y, own_x = after(jump, own_y, own_x)
    hop = up(jnp.where(plane == 2, jump, shard), 1, (0, 1, 2))
    left_two = up(left_one, -1, (2, 1))
    near_one = jnp.where(plane == 0, left_one, jnp.where(plane == 2, jump, hop))
    near_one, hop, left_two, vectors_later, own_both = after(
        near_one, hop, left_two, vectors, own_both
    )
    own_chips = [shard, own_y, own_x, own_both]
    vec_flat = lax.all_to_all(jnp.tile(vectors_later, (SHARDS, 1)), FINE, 0, 0, tiled=True)
    near_chips = spread(near_one)
    left_three = up(left_two, -1, (1,))
    right_two = up(hop, 1, (2,))
    low = jnp.where(plane == 1, left_one, jnp.where(plane == 2, hop, right_two))
    low = jnp.where(plane == 0, left_two, low)
    high = jnp.where(plane == 1, left_two, jnp.where(plane == 2, left_one, jump))
    high = jnp.where(plane == 0, left_three, high)
    far, *near_chips = after(jnp.stack([low, high]), *near_chips)
    far_chips = spread(far)
    own = with_partner(own_chips)
    near = with_partner(near_chips)
    vec_flat = vec_flat.reshape(-1).astype(F32)
    vec, taps = split_vectors(vec_flat, width)
    low_one, mixed, project, attended, lse = forward(place, tokens_in, meta, own, near, vec, taps)
    attended, *far_chips = after(attended, *far_chips)
    far = with_partner(far_chips)
    bufs = (*own, *near, *far)
    residual, low_two, cot, active, mine, other, first = dense_up(
        place, tokens_in, grad_out, meta, attended, bufs, vec
    )

    def to_plane(parts, target):
        total = add_four(parts)
        return [total] + [
            swap(total, 8 * k, lambda i, k=k: plane_of(i) ^ k == target) for k in (1, 2, 3)
        ]

    def to_square(mine, other):
        return (mine.astype(F32) + other.astype(F32)).astype(BF)

    def exchange(blocks):
        return lax.all_to_all(blocks, SQUARE, 0, 0, tiled=True)

    def summed(blocks):
        return blocks.astype(F32).sum(axis=0).astype(BF)

    residual, highs = after(residual, to_square(mine, swap(other, 1)))
    highs = exchange(highs)
    block_out, grad_att, grad_res, dvec_two, mine, other = dense_down(
        place, attended, low_two, residual, cot, active, vec, first, bufs
    )
    grad_att, highs = after(grad_att, summed(highs))
    high_sums = send_planes(highs, 3)
    received = swap(other, 1)
    grads_one, taps_one = attend_back(
        PIECES[0], mixed, grad_att, attended, lse, meta, project, taps
    )
    grads_one, received, grad_att = after(grads_one, received, grad_att)
    grad_att, lows = after(grad_att, to_square(mine, received))
    lows = exchange(lows)
    grads_two, taps_two = attend_back(
        PIECES[1], mixed, grad_att, attended, lse, meta, project, taps
    )
    size = shard.shape[0]
    mine, *other = post(place, (grads_one, grads_two), low_one, size)
    grad_att, taps_two, *high_sums = after(grad_att, taps_two, *high_sums)
    received = [swap(part, 1) for part in other]
    grads_b, taps_b = attend_back(HALVES[1], mixed, grad_att, attended, lse, meta, project, taps)
    grads_b, lows, *received = after(grads_b, lows, *received)
    qkv_a = exchange(to_square(mine, jnp.concatenate(received)))
    lifted = lift(place, lows)
    grads_b, *lifted = after(grads_b, *lifted)
    low_sums = [lifted[0]] + [
        swap(lifted[k], 8 * k, lambda i, k=k: plane_of(i) ^ k in (1, 2)) for k in (1, 2, 3)
    ]
    mine, *other = post(place, (grads_b,), low_one, size)
    grads_b, qkv_a, *received = after(grads_b, qkv_a, *[swap(part, 1) for part in other])
    sums_a = send_planes(summed(qkv_a), 0)
    square_b = to_square(mine, jnp.concatenate(received))
    grads_b, square_b, sums_a[0] = after(grads_b, square_b, sums_a[0])
    qkv_b = exchange(square_b)
    tokens_grad, dvec_one = back(
        place, (grads_one, grads_two, grads_b), tokens_in, grad_res, vec, own, near
    )
    dvec_one, qkv_b, sums_a[1], sums_a[2], *low_sums = after(
        dvec_one, qkv_b, sums_a[1], sums_a[2], *low_sums
    )
    grad_vec = join_vectors(
        dvec_one, dvec_two, (taps_one, taps_two, taps_b), vec_flat.size, roww
    )
    grad_vec = jnp.tile(grad_vec.reshape(SHARDS, -1, roww), (1, REPEAT, 1)).reshape(-1, roww)
    owned_vec = lax.all_to_all(grad_vec, FINE, 0, 0, tiled=True)
    sums_b = send_planes(summed(qkv_b), 0)
    owned_vec, *sums_b = after(owned_vec, *sums_b)
    owned = finish(place, (*sums_a, *sums_b, *low_sums, *high_sums), rows, roww)
    owned_vec = owned_vec.reshape(SHARDS, REPEAT, *vectors.shape)[:, 0].sum(axis=0)
    return block_out, tokens_grad, owned, owned_vec


def per_device_any(tokens_in, grad_out, seq_start, valid, matrices, vectors):
    width = tokens_in.shape[1]
    rows, roww = matrices.shape
    step = GROUP // FOLD
    place = jnp.array([0, 0, 0, 0, 0, 1, 2, 3], jnp.int32)
    meta = meta_rows(seq_start, valid)
    view = lax.all_gather(matrices, AXES, axis=0, tiled=True).reshape(-1, width)
    vec_flat = lax.all_gather(vectors, AXES, axis=0, tiled=True).reshape(-1).astype(F32)
    vec, taps = split_vectors(vec_flat, width)
    cut = (UP_FIRST * GROUP, UP_END * GROUP)
    up = view[cut[0] : cut[1]].reshape(UP_GROUPS, step, FOLD, width).swapaxes(1, 2)
    view = jnp.concatenate([view[: cut[0]], up.reshape(-1, width), view[cut[1] :]])
    shards = view.reshape(4, 8, -1, width)
    own = [shards[0, r] for r in range(8)]
    near = [shards[1, r] for r in range(8)]
    far = [shards[2:, r] for r in range(8)]
    low_one, mixed, project, attended, lse = forward(place, tokens_in, meta, own, near, vec, taps)
    bufs = (*own, *near, *far)
    residual, low_two, cot, active, mine_three, other_three, first = dense_up(
        place, tokens_in, grad_out, meta, attended, bufs, vec
    )
    block_out, grad_att, grad_res, dvec_two, mine_low, other_low = dense_down(
        place, attended, low_two, residual, cot, active, vec, first, bufs
    )
    qkv, grad_taps, grads = [], [], []
    for half in HALVES:
        grad, grad_tap = attend_back(
            half, mixed, grad_att, attended, lse, meta, project, taps
        )
        mine, *other = post(place, (grad,), low_one, own[0].shape[0])
        qkv.append(jnp.stack([mine, jnp.concatenate(other)], axis=1))
        grad_taps.append(grad_tap)
        grads.append(grad)
    tokens_grad, dvec_one = back(place, grads, tokens_in, grad_res, vec, own, near)
    planes = [
        jnp.concatenate(qkv, axis=-1)[:, :, None],
        jnp.stack([mine_low, other_low], axis=1),
        jnp.stack([mine_three, other_three], axis=1)[:, :, None],
    ]
    grad = jnp.concatenate(planes, axis=2)
    grad = grad.transpose(2, 0, 1, 3, 4).reshape(-1, width)
    up = grad[cut[0] : cut[1]].reshape(UP_GROUPS, FOLD, step, width).swapaxes(1, 2)
    grad = jnp.concatenate([grad[: cut[0]], up.reshape(-1, width), grad[cut[1] :]])
    owned = lax.psum_scatter(
        grad.reshape(-1, roww).astype(F32), AXES, scatter_dimension=0, tiled=True
    )
    grad_vec = join_vectors(dvec_one, dvec_two, grad_taps, vec_flat.size, roww)
    owned_vec = lax.psum_scatter(grad_vec, AXES, scatter_dimension=0, tiled=True)
    return block_out, tokens_grad, owned, owned_vec


def solution(mesh):
    body, axes = per_device_any, AXES
    if mesh.devices.size == SHARDS:
        mesh = Mesh(mesh.devices.reshape(4, 2, 2, 2), FINE)
        body, axes = per_device, FINE
    row = P(axes, None)
    flat = P(axes)
    return jax.shard_map(
        body,
        mesh=mesh,
        in_specs=(row, row, flat, flat, row, row),
        out_specs=(row, row, row, row),
        check_vma=False,
    )
```

```python
import functools

import jax
import jax.numpy as jnp
from jax import lax
from jax.experimental import pallas as pl
from jax.experimental.pallas import tpu as pltpu
from jax.sharding import Mesh
from jax.sharding import PartitionSpec as P

HEADS = 12
EPSILON = 1e-05
NEG_FILL = -1e30
BF = jnp.bfloat16
F32 = jnp.float32
AXES = ("dp", "sub")
FINE = ("z", "x", "y", "core")
SQUARE = ("x", "y")
LANES = 128
BLOCK = 256
SPAN = 512
GROUP = 96
FOLD = 4
SHARDS = 32
WEIGHT = 100
DEEP = 16
OUT_GROUPS = 8
UP_GROUPS = 32
UP_FIRST, UP_END = 32, 64
HALVES = ((0, 4), (4, 2))
PIECES = ((0, 2), (2, 2))
(
    PLACE_LINEAR, PLACE_Z, PLACE_IN_PLANE, PLACE_XY, PLACE_CORE,
    PLACE_NEAR, PLACE_LOW, PLACE_HIGH,
) = range(8)
HBM = pl.BlockSpec(memory_space=pl.ANY)


def dot(a, b):
    return jnp.dot(a, b, preferred_element_type=F32)


def dot_nt(a, b):
    return lax.dot_general(a, b, (((1,), (1,)), ((), ())), preferred_element_type=F32)


def dot_tn(a, b):
    return lax.dot_general(a, b, (((0,), (0,)), ((), ())), preferred_element_type=F32)


def whole(shape):
    return pl.BlockSpec(shape, lambda *_: (0,) * len(shape))


def fixed(shape):
    return pl.BlockSpec(shape, lambda *_: (0,) * len(shape), pipeline_mode=pl.Buffered(1))


def call(body, grid, ins, outs, out_shape, scratch, args, flops, moved, place=None, weight=WEIGHT, room=16):
    return pl.pallas_call(
        body,
        grid_spec=pltpu.PrefetchScalarGridSpec(
            num_scalar_prefetch=0 if place is None else 1,
            grid=grid,
            in_specs=ins,
            out_specs=outs,
            scratch_shapes=scratch,
        ),
        out_shape=out_shape,
        compiler_params=pltpu.CompilerParams(
            dimension_semantics=("arbitrary",) * len(grid), vmem_limit_bytes=room << 20
        ),
        cost_estimate=pl.CostEstimate(
            flops=weight * flops, bytes_accessed=weight * moved, transcendentals=0
        ),
    )(*(() if place is None else (place,)), *args)


def like(shape, dtype):
    return jax.ShapeDtypeStruct(shape, dtype)


def normalize(v):
    centre = v - jnp.mean(v, axis=-1, keepdims=True)
    scaled = lax.rsqrt(jnp.mean(centre * centre, axis=-1, keepdims=True) + EPSILON)
    return centre * scaled, scaled


def norm_back(incoming, normed, scaled, gain):
    weighted = incoming * gain
    return scaled * (
        weighted
        - jnp.mean(weighted, axis=-1, keepdims=True)
        - normed * jnp.mean(weighted * normed, axis=-1, keepdims=True)
    )


def columns(meta):
    return jnp.transpose(meta, (1, 0))


def mix_masks(meta_ref, slots):
    cols = columns(meta_ref[...])
    position = lax.broadcasted_iota(jnp.int32, (slots, 1), 0).astype(F32) - cols[:, 0:1]
    return jnp.where(position >= 1.0, 1.0, 0.0), jnp.where(position >= 2.0, 1.0, 0.0)


def xor_pairs(mask, keep=None):
    return [(i, i ^ mask) for i in range(SHARDS) if keep is None or keep(i)]


def swap(value, mask, keep=None):
    return lax.ppermute(value, FINE, xor_pairs(mask, keep))


def plane_of(index):
    return index >> 3


def prep_body(place_ref, in_ref, out_ref, wide_ref):
    width = out_ref.shape[1]
    cols = width // LANES
    wide_ref[...] = in_ref[...].astype(F32)
    first = place_ref[PLACE_LINEAR] * (out_ref.shape[0] // GROUP)
    for n in range(out_ref.shape[0] // GROUP):
        base = n * GROUP * cols
        up = jnp.logical_and(first + n >= UP_FIRST, first + n < UP_END)

        @pl.when(up)
        def _():
            for j in range(cols):
                parts = [
                    wide_ref[pl.ds(base + q * cols + j, GROUP // FOLD, stride=cols * FOLD), :]
                    for q in range(FOLD)
                ]
                out_ref[n * GROUP : (n + 1) * GROUP, j * LANES : (j + 1) * LANES] = (
                    jnp.concatenate(parts, axis=0).astype(BF)
                )

        @pl.when(jnp.logical_not(up))
        def _():
            for j in range(cols):
                out_ref[n * GROUP : (n + 1) * GROUP, j * LANES : (j + 1) * LANES] = wide_ref[
                    pl.ds(base + j, GROUP, stride=cols), :
                ].astype(BF)


def finish_body(place_ref, *refs):
    zero, middle, last = refs[:4], refs[4:8], refs[8:12]
    out_ref, total_ref = refs[-2:]
    width = total_ref.shape[1]
    cols = width // LANES
    plane = place_ref[PLACE_Z]

    def add(parts):
        total = parts[0][...].astype(F32)
        for part in parts[1:]:
            total = total + part[...].astype(F32)
        return total

    @pl.when(plane == 0)
    def _():
        total_ref[...] = add(zero)

    @pl.when(jnp.logical_or(plane == 1, plane == 2))
    def _():
        total_ref[...] = add(middle)

    @pl.when(plane == 3)
    def _():
        total_ref[...] = add(last)

    first = place_ref[PLACE_LINEAR] * (total_ref.shape[0] // GROUP)
    for n in range(total_ref.shape[0] // GROUP):
        base = n * GROUP * cols
        up = jnp.logical_and(first + n >= UP_FIRST, first + n < UP_END)

        @pl.when(up)
        def _():
            step = GROUP // FOLD
            for j in range(cols):
                for q in range(FOLD):
                    lo = n * GROUP + q * step
                    out_ref[pl.ds(base + q * cols + j, step, stride=cols * FOLD), :] = total_ref[
                        lo : lo + step, j * LANES : (j + 1) * LANES
                    ]

        @pl.when(jnp.logical_not(up))
        def _():
            for j in range(cols):
                out_ref[pl.ds(base + j, GROUP, stride=cols), :] = total_ref[
                    n * GROUP : (n + 1) * GROUP, j * LANES : (j + 1) * LANES
                ]


def route_body(place_ref, mine_ref, other_ref, *outs):
    for r, out in enumerate(outs):
        at = place_ref[PLACE_XY] ^ r
        out[...] = (mine_ref[at].astype(F32) + other_ref[at].astype(F32)).astype(BF)


def lift_body(place_ref, in_ref, *outs):
    plane = place_ref[PLACE_Z]
    for k, out in enumerate(outs):
        p = jnp.clip(plane ^ k, 1, 2) - 1
        total = in_ref[0, p].astype(F32)
        for r in range(1, 4):
            total = total + in_ref[r, p].astype(F32)
        out[...] = total.astype(BF)


def sum_body(a_ref, b_ref, c_ref, d_ref, out_ref):
    out_ref[...] = (
        a_ref[...].astype(F32) + b_ref[...].astype(F32) + c_ref[...].astype(F32) + d_ref[...].astype(F32)
    ).astype(BF)


def start_qkv(place_ref, own, near, w_ref, sem):
    size = own[0].shape[0]
    for r in range(8):
        at = pl.multiple_of((place_ref[PLACE_IN_PLANE] ^ r) * size, 32)

        @pl.when(place_ref[PLACE_Z] == 0)
        def _():
            pltpu.make_async_copy(own[r], w_ref.at[pl.ds(at, size)], sem).start()

        @pl.when(place_ref[PLACE_Z] != 0)
        def _():
            pltpu.make_async_copy(near[r], w_ref.at[pl.ds(at, size)], sem).start()


def wait_all(ref, sem):
    pltpu.make_async_copy(ref, ref, sem).wait()


def start_dense(place_ref, own, near, far, wo_ref, w1_ref, w2_ref, sems):
    step = GROUP // FOLD
    width = own[0].shape[1]
    slots = [(own, None, PLACE_Z, (1, 2, 3)), (near, None, PLACE_NEAR, (1,))]
    slots += [(far, 0, PLACE_LOW, (1, 2)), (far, 1, PLACE_HIGH, (2, 3))]
    for bufs, slot, plane_at, planes in slots:
        for p in planes:

            @pl.when(place_ref[plane_at] == p)
            def _():
                for r in range(8):
                    buf = bufs[r] if slot is None else bufs[r].at[slot]
                    place = place_ref[PLACE_IN_PLANE] ^ r
                    for n in range(3):
                        group = 24 * (p - 1) + 3 * place + n
                        rows = buf.at[pl.ds(n * GROUP, GROUP)]

                        def to_out():
                            at = pl.multiple_of(group * GROUP, 32)
                            pltpu.make_async_copy(
                                rows, wo_ref.at[pl.ds(at, GROUP)], sems.at[0]
                            ).start()

                        def to_up():
                            at = pl.multiple_of((group - OUT_GROUPS) * step, 8)
                            for q in range(FOLD):
                                pltpu.make_async_copy(
                                    rows.at[pl.ds(q * step, step)],
                                    w1_ref.at[pl.ds(at, step), pl.ds(q * width, width)],
                                    sems.at[1],
                                ).start()

                        def to_down():
                            at = pl.multiple_of((group - OUT_GROUPS - UP_GROUPS) * GROUP, 32)
                            pltpu.make_async_copy(
                                rows, w2_ref.at[pl.ds(at, GROUP)], sems.at[2]
                            ).start()

                        if p == 1:
                            pl.when(group < OUT_GROUPS)(to_out)
                            pl.when(group >= OUT_GROUPS)(to_up)
                        elif p == 2:
                            pl.when(group < OUT_GROUPS + UP_GROUPS)(to_up)
                            if w2_ref is not None:
                                pl.when(group >= OUT_GROUPS + UP_GROUPS)(to_down)
                        elif w2_ref is not None:
                            to_down()


def deal(place_ref, targets, sems, copy):
    core = place_ref[PLACE_CORE]
    for j in range(8):
        for which in range(2):

            @pl.when(core ^ (j % 2) == which)
            def _():
                copy(j, targets[which].at[j // 2], sems.at[which])


def pre_body(place_ref, x_ref, vec_ref, taps_ref, meta_ref, *refs):
    own, near = refs[:8], refs[8:16]
    low_ref, mixed_ref, proj_ref, w_ref, keep_ref, sem = refs[16:]
    slots, width = x_ref.shape
    here = pl.multiple_of(pl.program_id(0) * width, width)

    @pl.when(pl.program_id(0) == 0)
    def _():
        start_qkv(place_ref, own, near, w_ref, sem)
        for lo in range(0, slots, BLOCK):
            rows = slice(lo, lo + BLOCK)
            normed, _ = normalize(x_ref[rows, :].astype(F32))
            low_ref[rows, :] = (normed * vec_ref[0:1, :] + vec_ref[1:2, :]).astype(BF)
        wait_all(w_ref, sem)

    first, second = mix_masks(meta_ref, slots)
    weight = w_ref[pl.ds(here, width), :]
    ahead = dot(low_ref[0:BLOCK, :], weight)
    for lo in range(0, slots, BLOCK):
        end = lo + BLOCK
        value = ahead
        if end < slots:
            ahead = dot(low_ref[end : end + BLOCK, :], weight)
        proj_ref[lo:end, :] = value.astype(BF)
        keep_ref[lo:end, :] = value
        one_back = pltpu.roll(value, 1, 0) if lo == 0 else keep_ref[lo - 1 : end - 1, :]
        two_back = pltpu.roll(value, 2, 0) if lo == 0 else keep_ref[lo - 2 : end - 2, :]
        mixed_ref[lo:end, :] = (
            taps_ref[0:1, :] * value
            + taps_ref[1:2, :] * (one_back * first[lo:end])
            + taps_ref[2:3, :] * (two_back * second[lo:end])
        ).astype(BF)


def mask_columns(cols):
    lane = lax.broadcasted_iota(jnp.int32, (1, LANES), 1) % (LANES // 2)
    bucket = (lane >= 16) & (lane < 32)
    same = cols[:, 0:1] * (1.0 / 64.0) == (lane - 16).astype(F32)
    query = jnp.where(bucket & same, 0.0, jnp.where((lane >= 16) & (lane <= 32), NEG_FILL, 0.0))
    key = jnp.where(bucket & same, 1.0, jnp.where(lane == 32, 1.0 - cols[:, 1:2], 0.0))
    return query.astype(BF), key.astype(BF)


def triangle(lower):
    row = lax.broadcasted_iota(jnp.int32, (BLOCK, BLOCK), 0)
    col = lax.broadcasted_iota(jnp.int32, (BLOCK, BLOCK), 1)
    return jnp.where(col <= row if lower else row <= col, 0.0, NEG_FILL)


def attend_body(
    scale, q_ref, k_ref, v_ref, meta_ref, out_ref, lse_ref,
    tri_ref, qm_ref, km_ref, qa_ref, ka_ref, va_ref,
):
    slots = q_ref.shape[0]
    half = LANES // 2

    @pl.when(pl.program_id(0) == 0)
    def _():
        tri_ref[...] = triangle(True)
        qm_ref[...], km_ref[...] = mask_columns(columns(meta_ref[...]))

    left = lax.broadcasted_iota(jnp.int32, (1, LANES), 1) < half
    query = q_ref[...] * jnp.asarray(scale, BF)
    one = jnp.ones_like(query)
    for head in range(2):
        own = left if head == 0 else jnp.logical_not(left)
        qa_ref[head] = jnp.where(own, query, qm_ref[...])
        ka_ref[head] = jnp.where(own, k_ref[...], km_ref[...])
        va_ref[head] = jnp.where(own, v_ref[...], one)
    stages = [(lo, head) for lo in range(0, slots, BLOCK) for head in range(2)]
    outs, logs = [], []

    def score(lo, head):
        return dot_nt(qa_ref[head, lo : lo + BLOCK, :], ka_ref[head, : lo + BLOCK, :])

    def finish_stage(lo, head, terms, peak):
        end = lo + BLOCK
        both = dot(terms, va_ref[head, :end, :])
        outs.append(both / pltpu.roll(both, half, 1))
        logs.append(peak + jnp.log(both))
        if head == 1:
            out_ref[lo:end, :] = jnp.where(left, outs[-2], outs[-1]).astype(BF)
            lse_ref[lo:end, :] = jnp.where(left, logs[-1], logs[-2])

    ahead = score(*stages[0])
    behind = None
    for n, (lo, head) in enumerate(stages):
        scores = ahead
        if n + 1 < len(stages):
            ahead = score(*stages[n + 1])
        if behind is not None:
            finish_stage(*behind)
        near = scores[:, lo:] + tri_ref[...]
        scores = jnp.concatenate([scores[:, :lo], near], axis=1) if lo else near
        peak = jnp.max(scores, axis=-1, keepdims=True)
        behind = (lo, head, jnp.exp(scores - peak).astype(BF), peak)
    finish_stage(*behind)


def up_body(place_ref, att_ref, x_ref, go_ref, meta_ref, vec_ref, *refs):
    own, near, far = refs[:8], refs[8:16], refs[16:24]
    (
        res_ref, low_ref, cot_ref, out_ref, mine_ref, other_ref, first_ref,
        wo_ref, w1_ref, act_ref, cots_ref, g2_ref, sems,
    ) = refs[24:]
    width = x_ref.shape[1]
    step = pl.program_id(0)
    blocks = act_ref.shape[0] // SPAN
    here = pl.multiple_of(step * SPAN, SPAN)

    @pl.when(step == 0)
    def _():
        start_dense(place_ref, own, near, far, wo_ref, w1_ref, None, sems)
        wait_all(wo_ref, sems.at[0])
        wait_all(w1_ref, sems.at[1])

    @pl.when(step < blocks)
    def _():
        live = columns(meta_ref[...])[:, 1:2]
        cot = (go_ref[...].astype(F32) * live).astype(BF)
        cot_ref[...] = cot
        cots_ref[pl.ds(here, SPAN), :] = cot
        pieces = range(0, SPAN, BLOCK)
        residuals = [
            x_ref[lo : lo + BLOCK, :].astype(F32) + dot(att_ref[lo : lo + BLOCK, :], wo_ref[...])
            for lo in pieces
        ]
        lows = []

        def norm(lo, residual):
            res_ref[lo : lo + BLOCK, :] = residual
            normed, _ = normalize(residual)
            low = (normed * vec_ref[2:3, :] + vec_ref[3:4, :]).astype(BF)
            low_ref[lo : lo + BLOCK, :] = low
            lows.append(low)

        norm(0, residuals[0])
        stages = [(at, part) for at in range(len(pieces)) for part in range(FOLD)]

        def project(at, part):
            return dot(lows[at], w1_ref[:, part * width : (part + 1) * width])

        ahead = project(0, 0)
        for n, (at, part) in enumerate(stages):
            upward = jnp.maximum(ahead, 0.0)
            if part == 0 and at + 1 < len(pieces):
                norm(pieces[at + 1], residuals[at + 1])
            if n + 1 < len(stages):
                ahead = project(*stages[n + 1])
            cut = slice(part * width, (part + 1) * width)
            rows = pl.ds(pl.multiple_of(here + at * BLOCK, BLOCK), BLOCK)
            active = (upward * upward).astype(BF)
            act_ref[rows, cut] = active
            out_ref[at * BLOCK : (at + 1) * BLOCK, cut] = active

    for part in range(FOLD):

        @pl.when(step == blocks + part)
        def _():
            cut = slice(part * width, (part + 1) * width)
            g2_ref[cut, :] = dot_tn(act_ref[:, cut], cots_ref[...]).astype(BF)

    @pl.when(step == blocks + FOLD - 1)
    def _():
        size = mine_ref.shape[1]
        skip = g2_ref.shape[0] - 8 * size

        def copy(j, target, sem):
            pltpu.make_async_copy(g2_ref.at[pl.ds(skip + j * size, size)], target, sem).start()

        deal(place_ref, (mine_ref, other_ref), sems, copy)
        first_ref[...] = g2_ref[0:skip, :]
        wait_all(mine_ref, sems.at[0])
        wait_all(other_ref, sems.at[1])


def down_body(
    place_ref, att_ref, low_ref, res_ref, cot_ref, act_ref, vec_ref, first_ref, *refs
):
    own, near, far = refs[:8], refs[8:16], refs[16:24]
    (
        out_ref, gatt_ref, gres_ref, dvec_ref, mine_ref, other_ref,
        wo_ref, w1_ref, w2_ref, up_ref, reslow_ref, g1_ref, go_ref, sems,
    ) = refs[24:]
    width = res_ref.shape[1]
    step = pl.program_id(0)
    blocks = up_ref.shape[0] // SPAN
    here = pl.multiple_of(step * SPAN, SPAN)

    @pl.when(step == 0)
    def _():
        start_dense(place_ref, own, near, far, wo_ref, w1_ref, w2_ref, sems)
        dvec_ref[...] = jnp.zeros_like(dvec_ref)
        wait_all(w2_ref, sems.at[2])

    @pl.when(step < blocks)
    def _():
        pieces = range(0, SPAN, BLOCK)
        stages = [(lo, part) for lo in pieces for part in range(FOLD)]

        def incoming(lo, part):
            return dot_nt(cot_ref[lo : lo + BLOCK, :], w2_ref[part * width : (part + 1) * width, :])

        ahead = incoming(*stages[0])
        for n, (lo, part) in enumerate(stages):
            grad_active = ahead
            if n + 1 < len(stages):
                ahead = incoming(*stages[n + 1])
            cut = slice(part * width, (part + 1) * width)
            upward = jnp.sqrt(act_ref[lo : lo + BLOCK, cut].astype(F32))
            rows = pl.ds(pl.multiple_of(here + lo, BLOCK), BLOCK)
            up_ref[rows, cut] = (grad_active * (2.0 * upward)).astype(BF)
        for lo in pieces:
            out = res_ref[lo : lo + BLOCK, :] + dot(act_ref[lo : lo + BLOCK, :], w2_ref[...])
            out_ref[lo : lo + BLOCK, :] = out.astype(BF)

    @pl.when(step == 0)
    def _():
        wait_all(w1_ref, sems.at[1])
        wait_all(wo_ref, sems.at[0])

    @pl.when(step < blocks)
    def _():
        pieces = range(0, SPAN, BLOCK)

        def outgoing(lo):
            return dot_nt(up_ref[pl.ds(pl.multiple_of(here + lo, BLOCK), BLOCK), :], w1_ref[...])

        ahead = outgoing(0)
        for lo in pieces:
            grad = ahead
            if lo + BLOCK < SPAN:
                ahead = outgoing(lo + BLOCK)
            span = slice(lo, lo + BLOCK)
            normed, scaled = normalize(res_ref[span, :])
            back = norm_back(grad, normed, scaled, vec_ref[2:3, :])
            grad_residual = cot_ref[span, :].astype(F32) + back
            gres_ref[span, :] = grad_residual
            res_low = grad_residual.astype(BF)
            reslow_ref[pl.ds(pl.multiple_of(here + lo, BLOCK), BLOCK), :] = res_low
            gatt_ref[span, :] = dot_nt(res_low, wo_ref[...]).astype(BF)
            dvec_ref[0:1, :] += jnp.sum(grad * normed, axis=0, keepdims=True)
            dvec_ref[1:2, :] += jnp.sum(grad, axis=0, keepdims=True)

    for part in range(FOLD):

        @pl.when(step == blocks + part)
        def _():
            cut = slice(part * width, (part + 1) * width)
            g1_ref[part] = dot_tn(low_ref[...], up_ref[:, cut]).astype(BF)

    @pl.when(step == blocks + FOLD - 1)
    def _():
        go_ref[...] = dot_tn(att_ref[...], reslow_ref[...]).astype(BF)
        span = GROUP // FOLD

        def copy(j, target, sem):
            for p in range(2):
                for n in range(3):
                    group = 24 * p + 3 * j + n
                    rows = target.at[p, pl.ds(n * GROUP, GROUP)]
                    if group < OUT_GROUPS:
                        source = go_ref.at[pl.ds(group * GROUP, GROUP)]
                    elif group < OUT_GROUPS + UP_GROUPS:
                        source = g1_ref.at[:, pl.ds((group - OUT_GROUPS) * span, span)]
                        rows = rows.reshape(FOLD, span, width)
                    else:
                        at = (group - OUT_GROUPS - UP_GROUPS) * GROUP
                        source = first_ref.at[pl.ds(at, GROUP)]
                    pltpu.make_async_copy(source, rows, sem).start()

        deal(place_ref, (mine_ref, other_ref), sems, copy)
        wait_all(mine_ref, sems.at[0])
        wait_all(other_ref, sems.at[1])


def split_three(value):
    high = value.astype(BF)
    rest = value - high.astype(F32)
    middle = rest.astype(BF)
    return high, middle, (rest - middle.astype(F32)).astype(BF)


def attend_back_body(
    scale, q_ref, k_ref, v_ref, do_ref, o_ref, lse_ref, meta_ref, proj_ref, taps_ref,
    gproj_ref, gtaps_ref, grad_ref, mask_ref, bias_ref, qa_ref, ka_ref, va_ref, da_ref, kt_ref, dq_ref,
):
    slots = q_ref.shape[0]
    half = LANES // 2

    @pl.when(pl.program_id(0) == 0)
    def _():
        cols = columns(meta_ref[...])
        for lo in range(0, slots, BLOCK):
            end = lo + BLOCK
            size = slots - lo
            row = lax.broadcasted_iota(jnp.int32, (BLOCK, size), 0)
            col = lax.broadcasted_iota(jnp.int32, (BLOCK, size), 1)
            keep = (
                (cols[lo:end, 0:1] == meta_ref[0:1, lo:])
                & (cols[lo:end, 1:2] > 0.5)
                & (row <= col)
            )
            bias_ref[lo:end, lo:] = jnp.where(keep, 0.0, NEG_FILL)
        for n, mask in enumerate(mix_masks(meta_ref, slots)):
            mask_ref[n] = jnp.broadcast_to(mask, (slots, LANES))

    lane = lax.broadcasted_iota(jnp.int32, (1, LANES), 1)
    left = lane < half
    query = q_ref[...]
    key = k_ref[...]
    value = v_ref[...]
    grad_out = do_ref[...]
    product = grad_out.astype(F32) * o_ref[...].astype(F32)
    kt_ref[...] = jnp.transpose(key.astype(F32), (1, 0)).astype(BF)
    logs = split_three(-lse_ref[...])
    zero = jnp.zeros_like(query)
    one = jnp.ones_like(query)
    for head in range(2):
        own = left if head == 0 else jnp.logical_not(left)
        base = half if head == 0 else 0
        delta = jnp.sum(jnp.where(own, product, 0.0), axis=-1, keepdims=True)
        deltas = split_three(-delta)
        marks = [lane == base + n for n in range(3)]

        def spread(terms):
            result = zero
            for mark, term in zip(marks, terms):
                result = jnp.where(mark, term, result)
            return result

        ones = spread((one, one, one))
        qa_ref[head] = jnp.where(own, query * jnp.asarray(scale, BF), spread(logs))
        ka_ref[head] = jnp.where(own, key, ones)
        va_ref[head] = jnp.where(own, value, ones)
        da_ref[head] = jnp.where(own, grad_out, spread(deltas))
    dq_ref[...] = jnp.zeros_like(dq_ref)
    for lo in range(0, slots, BLOCK):
        end = lo + BLOCK
        grad_keys, grad_values = [], []
        for head in range(2):
            rows = slice(head * half, (head + 1) * half)
            scores = dot_nt(ka_ref[head, lo:end, :], qa_ref[head, lo:, :]) + bias_ref[lo:end, lo:]
            probs = jnp.exp(scores)
            inner = dot_nt(va_ref[head, lo:end, :], da_ref[head, lo:, :])
            grad_scores = (probs * inner).astype(BF)
            grad_values.append(dot(probs.astype(BF), do_ref[lo:, :]))
            grad_keys.append(dot(grad_scores, q_ref[lo:, :]))
            dq_ref[rows, lo:] += dot(kt_ref[rows, lo:end], grad_scores)
        grad_ref[1, lo:end, :] = jnp.where(left, grad_keys[0], grad_keys[1]) * scale
        grad_ref[2, lo:end, :] = jnp.where(left, grad_values[0], grad_values[1])
    grad_ref[0, :, :] = jnp.transpose(dq_ref[...], (1, 0)) * scale
    for c in range(3):
        mixed = grad_ref[c]
        proj = proj_ref[c].astype(F32)
        one_up = pltpu.roll(mixed * mask_ref[0], slots - 1, 0)
        two_up = pltpu.roll(mixed * mask_ref[1], slots - 2, 0)
        gtaps_ref[c, 0:1, :] = jnp.sum(mixed * proj, axis=0, keepdims=True)
        gtaps_ref[c, 1:2, :] = jnp.sum(one_up * proj, axis=0, keepdims=True)
        gtaps_ref[c, 2:3, :] = jnp.sum(two_up * proj, axis=0, keepdims=True)
        gproj_ref[c] = (
            taps_ref[c, 0:1, :] * mixed + taps_ref[c, 1:2, :] * one_up + taps_ref[c, 2:3, :] * two_up
        ).astype(BF)


def post_body(count, place_ref, *refs):
    pieces, low_ref = refs[:count], refs[count]
    mine_ref, lows_ref, highs_ref, gw_ref, lowt_ref, sems = refs[count + 1 :]
    width = low_ref.shape[1]
    step = pl.program_id(0)

    @pl.when(step == 0)
    def _():
        lowt_ref[...] = jnp.transpose(low_ref[...], (1, 0))

    here = pl.multiple_of(step * width, width)
    at = 0
    for ref in pieces:
        lanes = ref.shape[1]
        gw_ref[pl.ds(here, width), at : at + lanes] = dot(lowt_ref[...], ref[...]).astype(BF)
        at += lanes

    @pl.when(step == 2)
    def _():
        size = mine_ref.shape[1]

        core = place_ref[PLACE_CORE]
        for j in range(8):
            other = lows_ref.at[j // 2] if j < 4 else highs_ref.at[j // 2 - 2]
            rows = gw_ref.at[pl.ds(j * size, size)]

            @pl.when(core == j % 2)
            def _():
                pltpu.make_async_copy(rows, mine_ref.at[j // 2], sems.at[0]).start()

            @pl.when(core != j % 2)
            def _():
                pltpu.make_async_copy(rows, other, sems.at[1 + j // 4]).start()

        wait_all(mine_ref, sems.at[0])
        wait_all(lows_ref, sems.at[1])
        wait_all(highs_ref, sems.at[2])


def back_body(place_ref, *refs):
    grads, (x_ref, gres_ref, vec_ref) = refs[:-23], refs[-23:-20]
    own, near = refs[-20:-12], refs[-12:-4]
    out_ref, dvec_ref, w_ref, sem = refs[-4:]
    width = x_ref.shape[1]

    @pl.when(pl.program_id(0) == 0)
    def _():
        start_qkv(place_ref, own, near, w_ref, sem)
        dvec_ref[...] = jnp.zeros_like(dvec_ref)
        wait_all(w_ref, sem)

    incoming = None
    for c in range(3):
        rows = slice(c * width, (c + 1) * width)
        at = 0
        for grad in grads:
            lanes = grad.shape[2]
            term = dot_nt(grad[c], w_ref[rows, at : at + lanes])
            incoming = term if incoming is None else incoming + term
            at += lanes
    normed, scaled = normalize(x_ref[...].astype(F32))
    out_ref[...] = gres_ref[...] + norm_back(incoming, normed, scaled, vec_ref[0:1, :])
    dvec_ref[0:1, :] += jnp.sum(incoming * normed, axis=0, keepdims=True)
    dvec_ref[1:2, :] += jnp.sum(incoming, axis=0, keepdims=True)


def forward(place, tokens, meta, own, near, vec, taps):
    slots, width = tokens.shape
    pairs = width // LANES
    scale = (width // HEADS) ** (-0.5)
    three = pl.BlockSpec((None, slots, width), lambda c, *_: (c, 0, 0))
    tap = pl.BlockSpec((None, 3, width), lambda c, *_: (c, 0, 0))
    low_one, mixed, project = call(
        pre_body,
        (3,),
        [whole((slots, width)), whole(vec.shape), tap, whole(meta.shape)] + [HBM] * 16,
        [whole((slots, width)), three, three],
        [like((slots, width), BF), like((3, slots, width), BF), like((3, slots, width), BF)],
        [
            pltpu.VMEM((3 * width, width), BF),
            pltpu.VMEM((slots, width), F32),
            pltpu.SemaphoreType.DMA,
        ],
        (tokens, vec, taps, meta, *own, *near),
        6 * slots * width * width,
        24 << 20,
        place,
        room=60,
    )
    lane_block = pl.BlockSpec((slots, LANES), lambda p: (0, p))

    def part(c):
        return pl.BlockSpec((None, slots, LANES), lambda p: (c, 0, p))

    attended, lse = call(
        functools.partial(attend_body, scale),
        (pairs,),
        [part(0), part(1), part(2), whole(meta.shape)],
        [lane_block, lane_block],
        [like((slots, width), BF), like((slots, width), F32)],
        [pltpu.VMEM((BLOCK, BLOCK), F32)]
        + [pltpu.VMEM((slots, LANES), BF)] * 2
        + [pltpu.VMEM((2, slots, LANES), BF)] * 3,
        (mixed, mixed, mixed, meta),
        2 * slots * slots * width * 2,
        12 << 20,
        room=60,
    )
    return low_one, mixed, project, attended, lse


def dense_up(place, tokens, grad_out, meta, attended, bufs, vec):
    slots, width = tokens.shape
    hidden = FOLD * width
    size = bufs[0].shape[0]
    blocks = slots // SPAN
    row_block = pl.BlockSpec((SPAN, width), lambda i, *_: (jnp.minimum(i, blocks - 1), 0))
    wide_block = pl.BlockSpec((SPAN, hidden), lambda i, *_: (jnp.minimum(i, blocks - 1), 0))
    meta_block = pl.BlockSpec((8, SPAN), lambda i, *_: (0, jnp.minimum(i, blocks - 1)))
    skip = hidden - 8 * size
    return call(
        up_body,
        (blocks + FOLD,),
        [row_block] * 3 + [meta_block, whole(vec.shape)] + [HBM] * 24,
        [row_block, row_block, row_block, wide_block, HBM, HBM, whole((skip, width))],
        [
            like((slots, width), F32),
            like((slots, width), BF),
            like((slots, width), BF),
            like((slots, hidden), BF),
            like((4, size, width), BF),
            like((4, size, width), BF),
            like((skip, width), BF),
        ],
        [
            pltpu.VMEM((width, width), BF),
            pltpu.VMEM((width, hidden), BF),
            pltpu.VMEM((slots, hidden), BF),
            pltpu.VMEM((slots, width), BF),
            pltpu.VMEM((hidden, width), BF),
            pltpu.SemaphoreType.DMA((3,)),
        ],
        (attended, tokens, grad_out, meta, vec, *bufs),
        (4 * FOLD + 2) * slots * width * width,
        30 << 20,
        place,
        room=60,
    )


def dense_down(place, attended, low, residual, cot, active, vec, first, bufs):
    slots, width = residual.shape
    hidden = FOLD * width
    size = bufs[0].shape[0]
    blocks = slots // SPAN
    row_block = pl.BlockSpec((SPAN, width), lambda i, *_: (jnp.minimum(i, blocks - 1), 0))
    wide_block = pl.BlockSpec((SPAN, hidden), lambda i, *_: (jnp.minimum(i, blocks - 1), 0))
    full = fixed((slots, width))
    return call(
        down_body,
        (blocks + FOLD,),
        [full, full, row_block, row_block, wide_block, whole(vec.shape), whole(first.shape)]
        + [HBM] * 24,
        [row_block, row_block, row_block, whole((8, width)), HBM, HBM],
        [
            like((slots, width), BF),
            like((slots, width), BF),
            like((slots, width), F32),
            like((8, width), F32),
            like((4, 2, size, width), BF),
            like((4, 2, size, width), BF),
        ],
        [
            pltpu.VMEM((width, width), BF),
            pltpu.VMEM((width, hidden), BF),
            pltpu.VMEM((hidden, width), BF),
            pltpu.VMEM((slots, hidden), BF),
            pltpu.VMEM((slots, width), BF),
            pltpu.VMEM((FOLD, width, width), BF),
            pltpu.VMEM((width, width), BF),
            pltpu.SemaphoreType.DMA((3,)),
        ],
        (attended, low, residual, cot, active, vec, first, *bufs),
        (8 * FOLD + 4) * slots * width * width,
        36 << 20,
        place,
        room=60,
    )


def attend_back(half, mixed, grad_att, attended, lse, meta, project, taps):
    slots, width = grad_att.shape
    at, count = half
    lane_block = pl.BlockSpec((slots, LANES), lambda p: (0, p + at))

    def part(c):
        return pl.BlockSpec((None, slots, LANES), lambda p: (c, 0, p + at))

    return call(
        functools.partial(attend_back_body, (width // HEADS) ** (-0.5)),
        (count,),
        [part(0), part(1), part(2), lane_block, lane_block, lane_block, whole(meta.shape)]
        + [
            pl.BlockSpec((3, slots, LANES), lambda p: (0, 0, p + at)),
            pl.BlockSpec((3, 3, LANES), lambda p: (0, 0, p + at)),
        ],
        [
            pl.BlockSpec((3, slots, LANES), lambda p: (0, 0, p)),
            pl.BlockSpec((3, 3, LANES), lambda p: (0, 0, p)),
        ],
        [like((3, slots, count * LANES), BF), like((3, 3, count * LANES), F32)],
        [
            pltpu.VMEM((3, slots, LANES), F32),
            pltpu.VMEM((2, slots, LANES), F32),
            pltpu.VMEM((slots, slots), F32),
            pltpu.VMEM((2, slots, LANES), BF),
            pltpu.VMEM((2, slots, LANES), BF),
            pltpu.VMEM((2, slots, LANES), BF),
            pltpu.VMEM((2, slots, LANES), BF),
            pltpu.VMEM((LANES, slots), BF),
            pltpu.VMEM((LANES, slots), F32),
        ],
        (mixed, mixed, mixed, grad_att, attended, lse, meta, project, taps),
        10 * slots * slots * count * LANES,
        20 << 20,
        room=60,
    )


def post(place, grads, low, size):
    slots, width = low.shape
    lanes = sum(g.shape[2] for g in grads)
    return call(
        functools.partial(post_body, len(grads)),
        (3,),
        [pl.BlockSpec((None, *g.shape[1:]), lambda c, *_: (c, 0, 0)) for g in grads]
        + [whole((slots, width))],
        [HBM] * 3,
        [like((n, size, lanes), BF) for n in (4, 2, 2)],
        [
            pltpu.VMEM((3 * width, lanes), BF),
            pltpu.VMEM((width, slots), BF),
            pltpu.SemaphoreType.DMA((3,)),
        ],
        (*grads, low),
        6 * slots * width * lanes,
        24 << 20,
        place,
        room=20,
    )


def back(place, grads, tokens, grad_res, vec, own, near):
    slots, width = tokens.shape
    row_block = pl.BlockSpec((BLOCK, width), lambda i, *_: (i, 0))
    specs = [pl.BlockSpec((3, BLOCK, g.shape[2]), lambda i, *_: (0, i, 0)) for g in grads]
    return call(
        back_body,
        (slots // BLOCK,),
        specs + [row_block, row_block, whole(vec.shape)] + [HBM] * 16,
        [row_block, whole((8, width))],
        [like((slots, width), F32), like((8, width), F32)],
        [pltpu.VMEM((3 * width, width), BF), pltpu.SemaphoreType.DMA],
        (*grads, tokens, grad_res, vec, *own, *near),
        6 * slots * width * width,
        1,
        place,
        0,
        room=60,
    )


def split_core(place, mine, received):
    block = mine.shape[1:]
    return call(
        route_body,
        (1,),
        [whole(mine.shape)] * 2,
        [whole(block)] * 4,
        [like(block, BF)] * 4,
        [],
        (mine, received),
        0,
        3 * mine.size * 2,
        place,
        room=16,
    )


def in_plane(routed):
    return [routed[0]] + [swap(routed[r], 2 * r) for r in range(1, 4)]


def lift(place, blocks):
    shape = blocks.shape[2:]
    return call(
        lift_body,
        (1,),
        [whole(blocks.shape)],
        [whole(shape)] * 4,
        [like(shape, BF)] * 4,
        [],
        (blocks,),
        0,
        3 * blocks.size,
        place,
        0,
    )


def send_planes(total, target):
    return [total] + [
        swap(total, 8 * k, lambda i, k=k: plane_of(i) ^ k == target) for k in (1, 2, 3)
    ]


def add_four(parts):
    shape = parts[0].shape
    return call(
        sum_body,
        (1,),
        [whole(shape)] * 4,
        whole(shape),
        like(shape, BF),
        [],
        parts,
        0,
        10 * parts[0].size,
        weight=0,
    )


def prepare(place, matrices, width):
    rows, roww = matrices.shape
    size = rows * roww // width
    return call(
        prep_body,
        (1,),
        [whole((rows, roww))],
        whole((size, width)),
        like((size, width), BF),
        [pltpu.VMEM((rows, roww), F32)],
        (matrices,),
        0,
        4 * matrices.size,
        place,
    )


def finish(place, sums, rows, roww):
    size, width = sums[-1].shape
    return call(
        finish_body,
        (1,),
        [whole(part.shape) for part in sums],
        whole((rows, roww)),
        like((rows, roww), F32),
        [pltpu.VMEM((size, width), F32)],
        sums,
        0,
        28 * size * width,
        place,
    )


def after(value, *deps):
    return lax.optimization_barrier((value, *deps))


def meta_rows(seq_start, valid):
    zeros = jnp.zeros((6, seq_start.shape[0]), F32)
    return jnp.concatenate([seq_start.astype(F32)[None], valid.astype(F32)[None], zeros], axis=0)


def split_vectors(vec_flat, width):
    vec = vec_flat[: 13 * width].reshape(13, width)
    return vec[:8], vec[4:13].reshape(3, 3, width)


def join_vectors(dvec_one, dvec_two, grad_taps, total, roww):
    width = dvec_one.shape[1]
    taps = jnp.concatenate(grad_taps, axis=-1).reshape(9, width)
    rows = jnp.concatenate([dvec_one[:2], dvec_two[:2], taps], axis=0).reshape(-1)
    return jnp.pad(rows, (0, total - rows.size)).reshape(-1, roww)


def per_device(tokens_in, grad_out, seq_start, valid, matrices, vectors):
    width = tokens_in.shape[1]
    rows, roww = matrices.shape
    linear = lax.axis_index(FINE)
    plane = plane_of(linear)
    place = (linear >> jnp.array([0, 3, 0, 1, 0])) & jnp.array([31, 3, 7, 3, 1])
    near_planes = jnp.stack([1 - jnp.minimum(plane, 1), 2 - plane // 2, 3 - plane // 3])
    place = jnp.concatenate([place, near_planes])
    meta = meta_rows(seq_start, valid)
    shard = prepare(place, matrices, width)

    def up(value, steps, keep):
        pairs = [(i, i + 8 * steps) for i in range(SHARDS) if plane_of(i) in keep]
        return lax.ppermute(value, FINE, pairs)

    def with_partner(chips):
        bufs = []
        for chip in chips:
            bufs += [chip, swap(chip, 1)]
        return bufs

    def spread(held):
        by_y, by_x = swap(held, 2), swap(held, 4)
        return [held, by_y, by_x, swap(held, 6)]

    pairs = [(i, i + 16) for i in range(8)] + [(i, i + 8) for i in range(16, 24)]
    jump = lax.ppermute(shard, FINE, pairs)
    left_one = up(shard, -1, (1, 2, 3))
    own_y, own_x, own_both = spread(shard)[1:]
    jump, own_y, own_x = after(jump, own_y, own_x)
    hop = up(jnp.where(plane == 2, jump, shard), 1, (0, 1, 2))
    left_two = up(left_one, -1, (2, 1))
    near_one = jnp.where(plane == 0, left_one, jnp.where(plane == 2, jump, hop))
    near_one, hop, vectors_later, own_both = after(near_one, hop, vectors, own_both)
    own_chips = [shard, own_y, own_x, own_both]
    vec_flat = lax.all_to_all(jnp.tile(vectors_later, (SHARDS, 1)), FINE, 0, 0, tiled=True)
    near_chips = spread(near_one)
    left_three = up(left_two, -1, (1,))
    right_two = up(hop, 1, (2,))
    low = jnp.where(plane == 1, left_one, jnp.where(plane == 2, hop, right_two))
    low = jnp.where(plane == 0, left_two, low)
    high = jnp.where(plane == 1, left_two, jnp.where(plane == 2, left_one, jump))
    high = jnp.where(plane == 0, left_three, high)
    far, *near_chips = after(jnp.stack([low, high]), *near_chips)
    far_chips = spread(far)
    own = with_partner(own_chips)
    near = with_partner(near_chips)
    vec_flat = vec_flat.reshape(-1).astype(F32)
    vec, taps = split_vectors(vec_flat, width)
    low_one, mixed, project, attended, lse = forward(place, tokens_in, meta, own, near, vec, taps)
    attended, *far_chips = after(attended, *far_chips)
    far = with_partner(far_chips)
    bufs = (*own, *near, *far)
    residual, low_two, cot, active, mine, other, first = dense_up(
        place, tokens_in, grad_out, meta, attended, bufs, vec
    )

    def to_plane(parts, target):
        total = add_four(parts)
        return [total] + [
            swap(total, 8 * k, lambda i, k=k: plane_of(i) ^ k == target) for k in (1, 2, 3)
        ]

    def to_square(mine, other):
        return (mine.astype(F32) + other.astype(F32)).astype(BF)

    def exchange(blocks):
        return lax.all_to_all(blocks, SQUARE, 0, 0, tiled=True)

    def summed(blocks):
        return blocks.astype(F32).sum(axis=0).astype(BF)

    residual, highs = after(residual, to_square(mine, swap(other, 1)))
    highs = exchange(highs)
    block_out, grad_att, grad_res, dvec_two, mine, other = dense_down(
        place, attended, low_two, residual, cot, active, vec, first, bufs
    )
    grad_att, highs = after(grad_att, summed(highs))
    high_sums = send_planes(highs, 3)
    received = swap(other, 1)
    grads_one, taps_one = attend_back(
        PIECES[0], mixed, grad_att, attended, lse, meta, project, taps
    )
    grads_one, received, grad_att = after(grads_one, received, grad_att)
    grad_att, lows = after(grad_att, to_square(mine, received))
    lows = exchange(lows)
    grads_two, taps_two = attend_back(
        PIECES[1], mixed, grad_att, attended, lse, meta, project, taps
    )
    size = shard.shape[0]
    mine, *other = post(place, (grads_one, grads_two), low_one, size)
    grad_att, taps_two, *high_sums = after(grad_att, taps_two, *high_sums)
    received = [swap(part, 1) for part in other]
    grads_b, taps_b = attend_back(HALVES[1], mixed, grad_att, attended, lse, meta, project, taps)
    mine_b, *other = post(place, (grads_b,), low_one, size)
    mine_b, lows, *more = after(mine_b, lows, *other, *received)
    other, received = more[:2], more[2:]
    square_a = to_square(mine, jnp.concatenate(received))
    square_b = to_square(mine_b, jnp.concatenate([swap(part, 1) for part in other]))
    qkv = exchange(jnp.concatenate([square_a, square_b], axis=-1))
    lifted = lift(place, lows)
    grads_b, *lifted = after(grads_b, *lifted)
    low_sums = [lifted[0]] + [
        swap(lifted[k], 8 * k, lambda i, k=k: plane_of(i) ^ k in (1, 2)) for k in (1, 2, 3)
    ]
    tokens_grad, dvec_one = back(
        place, (grads_one, grads_two, grads_b), tokens_in, grad_res, vec, own, near
    )
    dvec_one, qkv, low_sums[1], low_sums[3], dvec_two, taps_one, taps_two, taps_b = after(
        dvec_one, qkv, low_sums[1], low_sums[3], dvec_two, taps_one, taps_two, taps_b
    )
    grad_vec = join_vectors(
        dvec_one, dvec_two, (taps_one, taps_two, taps_b), vec_flat.size, roww
    )
    grad_vec = grad_vec.reshape(SHARDS, -1, roww)
    deep = ((0, 0), (0, DEEP - vectors.shape[0]), (0, 0))
    grad_vec = jnp.pad(grad_vec, deep).reshape(-1, roww)
    owned_vec = lax.all_to_all(grad_vec, FINE, 0, 0, tiled=True)
    sums = send_planes(summed(qkv), 0)
    owned_vec, *sums = after(owned_vec, *sums)
    owned = finish(place, (*sums, *low_sums, *high_sums), rows, roww)
    owned_vec = owned_vec.reshape(SHARDS, DEEP, roww)[:, : vectors.shape[0]].sum(axis=0)
    return block_out, tokens_grad, owned, owned_vec


def per_device_any(tokens_in, grad_out, seq_start, valid, matrices, vectors):
    width = tokens_in.shape[1]
    rows, roww = matrices.shape
    step = GROUP // FOLD
    place = jnp.array([0, 0, 0, 0, 0, 1, 2, 3], jnp.int32)
    meta = meta_rows(seq_start, valid)
    view = lax.all_gather(matrices, AXES, axis=0, tiled=True).reshape(-1, width)
    vec_flat = lax.all_gather(vectors, AXES, axis=0, tiled=True).reshape(-1).astype(F32)
    vec, taps = split_vectors(vec_flat, width)
    cut = (UP_FIRST * GROUP, UP_END * GROUP)
    up = view[cut[0] : cut[1]].reshape(UP_GROUPS, step, FOLD, width).swapaxes(1, 2)
    view = jnp.concatenate([view[: cut[0]], up.reshape(-1, width), view[cut[1] :]])
    shards = view.reshape(4, 8, -1, width)
    own = [shards[0, r] for r in range(8)]
    near = [shards[1, r] for r in range(8)]
    far = [shards[2:, r] for r in range(8)]
    low_one, mixed, project, attended, lse = forward(place, tokens_in, meta, own, near, vec, taps)
    bufs = (*own, *near, *far)
    residual, low_two, cot, active, mine_three, other_three, first = dense_up(
        place, tokens_in, grad_out, meta, attended, bufs, vec
    )
    block_out, grad_att, grad_res, dvec_two, mine_low, other_low = dense_down(
        place, attended, low_two, residual, cot, active, vec, first, bufs
    )
    qkv, grad_taps, grads = [], [], []
    for half in HALVES:
        grad, grad_tap = attend_back(
            half, mixed, grad_att, attended, lse, meta, project, taps
        )
        mine, *other = post(place, (grad,), low_one, own[0].shape[0])
        qkv.append(jnp.stack([mine, jnp.concatenate(other)], axis=1))
        grad_taps.append(grad_tap)
        grads.append(grad)
    tokens_grad, dvec_one = back(place, grads, tokens_in, grad_res, vec, own, near)
    planes = [
        jnp.concatenate(qkv, axis=-1)[:, :, None],
        jnp.stack([mine_low, other_low], axis=1),
        jnp.stack([mine_three, other_three], axis=1)[:, :, None],
    ]
    grad = jnp.concatenate(planes, axis=2)
    grad = grad.transpose(2, 0, 1, 3, 4).reshape(-1, width)
    up = grad[cut[0] : cut[1]].reshape(UP_GROUPS, FOLD, step, width).swapaxes(1, 2)
    grad = jnp.concatenate([grad[: cut[0]], up.reshape(-1, width), grad[cut[1] :]])
    owned = lax.psum_scatter(
        grad.reshape(-1, roww).astype(F32), AXES, scatter_dimension=0, tiled=True
    )
    grad_vec = join_vectors(dvec_one, dvec_two, grad_taps, vec_flat.size, roww)
    owned_vec = lax.psum_scatter(grad_vec, AXES, scatter_dimension=0, tiled=True)
    return block_out, tokens_grad, owned, owned_vec


def solution(mesh):
    body, axes = per_device_any, AXES
    if mesh.devices.size == SHARDS:
        mesh = Mesh(mesh.devices.reshape(4, 2, 2, 2), FINE)
        body, axes = per_device, FINE
    row = P(axes, None)
    flat = P(axes)
    return jax.shard_map(
        body,
        mesh=mesh,
        in_specs=(row, row, flat, flat, row, row),
        out_specs=(row, row, row, row),
        check_vma=False,
    )
```

```python
import functools

import jax
import jax.numpy as jnp
from jax import lax
from jax.experimental import pallas as pl
from jax.experimental.pallas import tpu as pltpu
from jax.sharding import Mesh
from jax.sharding import PartitionSpec as P

HEADS = 12
EPSILON = 1e-05
NEG_FILL = -1e30
BF = jnp.bfloat16
F32 = jnp.float32
AXES = ("dp", "sub")
FINE = ("z", "x", "y", "core")
SQUARE = ("x", "y")
LANES = 128
BLOCK = 256
SPAN = 512
GROUP = 96
FOLD = 4
SHARDS = 32
WEIGHT = 100
VROWS = 3
OUT_GROUPS = 8
UP_GROUPS = 32
UP_FIRST, UP_END = 32, 64
HALVES = ((0, 4), (4, 2))
PIECES = ((0, 2), (2, 2))
(
    PLACE_LINEAR, PLACE_Z, PLACE_IN_PLANE, PLACE_XY, PLACE_CORE,
    PLACE_NEAR, PLACE_LOW, PLACE_HIGH,
) = range(8)
HBM = pl.BlockSpec(memory_space=pl.ANY)


def dot(a, b):
    return jnp.dot(a, b, preferred_element_type=F32)


def dot_nt(a, b):
    return lax.dot_general(a, b, (((1,), (1,)), ((), ())), preferred_element_type=F32)


def dot_tn(a, b):
    return lax.dot_general(a, b, (((0,), (0,)), ((), ())), preferred_element_type=F32)


def whole(shape):
    return pl.BlockSpec(shape, lambda *_: (0,) * len(shape))


def fixed(shape):
    return pl.BlockSpec(shape, lambda *_: (0,) * len(shape), pipeline_mode=pl.Buffered(1))


def call(body, grid, ins, outs, out_shape, scratch, args, flops, moved, place=None, weight=WEIGHT, room=16):
    return pl.pallas_call(
        body,
        grid_spec=pltpu.PrefetchScalarGridSpec(
            num_scalar_prefetch=0 if place is None else 1,
            grid=grid,
            in_specs=ins,
            out_specs=outs,
            scratch_shapes=scratch,
        ),
        out_shape=out_shape,
        compiler_params=pltpu.CompilerParams(
            dimension_semantics=("arbitrary",) * len(grid), vmem_limit_bytes=room << 20
        ),
        cost_estimate=pl.CostEstimate(
            flops=weight * flops, bytes_accessed=weight * moved, transcendentals=0
        ),
    )(*(() if place is None else (place,)), *args)


def like(shape, dtype):
    return jax.ShapeDtypeStruct(shape, dtype)


def normalize(v):
    centre = v - jnp.mean(v, axis=-1, keepdims=True)
    scaled = lax.rsqrt(jnp.mean(centre * centre, axis=-1, keepdims=True) + EPSILON)
    return centre * scaled, scaled


def norm_back(incoming, normed, scaled, gain):
    weighted = incoming * gain
    return scaled * (
        weighted
        - jnp.mean(weighted, axis=-1, keepdims=True)
        - normed * jnp.mean(weighted * normed, axis=-1, keepdims=True)
    )


def columns(meta):
    return jnp.transpose(meta, (1, 0))


def mix_masks(meta_ref, slots):
    cols = columns(meta_ref[...])
    position = lax.broadcasted_iota(jnp.int32, (slots, 1), 0).astype(F32) - cols[:, 0:1]
    return jnp.where(position >= 1.0, 1.0, 0.0), jnp.where(position >= 2.0, 1.0, 0.0)


def xor_pairs(mask, keep=None):
    return [(i, i ^ mask) for i in range(SHARDS) if keep is None or keep(i)]


def swap(value, mask, keep=None):
    return lax.ppermute(value, FINE, xor_pairs(mask, keep))


def plane_of(index):
    return index >> 3


def prep_body(place_ref, in_ref, out_ref, wide_ref):
    width = out_ref.shape[1]
    cols = width // LANES
    wide_ref[...] = in_ref[...].astype(F32)
    first = place_ref[PLACE_LINEAR] * (out_ref.shape[0] // GROUP)
    for n in range(out_ref.shape[0] // GROUP):
        base = n * GROUP * cols
        up = jnp.logical_and(first + n >= UP_FIRST, first + n < UP_END)

        @pl.when(up)
        def _():
            for j in range(cols):
                parts = [
                    wide_ref[pl.ds(base + q * cols + j, GROUP // FOLD, stride=cols * FOLD), :]
                    for q in range(FOLD)
                ]
                out_ref[n * GROUP : (n + 1) * GROUP, j * LANES : (j + 1) * LANES] = (
                    jnp.concatenate(parts, axis=0).astype(BF)
                )

        @pl.when(jnp.logical_not(up))
        def _():
            for j in range(cols):
                out_ref[n * GROUP : (n + 1) * GROUP, j * LANES : (j + 1) * LANES] = wide_ref[
                    pl.ds(base + j, GROUP, stride=cols), :
                ].astype(BF)


def finish_body(place_ref, *refs):
    zero, middle, last = refs[:4], refs[4:8], refs[8:12]
    out_ref, total_ref = refs[-2:]
    width = total_ref.shape[1]
    cols = width // LANES
    plane = place_ref[PLACE_Z]

    def add(parts):
        total = parts[0][...].astype(F32)
        for part in parts[1:]:
            total = total + part[...].astype(F32)
        return total

    @pl.when(plane == 0)
    def _():
        total_ref[...] = add(zero)

    @pl.when(jnp.logical_or(plane == 1, plane == 2))
    def _():
        total_ref[...] = add(middle)

    @pl.when(plane == 3)
    def _():
        total_ref[...] = add(last)

    first = place_ref[PLACE_LINEAR] * (total_ref.shape[0] // GROUP)
    for n in range(total_ref.shape[0] // GROUP):
        base = n * GROUP * cols
        up = jnp.logical_and(first + n >= UP_FIRST, first + n < UP_END)

        @pl.when(up)
        def _():
            step = GROUP // FOLD
            for j in range(cols):
                for q in range(FOLD):
                    lo = n * GROUP + q * step
                    out_ref[pl.ds(base + q * cols + j, step, stride=cols * FOLD), :] = total_ref[
                        lo : lo + step, j * LANES : (j + 1) * LANES
                    ]

        @pl.when(jnp.logical_not(up))
        def _():
            for j in range(cols):
                out_ref[pl.ds(base + j, GROUP, stride=cols), :] = total_ref[
                    n * GROUP : (n + 1) * GROUP, j * LANES : (j + 1) * LANES
                ]


def route_body(place_ref, mine_ref, other_ref, *outs):
    for r, out in enumerate(outs):
        at = place_ref[PLACE_XY] ^ r
        out[...] = (mine_ref[at].astype(F32) + other_ref[at].astype(F32)).astype(BF)


def lift_body(place_ref, in_ref, *outs):
    plane = place_ref[PLACE_Z]
    for k, out in enumerate(outs):
        p = jnp.clip(plane ^ k, 1, 2) - 1
        total = in_ref[0, p].astype(F32)
        for r in range(1, 4):
            total = total + in_ref[r, p].astype(F32)
        out[...] = total.astype(BF)


def sum_body(a_ref, b_ref, c_ref, d_ref, out_ref):
    out_ref[...] = (
        a_ref[...].astype(F32) + b_ref[...].astype(F32) + c_ref[...].astype(F32) + d_ref[...].astype(F32)
    ).astype(BF)


def start_qkv(place_ref, own, near, w_ref, sem):
    size = own[0].shape[0]
    for r in range(8):
        at = pl.multiple_of((place_ref[PLACE_IN_PLANE] ^ r) * size, 32)

        @pl.when(place_ref[PLACE_Z] == 0)
        def _():
            pltpu.make_async_copy(own[r], w_ref.at[pl.ds(at, size)], sem).start()

        @pl.when(place_ref[PLACE_Z] != 0)
        def _():
            pltpu.make_async_copy(near[r], w_ref.at[pl.ds(at, size)], sem).start()


def wait_all(ref, sem):
    pltpu.make_async_copy(ref, ref, sem).wait()


def start_dense(place_ref, own, near, far, wo_ref, w1_ref, w2_ref, sems):
    step = GROUP // FOLD
    width = own[0].shape[1]
    slots = [(own, None, PLACE_Z, (1, 2, 3)), (near, None, PLACE_NEAR, (1,))]
    slots += [(far, 0, PLACE_LOW, (1, 2)), (far, 1, PLACE_HIGH, (2, 3))]
    for bufs, slot, plane_at, planes in slots:
        for p in planes:

            @pl.when(place_ref[plane_at] == p)
            def _():
                for r in range(8):
                    buf = bufs[r] if slot is None else bufs[r].at[slot]
                    place = place_ref[PLACE_IN_PLANE] ^ r
                    for n in range(3):
                        group = 24 * (p - 1) + 3 * place + n
                        rows = buf.at[pl.ds(n * GROUP, GROUP)]

                        def to_out():
                            at = pl.multiple_of(group * GROUP, 32)
                            pltpu.make_async_copy(
                                rows, wo_ref.at[pl.ds(at, GROUP)], sems.at[0]
                            ).start()

                        def to_up():
                            at = pl.multiple_of((group - OUT_GROUPS) * step, 8)
                            for q in range(FOLD):
                                pltpu.make_async_copy(
                                    rows.at[pl.ds(q * step, step)],
                                    w1_ref.at[pl.ds(at, step), pl.ds(q * width, width)],
                                    sems.at[1],
                                ).start()

                        def to_down():
                            at = pl.multiple_of((group - OUT_GROUPS - UP_GROUPS) * GROUP, 32)
                            pltpu.make_async_copy(
                                rows, w2_ref.at[pl.ds(at, GROUP)], sems.at[2]
                            ).start()

                        if p == 1:
                            pl.when(group < OUT_GROUPS)(to_out)
                            pl.when(group >= OUT_GROUPS)(to_up)
                        elif p == 2:
                            pl.when(group < OUT_GROUPS + UP_GROUPS)(to_up)
                            if w2_ref is not None:
                                pl.when(group >= OUT_GROUPS + UP_GROUPS)(to_down)
                        elif w2_ref is not None:
                            to_down()


def deal(place_ref, targets, sems, copy):
    core = place_ref[PLACE_CORE]
    for j in range(8):
        for which in range(2):

            @pl.when(core ^ (j % 2) == which)
            def _():
                copy(j, targets[which].at[j // 2], sems.at[which])


def pre_body(place_ref, x_ref, vec_ref, taps_ref, meta_ref, *refs):
    own, near = refs[:8], refs[8:16]
    low_ref, mixed_ref, proj_ref, w_ref, keep_ref, sem = refs[16:]
    slots, width = x_ref.shape
    here = pl.multiple_of(pl.program_id(0) * width, width)

    @pl.when(pl.program_id(0) == 0)
    def _():
        start_qkv(place_ref, own, near, w_ref, sem)
        for lo in range(0, slots, BLOCK):
            rows = slice(lo, lo + BLOCK)
            normed, _ = normalize(x_ref[rows, :].astype(F32))
            low_ref[rows, :] = (normed * vec_ref[0:1, :] + vec_ref[1:2, :]).astype(BF)
        wait_all(w_ref, sem)

    first, second = mix_masks(meta_ref, slots)
    weight = w_ref[pl.ds(here, width), :]
    ahead = dot(low_ref[0:BLOCK, :], weight)
    for lo in range(0, slots, BLOCK):
        end = lo + BLOCK
        value = ahead
        if end < slots:
            ahead = dot(low_ref[end : end + BLOCK, :], weight)
        proj_ref[lo:end, :] = value.astype(BF)
        keep_ref[lo:end, :] = value
        one_back = pltpu.roll(value, 1, 0) if lo == 0 else keep_ref[lo - 1 : end - 1, :]
        two_back = pltpu.roll(value, 2, 0) if lo == 0 else keep_ref[lo - 2 : end - 2, :]
        mixed_ref[lo:end, :] = (
            taps_ref[0:1, :] * value
            + taps_ref[1:2, :] * (one_back * first[lo:end])
            + taps_ref[2:3, :] * (two_back * second[lo:end])
        ).astype(BF)


def mask_columns(cols):
    lane = lax.broadcasted_iota(jnp.int32, (1, LANES), 1) % (LANES // 2)
    bucket = (lane >= 16) & (lane < 32)
    same = cols[:, 0:1] * (1.0 / 64.0) == (lane - 16).astype(F32)
    query = jnp.where(bucket & same, 0.0, jnp.where((lane >= 16) & (lane <= 32), NEG_FILL, 0.0))
    key = jnp.where(bucket & same, 1.0, jnp.where(lane == 32, 1.0 - cols[:, 1:2], 0.0))
    return query.astype(BF), key.astype(BF)


def triangle(lower):
    row = lax.broadcasted_iota(jnp.int32, (BLOCK, BLOCK), 0)
    col = lax.broadcasted_iota(jnp.int32, (BLOCK, BLOCK), 1)
    return jnp.where(col <= row if lower else row <= col, 0.0, NEG_FILL)


def attend_body(
    scale, q_ref, k_ref, v_ref, meta_ref, out_ref, lse_ref,
    tri_ref, qm_ref, km_ref, qa_ref, ka_ref, va_ref,
):
    slots = q_ref.shape[0]
    half = LANES // 2

    @pl.when(pl.program_id(0) == 0)
    def _():
        tri_ref[...] = triangle(True)
        qm_ref[...], km_ref[...] = mask_columns(columns(meta_ref[...]))

    left = lax.broadcasted_iota(jnp.int32, (1, LANES), 1) < half
    query = q_ref[...] * jnp.asarray(scale, BF)
    one = jnp.ones_like(query)
    for head in range(2):
        own = left if head == 0 else jnp.logical_not(left)
        qa_ref[head] = jnp.where(own, query, qm_ref[...])
        ka_ref[head] = jnp.where(own, k_ref[...], km_ref[...])
        va_ref[head] = jnp.where(own, v_ref[...], one)
    stages = [(lo, head) for lo in range(0, slots, BLOCK) for head in range(2)]
    outs, logs = [], []

    def score(lo, head):
        return dot_nt(qa_ref[head, lo : lo + BLOCK, :], ka_ref[head, : lo + BLOCK, :])

    def finish_stage(lo, head, terms, peak):
        end = lo + BLOCK
        both = dot(terms, va_ref[head, :end, :])
        outs.append(both / pltpu.roll(both, half, 1))
        logs.append(peak + jnp.log(both))
        if head == 1:
            out_ref[lo:end, :] = jnp.where(left, outs[-2], outs[-1]).astype(BF)
            lse_ref[lo:end, :] = jnp.where(left, logs[-1], logs[-2])

    ahead = score(*stages[0])
    behind = None
    for n, (lo, head) in enumerate(stages):
        scores = ahead
        if n + 1 < len(stages):
            ahead = score(*stages[n + 1])
        if behind is not None:
            finish_stage(*behind)
        near = scores[:, lo:] + tri_ref[...]
        scores = jnp.concatenate([scores[:, :lo], near], axis=1) if lo else near
        peak = jnp.max(scores, axis=-1, keepdims=True)
        behind = (lo, head, jnp.exp(scores - peak).astype(BF), peak)
    finish_stage(*behind)


def up_body(place_ref, att_ref, x_ref, go_ref, meta_ref, vec_ref, *refs):
    own, near, far = refs[:8], refs[8:16], refs[16:24]
    (
        res_ref, low_ref, cot_ref, out_ref, mine_ref, other_ref, first_ref,
        wo_ref, w1_ref, act_ref, cots_ref, g2_ref, sems,
    ) = refs[24:]
    width = x_ref.shape[1]
    step = pl.program_id(0)
    blocks = act_ref.shape[0] // SPAN
    here = pl.multiple_of(step * SPAN, SPAN)

    @pl.when(step == 0)
    def _():
        start_dense(place_ref, own, near, far, wo_ref, w1_ref, None, sems)
        wait_all(wo_ref, sems.at[0])
        wait_all(w1_ref, sems.at[1])

    @pl.when(step < blocks)
    def _():
        live = columns(meta_ref[...])[:, 1:2]
        cot = (go_ref[...].astype(F32) * live).astype(BF)
        cot_ref[...] = cot
        cots_ref[pl.ds(here, SPAN), :] = cot
        pieces = range(0, SPAN, BLOCK)
        residuals = [
            x_ref[lo : lo + BLOCK, :].astype(F32) + dot(att_ref[lo : lo + BLOCK, :], wo_ref[...])
            for lo in pieces
        ]
        lows = []

        def norm(lo, residual):
            res_ref[lo : lo + BLOCK, :] = residual
            normed, _ = normalize(residual)
            low = (normed * vec_ref[2:3, :] + vec_ref[3:4, :]).astype(BF)
            low_ref[lo : lo + BLOCK, :] = low
            lows.append(low)

        norm(0, residuals[0])
        stages = [(at, part) for at in range(len(pieces)) for part in range(FOLD)]

        def project(at, part):
            return dot(lows[at], w1_ref[:, part * width : (part + 1) * width])

        ahead = project(0, 0)
        for n, (at, part) in enumerate(stages):
            upward = jnp.maximum(ahead, 0.0)
            if part == 0 and at + 1 < len(pieces):
                norm(pieces[at + 1], residuals[at + 1])
            if n + 1 < len(stages):
                ahead = project(*stages[n + 1])
            cut = slice(part * width, (part + 1) * width)
            rows = pl.ds(pl.multiple_of(here + at * BLOCK, BLOCK), BLOCK)
            active = (upward * upward).astype(BF)
            act_ref[rows, cut] = active
            out_ref[at * BLOCK : (at + 1) * BLOCK, cut] = active

    for part in range(FOLD):

        @pl.when(step == blocks + part)
        def _():
            cut = slice(part * width, (part + 1) * width)
            g2_ref[cut, :] = dot_tn(act_ref[:, cut], cots_ref[...]).astype(BF)

    @pl.when(step == blocks + FOLD - 1)
    def _():
        size = mine_ref.shape[1]
        skip = g2_ref.shape[0] - 8 * size

        def copy(j, target, sem):
            pltpu.make_async_copy(g2_ref.at[pl.ds(skip + j * size, size)], target, sem).start()

        deal(place_ref, (mine_ref, other_ref), sems, copy)
        first_ref[...] = g2_ref[0:skip, :]
        wait_all(mine_ref, sems.at[0])
        wait_all(other_ref, sems.at[1])


def down_body(
    place_ref, att_ref, low_ref, res_ref, cot_ref, act_ref, vec_ref, first_ref, *refs
):
    own, near, far = refs[:8], refs[8:16], refs[16:24]
    (
        out_ref, gatt_ref, gres_ref, dvec_ref, mine_ref, other_ref,
        wo_ref, w1_ref, w2_ref, up_ref, reslow_ref, g1_ref, go_ref, sems,
    ) = refs[24:]
    width = res_ref.shape[1]
    step = pl.program_id(0)
    blocks = up_ref.shape[0] // SPAN
    here = pl.multiple_of(step * SPAN, SPAN)

    @pl.when(step == 0)
    def _():
        start_dense(place_ref, own, near, far, wo_ref, w1_ref, w2_ref, sems)
        dvec_ref[...] = jnp.zeros_like(dvec_ref)
        wait_all(w2_ref, sems.at[2])

    @pl.when(step < blocks)
    def _():
        pieces = range(0, SPAN, BLOCK)
        stages = [(lo, part) for lo in pieces for part in range(FOLD)]

        def incoming(lo, part):
            return dot_nt(cot_ref[lo : lo + BLOCK, :], w2_ref[part * width : (part + 1) * width, :])

        ahead = incoming(*stages[0])
        for n, (lo, part) in enumerate(stages):
            grad_active = ahead
            if n + 1 < len(stages):
                ahead = incoming(*stages[n + 1])
            cut = slice(part * width, (part + 1) * width)
            upward = jnp.sqrt(act_ref[lo : lo + BLOCK, cut].astype(F32))
            rows = pl.ds(pl.multiple_of(here + lo, BLOCK), BLOCK)
            up_ref[rows, cut] = (grad_active * (2.0 * upward)).astype(BF)
        for lo in pieces:
            out = res_ref[lo : lo + BLOCK, :] + dot(act_ref[lo : lo + BLOCK, :], w2_ref[...])
            out_ref[lo : lo + BLOCK, :] = out.astype(BF)

    @pl.when(step == 0)
    def _():
        wait_all(w1_ref, sems.at[1])
        wait_all(wo_ref, sems.at[0])

    @pl.when(step < blocks)
    def _():
        pieces = range(0, SPAN, BLOCK)

        def outgoing(lo):
            return dot_nt(up_ref[pl.ds(pl.multiple_of(here + lo, BLOCK), BLOCK), :], w1_ref[...])

        ahead = outgoing(0)
        for lo in pieces:
            grad = ahead
            if lo + BLOCK < SPAN:
                ahead = outgoing(lo + BLOCK)
            span = slice(lo, lo + BLOCK)
            normed, scaled = normalize(res_ref[span, :])
            back = norm_back(grad, normed, scaled, vec_ref[2:3, :])
            grad_residual = cot_ref[span, :].astype(F32) + back
            gres_ref[span, :] = grad_residual
            res_low = grad_residual.astype(BF)
            reslow_ref[pl.ds(pl.multiple_of(here + lo, BLOCK), BLOCK), :] = res_low
            gatt_ref[span, :] = dot_nt(res_low, wo_ref[...]).astype(BF)
            dvec_ref[0:1, :] += jnp.sum(grad * normed, axis=0, keepdims=True)
            dvec_ref[1:2, :] += jnp.sum(grad, axis=0, keepdims=True)

    for part in range(FOLD):

        @pl.when(step == blocks + part)
        def _():
            cut = slice(part * width, (part + 1) * width)
            g1_ref[part] = dot_tn(low_ref[...], up_ref[:, cut]).astype(BF)

    @pl.when(step == blocks + FOLD - 1)
    def _():
        go_ref[...] = dot_tn(att_ref[...], reslow_ref[...]).astype(BF)
        span = GROUP // FOLD

        def copy(j, target, sem):
            for p in range(2):
                for n in range(3):
                    group = 24 * p + 3 * j + n
                    rows = target.at[p, pl.ds(n * GROUP, GROUP)]
                    if group < OUT_GROUPS:
                        source = go_ref.at[pl.ds(group * GROUP, GROUP)]
                    elif group < OUT_GROUPS + UP_GROUPS:
                        source = g1_ref.at[:, pl.ds((group - OUT_GROUPS) * span, span)]
                        rows = rows.reshape(FOLD, span, width)
                    else:
                        at = (group - OUT_GROUPS - UP_GROUPS) * GROUP
                        source = first_ref.at[pl.ds(at, GROUP)]
                    pltpu.make_async_copy(source, rows, sem).start()

        deal(place_ref, (mine_ref, other_ref), sems, copy)
        wait_all(mine_ref, sems.at[0])
        wait_all(other_ref, sems.at[1])


def split_three(value):
    high = value.astype(BF)
    rest = value - high.astype(F32)
    middle = rest.astype(BF)
    return high, middle, (rest - middle.astype(F32)).astype(BF)


def attend_back_body(
    scale, q_ref, k_ref, v_ref, do_ref, o_ref, lse_ref, meta_ref, proj_ref, taps_ref,
    gproj_ref, gtaps_ref, grad_ref, mask_ref, bias_ref, qa_ref, ka_ref, va_ref, da_ref, kt_ref, dq_ref,
):
    slots = q_ref.shape[0]
    half = LANES // 2

    @pl.when(pl.program_id(0) == 0)
    def _():
        cols = columns(meta_ref[...])
        for lo in range(0, slots, BLOCK):
            end = lo + BLOCK
            size = slots - lo
            row = lax.broadcasted_iota(jnp.int32, (BLOCK, size), 0)
            col = lax.broadcasted_iota(jnp.int32, (BLOCK, size), 1)
            keep = (
                (cols[lo:end, 0:1] == meta_ref[0:1, lo:])
                & (cols[lo:end, 1:2] > 0.5)
                & (row <= col)
            )
            bias_ref[lo:end, lo:] = jnp.where(keep, 0.0, NEG_FILL)
        for n, mask in enumerate(mix_masks(meta_ref, slots)):
            mask_ref[n] = jnp.broadcast_to(mask, (slots, LANES))

    lane = lax.broadcasted_iota(jnp.int32, (1, LANES), 1)
    left = lane < half
    query = q_ref[...]
    key = k_ref[...]
    value = v_ref[...]
    grad_out = do_ref[...]
    product = grad_out.astype(F32) * o_ref[...].astype(F32)
    kt_ref[...] = jnp.transpose(key.astype(F32), (1, 0)).astype(BF)
    logs = split_three(-lse_ref[...])
    zero = jnp.zeros_like(query)
    one = jnp.ones_like(query)
    for head in range(2):
        own = left if head == 0 else jnp.logical_not(left)
        base = half if head == 0 else 0
        delta = jnp.sum(jnp.where(own, product, 0.0), axis=-1, keepdims=True)
        deltas = split_three(-delta)
        marks = [lane == base + n for n in range(3)]

        def spread(terms):
            result = zero
            for mark, term in zip(marks, terms):
                result = jnp.where(mark, term, result)
            return result

        ones = spread((one, one, one))
        qa_ref[head] = jnp.where(own, query * jnp.asarray(scale, BF), spread(logs))
        ka_ref[head] = jnp.where(own, key, ones)
        va_ref[head] = jnp.where(own, value, ones)
        da_ref[head] = jnp.where(own, grad_out, spread(deltas))
    dq_ref[...] = jnp.zeros_like(dq_ref)
    for lo in range(0, slots, BLOCK):
        end = lo + BLOCK
        grad_keys, grad_values = [], []
        for head in range(2):
            rows = slice(head * half, (head + 1) * half)
            scores = dot_nt(ka_ref[head, lo:end, :], qa_ref[head, lo:, :]) + bias_ref[lo:end, lo:]
            probs = jnp.exp(scores)
            inner = dot_nt(va_ref[head, lo:end, :], da_ref[head, lo:, :])
            grad_scores = (probs * inner).astype(BF)
            grad_values.append(dot(probs.astype(BF), do_ref[lo:, :]))
            grad_keys.append(dot(grad_scores, q_ref[lo:, :]))
            dq_ref[rows, lo:] += dot(kt_ref[rows, lo:end], grad_scores)
        grad_ref[1, lo:end, :] = jnp.where(left, grad_keys[0], grad_keys[1]) * scale
        grad_ref[2, lo:end, :] = jnp.where(left, grad_values[0], grad_values[1])
    grad_ref[0, :, :] = jnp.transpose(dq_ref[...], (1, 0)) * scale
    for c in range(3):
        mixed = grad_ref[c]
        proj = proj_ref[c].astype(F32)
        one_up = pltpu.roll(mixed * mask_ref[0], slots - 1, 0)
        two_up = pltpu.roll(mixed * mask_ref[1], slots - 2, 0)
        gtaps_ref[c, 0:1, :] = jnp.sum(mixed * proj, axis=0, keepdims=True)
        gtaps_ref[c, 1:2, :] = jnp.sum(one_up * proj, axis=0, keepdims=True)
        gtaps_ref[c, 2:3, :] = jnp.sum(two_up * proj, axis=0, keepdims=True)
        gproj_ref[c] = (
            taps_ref[c, 0:1, :] * mixed + taps_ref[c, 1:2, :] * one_up + taps_ref[c, 2:3, :] * two_up
        ).astype(BF)


def post_body(count, place_ref, *refs):
    pieces, low_ref = refs[:count], refs[count]
    mine_ref, lows_ref, highs_ref, gw_ref, lowt_ref, sems = refs[count + 1 :]
    width = low_ref.shape[1]
    step = pl.program_id(0)

    @pl.when(step == 0)
    def _():
        lowt_ref[...] = jnp.transpose(low_ref[...], (1, 0))

    here = pl.multiple_of(step * width, width)
    at = 0
    for ref in pieces:
        lanes = ref.shape[1]
        gw_ref[pl.ds(here, width), at : at + lanes] = dot(lowt_ref[...], ref[...]).astype(BF)
        at += lanes

    @pl.when(step == 2)
    def _():
        size = mine_ref.shape[1]

        core = place_ref[PLACE_CORE]
        for j in range(8):
            other = lows_ref.at[j // 2] if j < 4 else highs_ref.at[j // 2 - 2]
            rows = gw_ref.at[pl.ds(j * size, size)]

            @pl.when(core == j % 2)
            def _():
                pltpu.make_async_copy(rows, mine_ref.at[j // 2], sems.at[0]).start()

            @pl.when(core != j % 2)
            def _():
                pltpu.make_async_copy(rows, other, sems.at[1 + j // 4]).start()

        wait_all(mine_ref, sems.at[0])
        wait_all(lows_ref, sems.at[1])
        wait_all(highs_ref, sems.at[2])


def back_body(place_ref, *refs):
    own, near = refs[-21:-13], refs[-13:-5]
    out_ref, all_ref, dvec_ref, w_ref, sem = refs[-5:]
    x_ref, gres_ref, vec_ref, two_ref = refs[-25:-21]
    count = (len(refs) - 25) // 2
    grads, taps = refs[:count], refs[count : 2 * count]
    width = x_ref.shape[1]

    @pl.when(pl.program_id(0) == 0)
    def _():
        start_qkv(place_ref, own, near, w_ref, sem)
        dvec_ref[...] = jnp.zeros_like(dvec_ref)
        wait_all(w_ref, sem)

    incoming = None
    for c in range(3):
        rows = slice(c * width, (c + 1) * width)
        at = 0
        for grad in grads:
            lanes = grad.shape[2]
            term = dot_nt(grad[c], w_ref[rows, at : at + lanes])
            incoming = term if incoming is None else incoming + term
            at += lanes
    normed, scaled = normalize(x_ref[...].astype(F32))
    out_ref[...] = gres_ref[...] + norm_back(incoming, normed, scaled, vec_ref[0:1, :])
    dvec_ref[0:1, :] += jnp.sum(incoming * normed, axis=0, keepdims=True)
    dvec_ref[1:2, :] += jnp.sum(incoming, axis=0, keepdims=True)

    @pl.when(pl.program_id(0) == pl.num_programs(0) - 1)
    def _():
        all_ref[...] = jnp.zeros_like(all_ref)
        rows = [dvec_ref[0:1, :], dvec_ref[1:2, :], two_ref[0:1, :], two_ref[1:2, :]]
        for c in range(3):
            for k in range(3):
                rows.append(jnp.concatenate([tap[c, k : k + 1, :] for tap in taps], axis=1))
        pieces = width // LANES
        for n, row in enumerate(rows):
            for part in range(pieces):
                at = n * pieces + part
                all_ref[at // VROWS, at % VROWS : at % VROWS + 1, :] = row[
                    :, part * LANES : (part + 1) * LANES
                ]


def forward(place, tokens, meta, own, near, vec, taps):
    slots, width = tokens.shape
    pairs = width // LANES
    scale = (width // HEADS) ** (-0.5)
    three = pl.BlockSpec((None, slots, width), lambda c, *_: (c, 0, 0))
    tap = pl.BlockSpec((None, 3, width), lambda c, *_: (c, 0, 0))
    low_one, mixed, project = call(
        pre_body,
        (3,),
        [whole((slots, width)), whole(vec.shape), tap, whole(meta.shape)] + [HBM] * 16,
        [whole((slots, width)), three, three],
        [like((slots, width), BF), like((3, slots, width), BF), like((3, slots, width), BF)],
        [
            pltpu.VMEM((3 * width, width), BF),
            pltpu.VMEM((slots, width), F32),
            pltpu.SemaphoreType.DMA,
        ],
        (tokens, vec, taps, meta, *own, *near),
        6 * slots * width * width,
        24 << 20,
        place,
        room=60,
    )
    lane_block = pl.BlockSpec((slots, LANES), lambda p: (0, p))

    def part(c):
        return pl.BlockSpec((None, slots, LANES), lambda p: (c, 0, p))

    attended, lse = call(
        functools.partial(attend_body, scale),
        (pairs,),
        [part(0), part(1), part(2), whole(meta.shape)],
        [lane_block, lane_block],
        [like((slots, width), BF), like((slots, width), F32)],
        [pltpu.VMEM((BLOCK, BLOCK), F32)]
        + [pltpu.VMEM((slots, LANES), BF)] * 2
        + [pltpu.VMEM((2, slots, LANES), BF)] * 3,
        (mixed, mixed, mixed, meta),
        2 * slots * slots * width * 2,
        12 << 20,
        room=60,
    )
    return low_one, mixed, project, attended, lse


def dense_up(place, tokens, grad_out, meta, attended, bufs, vec):
    slots, width = tokens.shape
    hidden = FOLD * width
    size = bufs[0].shape[0]
    blocks = slots // SPAN
    row_block = pl.BlockSpec((SPAN, width), lambda i, *_: (jnp.minimum(i, blocks - 1), 0))
    wide_block = pl.BlockSpec((SPAN, hidden), lambda i, *_: (jnp.minimum(i, blocks - 1), 0))
    meta_block = pl.BlockSpec((8, SPAN), lambda i, *_: (0, jnp.minimum(i, blocks - 1)))
    skip = hidden - 8 * size
    return call(
        up_body,
        (blocks + FOLD,),
        [row_block] * 3 + [meta_block, whole(vec.shape)] + [HBM] * 24,
        [row_block, row_block, row_block, wide_block, HBM, HBM, whole((skip, width))],
        [
            like((slots, width), F32),
            like((slots, width), BF),
            like((slots, width), BF),
            like((slots, hidden), BF),
            like((4, size, width), BF),
            like((4, size, width), BF),
            like((skip, width), BF),
        ],
        [
            pltpu.VMEM((width, width), BF),
            pltpu.VMEM((width, hidden), BF),
            pltpu.VMEM((slots, hidden), BF),
            pltpu.VMEM((slots, width), BF),
            pltpu.VMEM((hidden, width), BF),
            pltpu.SemaphoreType.DMA((3,)),
        ],
        (attended, tokens, grad_out, meta, vec, *bufs),
        (4 * FOLD + 2) * slots * width * width,
        30 << 20,
        place,
        room=60,
    )


def dense_down(place, attended, low, residual, cot, active, vec, first, bufs):
    slots, width = residual.shape
    hidden = FOLD * width
    size = bufs[0].shape[0]
    blocks = slots // SPAN
    row_block = pl.BlockSpec((SPAN, width), lambda i, *_: (jnp.minimum(i, blocks - 1), 0))
    wide_block = pl.BlockSpec((SPAN, hidden), lambda i, *_: (jnp.minimum(i, blocks - 1), 0))
    full = fixed((slots, width))
    return call(
        down_body,
        (blocks + FOLD,),
        [full, full, row_block, row_block, wide_block, whole(vec.shape), whole(first.shape)]
        + [HBM] * 24,
        [row_block, row_block, row_block, whole((8, width)), HBM, HBM],
        [
            like((slots, width), BF),
            like((slots, width), BF),
            like((slots, width), F32),
            like((8, width), F32),
            like((4, 2, size, width), BF),
            like((4, 2, size, width), BF),
        ],
        [
            pltpu.VMEM((width, width), BF),
            pltpu.VMEM((width, hidden), BF),
            pltpu.VMEM((hidden, width), BF),
            pltpu.VMEM((slots, hidden), BF),
            pltpu.VMEM((slots, width), BF),
            pltpu.VMEM((FOLD, width, width), BF),
            pltpu.VMEM((width, width), BF),
            pltpu.SemaphoreType.DMA((3,)),
        ],
        (attended, low, residual, cot, active, vec, first, *bufs),
        (8 * FOLD + 4) * slots * width * width,
        36 << 20,
        place,
        room=60,
    )


def attend_back(half, mixed, grad_att, attended, lse, meta, project, taps):
    slots, width = grad_att.shape
    at, count = half
    lane_block = pl.BlockSpec((slots, LANES), lambda p: (0, p + at))

    def part(c):
        return pl.BlockSpec((None, slots, LANES), lambda p: (c, 0, p + at))

    return call(
        functools.partial(attend_back_body, (width // HEADS) ** (-0.5)),
        (count,),
        [part(0), part(1), part(2), lane_block, lane_block, lane_block, whole(meta.shape)]
        + [
            pl.BlockSpec((3, slots, LANES), lambda p: (0, 0, p + at)),
            pl.BlockSpec((3, 3, LANES), lambda p: (0, 0, p + at)),
        ],
        [
            pl.BlockSpec((3, slots, LANES), lambda p: (0, 0, p)),
            pl.BlockSpec((3, 3, LANES), lambda p: (0, 0, p)),
        ],
        [like((3, slots, count * LANES), BF), like((3, 3, count * LANES), F32)],
        [
            pltpu.VMEM((3, slots, LANES), F32),
            pltpu.VMEM((2, slots, LANES), F32),
            pltpu.VMEM((slots, slots), F32),
            pltpu.VMEM((2, slots, LANES), BF),
            pltpu.VMEM((2, slots, LANES), BF),
            pltpu.VMEM((2, slots, LANES), BF),
            pltpu.VMEM((2, slots, LANES), BF),
            pltpu.VMEM((LANES, slots), BF),
            pltpu.VMEM((LANES, slots), F32),
        ],
        (mixed, mixed, mixed, grad_att, attended, lse, meta, project, taps),
        10 * slots * slots * count * LANES,
        20 << 20,
        room=60,
    )


def post(place, grads, low, size):
    slots, width = low.shape
    lanes = sum(g.shape[2] for g in grads)
    return call(
        functools.partial(post_body, len(grads)),
        (3,),
        [pl.BlockSpec((None, *g.shape[1:]), lambda c, *_: (c, 0, 0)) for g in grads]
        + [whole((slots, width))],
        [HBM] * 3,
        [like((n, size, lanes), BF) for n in (4, 2, 2)],
        [
            pltpu.VMEM((3 * width, lanes), BF),
            pltpu.VMEM((width, slots), BF),
            pltpu.SemaphoreType.DMA((3,)),
        ],
        (*grads, low),
        6 * slots * width * lanes,
        24 << 20,
        place,
        room=20,
    )


def back(place, grads, taps, tokens, grad_res, vec, dvec_two, own, near):
    slots, width = tokens.shape
    row_block = pl.BlockSpec((BLOCK, width), lambda i, *_: (i, 0))
    specs = [pl.BlockSpec((3, BLOCK, g.shape[2]), lambda i, *_: (0, i, 0)) for g in grads]
    specs += [whole(tap.shape) for tap in taps]
    return call(
        back_body,
        (slots // BLOCK,),
        specs + [row_block, row_block, whole(vec.shape), whole(dvec_two.shape)] + [HBM] * 16,
        [row_block, whole((SHARDS, 8, LANES))],
        [like((slots, width), F32), like((SHARDS, 8, LANES), F32)],
        [
            pltpu.VMEM((8, width), F32),
            pltpu.VMEM((3 * width, width), BF),
            pltpu.SemaphoreType.DMA,
        ],
        (*grads, *taps, tokens, grad_res, vec, dvec_two, *own, *near),
        6 * slots * width * width,
        1,
        place,
        0,
        room=60,
    )


def split_core(place, mine, received):
    block = mine.shape[1:]
    return call(
        route_body,
        (1,),
        [whole(mine.shape)] * 2,
        [whole(block)] * 4,
        [like(block, BF)] * 4,
        [],
        (mine, received),
        0,
        3 * mine.size * 2,
        place,
        room=16,
    )


def in_plane(routed):
    return [routed[0]] + [swap(routed[r], 2 * r) for r in range(1, 4)]


def lift(place, blocks):
    shape = blocks.shape[2:]
    return call(
        lift_body,
        (1,),
        [whole(blocks.shape)],
        [whole(shape)] * 4,
        [like(shape, BF)] * 4,
        [],
        (blocks,),
        0,
        3 * blocks.size,
        place,
        0,
    )


def send_planes(total, target):
    return [total] + [
        swap(total, 8 * k, lambda i, k=k: plane_of(i) ^ k == target) for k in (1, 2, 3)
    ]


def add_four(parts):
    shape = parts[0].shape
    return call(
        sum_body,
        (1,),
        [whole(shape)] * 4,
        whole(shape),
        like(shape, BF),
        [],
        parts,
        0,
        10 * parts[0].size,
        weight=0,
    )


def prepare(place, matrices, width):
    rows, roww = matrices.shape
    size = rows * roww // width
    return call(
        prep_body,
        (1,),
        [whole((rows, roww))],
        whole((size, width)),
        like((size, width), BF),
        [pltpu.VMEM((rows, roww), F32)],
        (matrices,),
        0,
        4 * matrices.size,
        place,
    )


def finish(place, sums, rows, roww):
    size, width = sums[-1].shape
    return call(
        finish_body,
        (1,),
        [whole(part.shape) for part in sums],
        whole((rows, roww)),
        like((rows, roww), F32),
        [pltpu.VMEM((size, width), F32)],
        sums,
        0,
        28 * size * width,
        place,
    )


def after(value, *deps):
    return lax.optimization_barrier((value, *deps))


def meta_rows(seq_start, valid):
    zeros = jnp.zeros((6, seq_start.shape[0]), F32)
    return jnp.concatenate([seq_start.astype(F32)[None], valid.astype(F32)[None], zeros], axis=0)


def split_vectors(vec_flat, width):
    vec = vec_flat[: 13 * width].reshape(13, width)
    return vec[:8], vec[4:13].reshape(3, 3, width)


def per_device(tokens_in, grad_out, seq_start, valid, matrices, vectors):
    width = tokens_in.shape[1]
    rows, roww = matrices.shape
    linear = lax.axis_index(FINE)
    plane = plane_of(linear)
    place = (linear >> jnp.array([0, 3, 0, 1, 0])) & jnp.array([31, 3, 7, 3, 1])
    near_planes = jnp.stack([1 - jnp.minimum(plane, 1), 2 - plane // 2, 3 - plane // 3])
    place = jnp.concatenate([place, near_planes])
    meta = meta_rows(seq_start, valid)
    shard = prepare(place, matrices, width)

    def up(value, steps, keep):
        pairs = [(i, i + 8 * steps) for i in range(SHARDS) if plane_of(i) in keep]
        return lax.ppermute(value, FINE, pairs)

    def with_partner(chips):
        bufs = []
        for chip in chips:
            bufs += [chip, swap(chip, 1)]
        return bufs

    def spread(held):
        by_y, by_x = swap(held, 2), swap(held, 4)
        return [held, by_y, by_x, swap(held, 6)]

    pairs = [(i, i + 16) for i in range(8)] + [(i, i + 8) for i in range(16, 24)]
    jump = lax.ppermute(shard, FINE, pairs)
    left_one = up(shard, -1, (1, 2, 3))
    own_y, own_x, own_both = spread(shard)[1:]
    jump, own_y, own_x = after(jump, own_y, own_x)
    hop = up(jnp.where(plane == 2, jump, shard), 1, (0, 1, 2))
    left_two = up(left_one, -1, (2, 1))
    near_one = jnp.where(plane == 0, left_one, jnp.where(plane == 2, jump, hop))
    near_one, hop, vectors_later, own_both = after(near_one, hop, vectors, own_both)
    own_chips = [shard, own_y, own_x, own_both]
    vec_flat = lax.all_to_all(jnp.tile(vectors_later, (SHARDS, 1)), FINE, 0, 0, tiled=True)
    near_chips = spread(near_one)
    left_three = up(left_two, -1, (1,))
    right_two = up(hop, 1, (2,))
    low = jnp.where(plane == 1, left_one, jnp.where(plane == 2, hop, right_two))
    low = jnp.where(plane == 0, left_two, low)
    high = jnp.where(plane == 1, left_two, jnp.where(plane == 2, left_one, jump))
    high = jnp.where(plane == 0, left_three, high)
    far, *near_chips = after(jnp.stack([low, high]), *near_chips)
    far_chips = spread(far)
    own = with_partner(own_chips)
    near = with_partner(near_chips)
    vec_flat = vec_flat.reshape(-1).astype(F32)
    vec, taps = split_vectors(vec_flat, width)
    low_one, mixed, project, attended, lse = forward(place, tokens_in, meta, own, near, vec, taps)
    attended, *far_chips = after(attended, *far_chips)
    far = with_partner(far_chips)
    bufs = (*own, *near, *far)
    residual, low_two, cot, active, mine, other, first = dense_up(
        place, tokens_in, grad_out, meta, attended, bufs, vec
    )

    def to_plane(parts, target):
        total = add_four(parts)
        return [total] + [
            swap(total, 8 * k, lambda i, k=k: plane_of(i) ^ k == target) for k in (1, 2, 3)
        ]

    def to_square(mine, other):
        return (mine.astype(F32) + other.astype(F32)).astype(BF)

    def exchange(blocks):
        return lax.all_to_all(blocks, SQUARE, 0, 0, tiled=True)

    def summed(blocks):
        return blocks.astype(F32).sum(axis=0).astype(BF)

    residual, highs = after(residual, to_square(mine, swap(other, 1)))
    highs = exchange(highs)
    block_out, grad_att, grad_res, dvec_two, mine, other = dense_down(
        place, attended, low_two, residual, cot, active, vec, first, bufs
    )
    grad_att, highs = after(grad_att, summed(highs))
    high_sums = send_planes(highs, 3)
    received = swap(other, 1)
    grads_one, taps_one = attend_back(
        PIECES[0], mixed, grad_att, attended, lse, meta, project, taps
    )
    grads_one, received, grad_att = after(grads_one, received, grad_att)
    grad_att, lows = after(grad_att, to_square(mine, received))
    lows = exchange(lows)
    grads_two, taps_two = attend_back(
        PIECES[1], mixed, grad_att, attended, lse, meta, project, taps
    )
    size = shard.shape[0]
    mine, *other = post(place, (grads_one, grads_two), low_one, size)
    grad_att, taps_two, *high_sums = after(grad_att, taps_two, *high_sums)
    received = [swap(part, 1) for part in other]
    grads_b, taps_b = attend_back(HALVES[1], mixed, grad_att, attended, lse, meta, project, taps)
    mine_b, *other = post(place, (grads_b,), low_one, size)
    mine_b, lows, *more = after(mine_b, lows, *other, *received)
    other, received = more[:2], more[2:]
    square_a = to_square(mine, jnp.concatenate(received))
    square_b = to_square(mine_b, jnp.concatenate([swap(part, 1) for part in other]))
    qkv = exchange(jnp.concatenate([square_a, square_b], axis=-1))
    lifted = lift(place, lows)
    grads_b, *lifted = after(grads_b, *lifted)
    low_sums = [lifted[0]] + [
        swap(lifted[k], 8 * k, lambda i, k=k: plane_of(i) ^ k in (1, 2)) for k in (1, 2, 3)
    ]
    tokens_grad, grad_vec = back(
        place, (grads_one, grads_two, grads_b), (taps_one, taps_two, taps_b),
        tokens_in, grad_res, vec, dvec_two, own, near,
    )
    grad_vec, qkv, low_sums[1], low_sums[3] = after(grad_vec, qkv, low_sums[1], low_sums[3])
    grad_vec, qkv = after(grad_vec, summed(qkv))
    owned_vec = lax.all_to_all(grad_vec.reshape(-1, roww), FINE, 0, 0, tiled=True)
    sums = send_planes(qkv, 0)
    owned_vec, *sums = after(owned_vec, *sums)
    owned = finish(place, (*sums, *low_sums, *high_sums), rows, roww)
    owned_vec = owned_vec.reshape(SHARDS, -1, roww).sum(axis=0)[: vectors.shape[0]]
    return block_out, tokens_grad, owned, owned_vec


def per_device_any(tokens_in, grad_out, seq_start, valid, matrices, vectors):
    width = tokens_in.shape[1]
    rows, roww = matrices.shape
    step = GROUP // FOLD
    place = jnp.array([0, 0, 0, 0, 0, 1, 2, 3], jnp.int32)
    meta = meta_rows(seq_start, valid)
    view = lax.all_gather(matrices, AXES, axis=0, tiled=True).reshape(-1, width)
    vec_flat = lax.all_gather(vectors, AXES, axis=0, tiled=True).reshape(-1).astype(F32)
    vec, taps = split_vectors(vec_flat, width)
    cut = (UP_FIRST * GROUP, UP_END * GROUP)
    up = view[cut[0] : cut[1]].reshape(UP_GROUPS, step, FOLD, width).swapaxes(1, 2)
    view = jnp.concatenate([view[: cut[0]], up.reshape(-1, width), view[cut[1] :]])
    shards = view.reshape(4, 8, -1, width)
    own = [shards[0, r] for r in range(8)]
    near = [shards[1, r] for r in range(8)]
    far = [shards[2:, r] for r in range(8)]
    low_one, mixed, project, attended, lse = forward(place, tokens_in, meta, own, near, vec, taps)
    bufs = (*own, *near, *far)
    residual, low_two, cot, active, mine_three, other_three, first = dense_up(
        place, tokens_in, grad_out, meta, attended, bufs, vec
    )
    block_out, grad_att, grad_res, dvec_two, mine_low, other_low = dense_down(
        place, attended, low_two, residual, cot, active, vec, first, bufs
    )
    qkv, grad_taps, grads = [], [], []
    for half in HALVES:
        grad, grad_tap = attend_back(
            half, mixed, grad_att, attended, lse, meta, project, taps
        )
        mine, *other = post(place, (grad,), low_one, own[0].shape[0])
        qkv.append(jnp.stack([mine, jnp.concatenate(other)], axis=1))
        grad_taps.append(grad_tap)
        grads.append(grad)
    tokens_grad, grad_vec = back(
        place, grads, grad_taps, tokens_in, grad_res, vec, dvec_two, own, near
    )
    planes = [
        jnp.concatenate(qkv, axis=-1)[:, :, None],
        jnp.stack([mine_low, other_low], axis=1),
        jnp.stack([mine_three, other_three], axis=1)[:, :, None],
    ]
    grad = jnp.concatenate(planes, axis=2)
    grad = grad.transpose(2, 0, 1, 3, 4).reshape(-1, width)
    up = grad[cut[0] : cut[1]].reshape(UP_GROUPS, FOLD, step, width).swapaxes(1, 2)
    grad = jnp.concatenate([grad[: cut[0]], up.reshape(-1, width), grad[cut[1] :]])
    owned = lax.psum_scatter(
        grad.reshape(-1, roww).astype(F32), AXES, scatter_dimension=0, tiled=True
    )
    grad_vec = grad_vec[:, :VROWS].reshape(-1, roww)
    total = vec_flat.size // roww
    grad_vec = jnp.pad(grad_vec, ((0, max(0, total - grad_vec.shape[0])), (0, 0)))[:total]
    owned_vec = lax.psum_scatter(grad_vec, AXES, scatter_dimension=0, tiled=True)
    return block_out, tokens_grad, owned, owned_vec


def solution(mesh):
    body, axes = per_device_any, AXES
    if mesh.devices.size == SHARDS:
        mesh = Mesh(mesh.devices.reshape(4, 2, 2, 2), FINE)
        body, axes = per_device, FINE
    row = P(axes, None)
    flat = P(axes)
    return jax.shard_map(
        body,
        mesh=mesh,
        in_specs=(row, row, flat, flat, row, row),
        out_specs=(row, row, row, row),
        check_vma=False,
    )
```

```python
import functools

import jax
import jax.numpy as jnp
from jax import lax
from jax.experimental import pallas as pl
from jax.experimental.pallas import tpu as pltpu
from jax.sharding import Mesh
from jax.sharding import PartitionSpec as P

HEADS = 12
EPSILON = 1e-05
NEG_FILL = -1e30
BF = jnp.bfloat16
F32 = jnp.float32
AXES = ("dp", "sub")
FINE = ("z", "x", "y", "core")
SQUARE = ("x", "y")
LANES = 128
BLOCK = 256
SPAN = 512
GROUP = 96
FOLD = 4
SHARDS = 32
WEIGHT = 100
VROWS = 3
OUT_GROUPS = 8
UP_GROUPS = 32
UP_FIRST, UP_END = 32, 64
HALVES = ((0, 4), (4, 2))
PIECES = ((0, 2), (2, 2))
(
    PLACE_LINEAR, PLACE_Z, PLACE_IN_PLANE, PLACE_XY, PLACE_CORE,
    PLACE_NEAR, PLACE_LOW, PLACE_HIGH,
) = range(8)
HBM = pl.BlockSpec(memory_space=pl.ANY)


def dot(a, b):
    return jnp.dot(a, b, preferred_element_type=F32)


def dot_nt(a, b):
    return lax.dot_general(a, b, (((1,), (1,)), ((), ())), preferred_element_type=F32)


def dot_tn(a, b):
    return lax.dot_general(a, b, (((0,), (0,)), ((), ())), preferred_element_type=F32)


def whole(shape):
    return pl.BlockSpec(shape, lambda *_: (0,) * len(shape))


def fixed(shape):
    return pl.BlockSpec(shape, lambda *_: (0,) * len(shape), pipeline_mode=pl.Buffered(1))


def call(body, grid, ins, outs, out_shape, scratch, args, flops, moved, place=None, weight=WEIGHT, room=16):
    return pl.pallas_call(
        body,
        grid_spec=pltpu.PrefetchScalarGridSpec(
            num_scalar_prefetch=0 if place is None else 1,
            grid=grid,
            in_specs=ins,
            out_specs=outs,
            scratch_shapes=scratch,
        ),
        out_shape=out_shape,
        compiler_params=pltpu.CompilerParams(
            dimension_semantics=("arbitrary",) * len(grid), vmem_limit_bytes=room << 20
        ),
        cost_estimate=pl.CostEstimate(
            flops=weight * flops, bytes_accessed=weight * moved, transcendentals=0
        ),
    )(*(() if place is None else (place,)), *args)


def like(shape, dtype):
    return jax.ShapeDtypeStruct(shape, dtype)


def normalize(v):
    centre = v - jnp.mean(v, axis=-1, keepdims=True)
    scaled = lax.rsqrt(jnp.mean(centre * centre, axis=-1, keepdims=True) + EPSILON)
    return centre * scaled, scaled


def norm_back(incoming, normed, scaled, gain):
    weighted = incoming * gain
    return scaled * (
        weighted
        - jnp.mean(weighted, axis=-1, keepdims=True)
        - normed * jnp.mean(weighted * normed, axis=-1, keepdims=True)
    )


def columns(meta):
    return jnp.transpose(meta, (1, 0))


def mix_masks(meta_ref, slots):
    cols = columns(meta_ref[...])
    position = lax.broadcasted_iota(jnp.int32, (slots, 1), 0).astype(F32) - cols[:, 0:1]
    return jnp.where(position >= 1.0, 1.0, 0.0), jnp.where(position >= 2.0, 1.0, 0.0)


def xor_pairs(mask, keep=None):
    return [(i, i ^ mask) for i in range(SHARDS) if keep is None or keep(i)]


def swap(value, mask, keep=None):
    return lax.ppermute(value, FINE, xor_pairs(mask, keep))


def plane_of(index):
    return index >> 3


def prep_body(place_ref, in_ref, out_ref, wide_ref):
    width = out_ref.shape[1]
    cols = width // LANES
    wide_ref[...] = in_ref[...].astype(F32)
    first = place_ref[PLACE_LINEAR] * (out_ref.shape[0] // GROUP)
    for n in range(out_ref.shape[0] // GROUP):
        base = n * GROUP * cols
        up = jnp.logical_and(first + n >= UP_FIRST, first + n < UP_END)

        @pl.when(up)
        def _():
            for j in range(cols):
                parts = [
                    wide_ref[pl.ds(base + q * cols + j, GROUP // FOLD, stride=cols * FOLD), :]
                    for q in range(FOLD)
                ]
                out_ref[n * GROUP : (n + 1) * GROUP, j * LANES : (j + 1) * LANES] = (
                    jnp.concatenate(parts, axis=0).astype(BF)
                )

        @pl.when(jnp.logical_not(up))
        def _():
            for j in range(cols):
                out_ref[n * GROUP : (n + 1) * GROUP, j * LANES : (j + 1) * LANES] = wide_ref[
                    pl.ds(base + j, GROUP, stride=cols), :
                ].astype(BF)


def finish_body(place_ref, *refs):
    zero, middle, last = refs[:4], refs[4:8], refs[8:12]
    out_ref, total_ref = refs[-2:]
    width = total_ref.shape[1]
    cols = width // LANES
    plane = place_ref[PLACE_Z]

    def add(parts):
        total = parts[0][...].astype(F32)
        for part in parts[1:]:
            total = total + part[...].astype(F32)
        return total

    @pl.when(plane == 0)
    def _():
        total_ref[...] = add(zero)

    @pl.when(jnp.logical_or(plane == 1, plane == 2))
    def _():
        total_ref[...] = add(middle)

    @pl.when(plane == 3)
    def _():
        total_ref[...] = add(last)

    first = place_ref[PLACE_LINEAR] * (total_ref.shape[0] // GROUP)
    for n in range(total_ref.shape[0] // GROUP):
        base = n * GROUP * cols
        up = jnp.logical_and(first + n >= UP_FIRST, first + n < UP_END)

        @pl.when(up)
        def _():
            step = GROUP // FOLD
            for j in range(cols):
                for q in range(FOLD):
                    lo = n * GROUP + q * step
                    out_ref[pl.ds(base + q * cols + j, step, stride=cols * FOLD), :] = total_ref[
                        lo : lo + step, j * LANES : (j + 1) * LANES
                    ]

        @pl.when(jnp.logical_not(up))
        def _():
            for j in range(cols):
                out_ref[pl.ds(base + j, GROUP, stride=cols), :] = total_ref[
                    n * GROUP : (n + 1) * GROUP, j * LANES : (j + 1) * LANES
                ]


def route_body(place_ref, mine_ref, other_ref, *outs):
    for r, out in enumerate(outs):
        at = place_ref[PLACE_XY] ^ r
        out[...] = (mine_ref[at].astype(F32) + other_ref[at].astype(F32)).astype(BF)


def lift_body(place_ref, in_ref, *outs):
    plane = place_ref[PLACE_Z]
    for k, out in enumerate(outs):
        p = jnp.clip(plane ^ k, 1, 2) - 1
        total = in_ref[0, p].astype(F32)
        for r in range(1, 4):
            total = total + in_ref[r, p].astype(F32)
        out[...] = total.astype(BF)


def sum_body(a_ref, b_ref, c_ref, d_ref, out_ref):
    out_ref[...] = (
        a_ref[...].astype(F32) + b_ref[...].astype(F32) + c_ref[...].astype(F32) + d_ref[...].astype(F32)
    ).astype(BF)


def start_qkv(place_ref, own, near, w_ref, sem):
    size = own[0].shape[0]
    for r in range(8):
        at = pl.multiple_of((place_ref[PLACE_IN_PLANE] ^ r) * size, 32)

        @pl.when(place_ref[PLACE_Z] == 0)
        def _():
            pltpu.make_async_copy(own[r], w_ref.at[pl.ds(at, size)], sem).start()

        @pl.when(place_ref[PLACE_Z] != 0)
        def _():
            pltpu.make_async_copy(near[r], w_ref.at[pl.ds(at, size)], sem).start()


def wait_all(ref, sem):
    pltpu.make_async_copy(ref, ref, sem).wait()


def start_dense(place_ref, own, near, far, wo_ref, w1_ref, w2_ref, sems):
    step = GROUP // FOLD
    width = own[0].shape[1]
    slots = [(own, None, PLACE_Z, (1, 2, 3)), (near, None, PLACE_NEAR, (1,))]
    slots += [(far, 0, PLACE_LOW, (1, 2)), (far, 1, PLACE_HIGH, (2, 3))]
    for bufs, slot, plane_at, planes in slots:
        for p in planes:

            @pl.when(place_ref[plane_at] == p)
            def _():
                for r in range(8):
                    buf = bufs[r] if slot is None else bufs[r].at[slot]
                    place = place_ref[PLACE_IN_PLANE] ^ r
                    for n in range(3):
                        group = 24 * (p - 1) + 3 * place + n
                        rows = buf.at[pl.ds(n * GROUP, GROUP)]

                        def to_out():
                            at = pl.multiple_of(group * GROUP, 32)
                            pltpu.make_async_copy(
                                rows, wo_ref.at[pl.ds(at, GROUP)], sems.at[0]
                            ).start()

                        def to_up():
                            at = pl.multiple_of((group - OUT_GROUPS) * step, 8)
                            for q in range(FOLD):
                                pltpu.make_async_copy(
                                    rows.at[pl.ds(q * step, step)],
                                    w1_ref.at[pl.ds(at, step), pl.ds(q * width, width)],
                                    sems.at[1],
                                ).start()

                        def to_down():
                            at = pl.multiple_of((group - OUT_GROUPS - UP_GROUPS) * GROUP, 32)
                            pltpu.make_async_copy(
                                rows, w2_ref.at[pl.ds(at, GROUP)], sems.at[2]
                            ).start()

                        if p == 1:
                            pl.when(group < OUT_GROUPS)(to_out)
                            pl.when(group >= OUT_GROUPS)(to_up)
                        elif p == 2:
                            pl.when(group < OUT_GROUPS + UP_GROUPS)(to_up)
                            if w2_ref is not None:
                                pl.when(group >= OUT_GROUPS + UP_GROUPS)(to_down)
                        elif w2_ref is not None:
                            to_down()


def deal(place_ref, targets, sems, copy):
    core = place_ref[PLACE_CORE]
    for j in range(8):
        for which in range(2):

            @pl.when(core ^ (j % 2) == which)
            def _():
                copy(j, targets[which].at[j // 2], sems.at[which])


def pre_body(place_ref, x_ref, vec_ref, taps_ref, meta_ref, *refs):
    own, near = refs[:8], refs[8:16]
    low_ref, mixed_ref, proj_ref, w_ref, keep_ref, sem = refs[16:]
    slots, width = x_ref.shape
    here = pl.multiple_of(pl.program_id(0) * width, width)

    @pl.when(pl.program_id(0) == 0)
    def _():
        start_qkv(place_ref, own, near, w_ref, sem)
        for lo in range(0, slots, BLOCK):
            rows = slice(lo, lo + BLOCK)
            normed, _ = normalize(x_ref[rows, :].astype(F32))
            low_ref[rows, :] = (normed * vec_ref[0:1, :] + vec_ref[1:2, :]).astype(BF)
        wait_all(w_ref, sem)

    first, second = mix_masks(meta_ref, slots)
    weight = w_ref[pl.ds(here, width), :]
    ahead = dot(low_ref[0:BLOCK, :], weight)
    for lo in range(0, slots, BLOCK):
        end = lo + BLOCK
        value = ahead
        if end < slots:
            ahead = dot(low_ref[end : end + BLOCK, :], weight)
        proj_ref[lo:end, :] = value.astype(BF)
        keep_ref[lo:end, :] = value
        one_back = pltpu.roll(value, 1, 0) if lo == 0 else keep_ref[lo - 1 : end - 1, :]
        two_back = pltpu.roll(value, 2, 0) if lo == 0 else keep_ref[lo - 2 : end - 2, :]
        mixed_ref[lo:end, :] = (
            taps_ref[0:1, :] * value
            + taps_ref[1:2, :] * (one_back * first[lo:end])
            + taps_ref[2:3, :] * (two_back * second[lo:end])
        ).astype(BF)


def mask_columns(cols):
    lane = lax.broadcasted_iota(jnp.int32, (1, LANES), 1) % (LANES // 2)
    bucket = (lane >= 16) & (lane < 32)
    same = cols[:, 0:1] * (1.0 / 64.0) == (lane - 16).astype(F32)
    query = jnp.where(bucket & same, 0.0, jnp.where((lane >= 16) & (lane <= 32), NEG_FILL, 0.0))
    key = jnp.where(bucket & same, 1.0, jnp.where(lane == 32, 1.0 - cols[:, 1:2], 0.0))
    return query.astype(BF), key.astype(BF)


def triangle(lower):
    row = lax.broadcasted_iota(jnp.int32, (BLOCK, BLOCK), 0)
    col = lax.broadcasted_iota(jnp.int32, (BLOCK, BLOCK), 1)
    return jnp.where(col <= row if lower else row <= col, 0.0, NEG_FILL)


def attend_body(
    scale, q_ref, k_ref, v_ref, meta_ref, out_ref, lse_ref,
    tri_ref, qm_ref, km_ref, qa_ref, ka_ref, va_ref,
):
    slots = q_ref.shape[0]
    half = LANES // 2

    @pl.when(pl.program_id(0) == 0)
    def _():
        tri_ref[...] = triangle(True)
        qm_ref[...], km_ref[...] = mask_columns(columns(meta_ref[...]))

    left = lax.broadcasted_iota(jnp.int32, (1, LANES), 1) < half
    query = q_ref[...] * jnp.asarray(scale, BF)
    one = jnp.ones_like(query)
    for head in range(2):
        own = left if head == 0 else jnp.logical_not(left)
        qa_ref[head] = jnp.where(own, query, qm_ref[...])
        ka_ref[head] = jnp.where(own, k_ref[...], km_ref[...])
        va_ref[head] = jnp.where(own, v_ref[...], one)
    stages = [(lo, head) for lo in range(0, slots, BLOCK) for head in range(2)]
    outs, logs = [], []

    def score(lo, head):
        return dot_nt(qa_ref[head, lo : lo + BLOCK, :], ka_ref[head, : lo + BLOCK, :])

    def finish_stage(lo, head, terms, peak):
        end = lo + BLOCK
        both = dot(terms, va_ref[head, :end, :])
        outs.append(both / pltpu.roll(both, half, 1))
        logs.append(peak + jnp.log(both))
        if head == 1:
            out_ref[lo:end, :] = jnp.where(left, outs[-2], outs[-1]).astype(BF)
            lse_ref[lo:end, :] = jnp.where(left, logs[-1], logs[-2])

    ahead = score(*stages[0])
    behind = None
    for n, (lo, head) in enumerate(stages):
        scores = ahead
        if n + 1 < len(stages):
            ahead = score(*stages[n + 1])
        if behind is not None:
            finish_stage(*behind)
        near = scores[:, lo:] + tri_ref[...]
        scores = jnp.concatenate([scores[:, :lo], near], axis=1) if lo else near
        peak = jnp.max(scores, axis=-1, keepdims=True)
        behind = (lo, head, jnp.exp(scores - peak).astype(BF), peak)
    finish_stage(*behind)


def up_body(place_ref, att_ref, x_ref, go_ref, meta_ref, vec_ref, *refs):
    own, near, far = refs[:8], refs[8:16], refs[16:24]
    (
        res_ref, low_ref, cot_ref, out_ref, mine_ref, other_ref, first_ref,
        wo_ref, w1_ref, act_ref, cots_ref, g2_ref, sems,
    ) = refs[24:]
    width = x_ref.shape[1]
    step = pl.program_id(0)
    blocks = act_ref.shape[0] // SPAN
    here = pl.multiple_of(step * SPAN, SPAN)

    @pl.when(step == 0)
    def _():
        start_dense(place_ref, own, near, far, wo_ref, w1_ref, None, sems)
        wait_all(wo_ref, sems.at[0])
        wait_all(w1_ref, sems.at[1])

    @pl.when(step < blocks)
    def _():
        live = columns(meta_ref[...])[:, 1:2]
        cot = (go_ref[...].astype(F32) * live).astype(BF)
        cot_ref[...] = cot
        cots_ref[pl.ds(here, SPAN), :] = cot
        pieces = range(0, SPAN, BLOCK)
        residuals = [
            x_ref[lo : lo + BLOCK, :].astype(F32) + dot(att_ref[lo : lo + BLOCK, :], wo_ref[...])
            for lo in pieces
        ]
        lows = []

        def norm(lo, residual):
            res_ref[lo : lo + BLOCK, :] = residual
            normed, _ = normalize(residual)
            low = (normed * vec_ref[2:3, :] + vec_ref[3:4, :]).astype(BF)
            low_ref[lo : lo + BLOCK, :] = low
            lows.append(low)

        norm(0, residuals[0])
        stages = [(at, part) for at in range(len(pieces)) for part in range(FOLD)]

        def project(at, part):
            return dot(lows[at], w1_ref[:, part * width : (part + 1) * width])

        ahead = project(0, 0)
        for n, (at, part) in enumerate(stages):
            upward = jnp.maximum(ahead, 0.0)
            if part == 0 and at + 1 < len(pieces):
                norm(pieces[at + 1], residuals[at + 1])
            if n + 1 < len(stages):
                ahead = project(*stages[n + 1])
            cut = slice(part * width, (part + 1) * width)
            rows = pl.ds(pl.multiple_of(here + at * BLOCK, BLOCK), BLOCK)
            active = (upward * upward).astype(BF)
            act_ref[rows, cut] = active
            out_ref[at * BLOCK : (at + 1) * BLOCK, cut] = active

    for part in range(FOLD):

        @pl.when(step == blocks + part)
        def _():
            cut = slice(part * width, (part + 1) * width)
            g2_ref[cut, :] = dot_tn(act_ref[:, cut], cots_ref[...]).astype(BF)

    @pl.when(step == blocks + FOLD - 1)
    def _():
        size = mine_ref.shape[1]
        skip = g2_ref.shape[0] - 8 * size

        def copy(j, target, sem):
            pltpu.make_async_copy(g2_ref.at[pl.ds(skip + j * size, size)], target, sem).start()

        deal(place_ref, (mine_ref, other_ref), sems, copy)
        first_ref[...] = g2_ref[0:skip, :]
        wait_all(mine_ref, sems.at[0])
        wait_all(other_ref, sems.at[1])


def down_body(
    place_ref, att_ref, low_ref, res_ref, cot_ref, act_ref, vec_ref, first_ref, *refs
):
    own, near, far = refs[:8], refs[8:16], refs[16:24]
    (
        out_ref, gatt_ref, gres_ref, dvec_ref, mine_ref, other_ref,
        wo_ref, w1_ref, w2_ref, up_ref, reslow_ref, g1_ref, go_ref, sems,
    ) = refs[24:]
    width = res_ref.shape[1]
    step = pl.program_id(0)
    blocks = up_ref.shape[0] // SPAN
    here = pl.multiple_of(step * SPAN, SPAN)

    @pl.when(step == 0)
    def _():
        start_dense(place_ref, own, near, far, wo_ref, w1_ref, w2_ref, sems)
        dvec_ref[...] = jnp.zeros_like(dvec_ref)
        wait_all(w2_ref, sems.at[2])

    @pl.when(step < blocks)
    def _():
        pieces = range(0, SPAN, BLOCK)
        stages = [(lo, part) for lo in pieces for part in range(FOLD)]

        def incoming(lo, part):
            return dot_nt(cot_ref[lo : lo + BLOCK, :], w2_ref[part * width : (part + 1) * width, :])

        ahead = incoming(*stages[0])
        for n, (lo, part) in enumerate(stages):
            grad_active = ahead
            if n + 1 < len(stages):
                ahead = incoming(*stages[n + 1])
            cut = slice(part * width, (part + 1) * width)
            upward = jnp.sqrt(act_ref[lo : lo + BLOCK, cut].astype(F32))
            rows = pl.ds(pl.multiple_of(here + lo, BLOCK), BLOCK)
            up_ref[rows, cut] = (grad_active * (2.0 * upward)).astype(BF)
        for lo in pieces:
            out = res_ref[lo : lo + BLOCK, :] + dot(act_ref[lo : lo + BLOCK, :], w2_ref[...])
            out_ref[lo : lo + BLOCK, :] = out.astype(BF)

    @pl.when(step == 0)
    def _():
        wait_all(w1_ref, sems.at[1])
        wait_all(wo_ref, sems.at[0])

    @pl.when(step < blocks)
    def _():
        pieces = range(0, SPAN, BLOCK)

        def outgoing(lo):
            return dot_nt(up_ref[pl.ds(pl.multiple_of(here + lo, BLOCK), BLOCK), :], w1_ref[...])

        ahead = outgoing(0)
        for lo in pieces:
            grad = ahead
            if lo + BLOCK < SPAN:
                ahead = outgoing(lo + BLOCK)
            span = slice(lo, lo + BLOCK)
            normed, scaled = normalize(res_ref[span, :])
            back = norm_back(grad, normed, scaled, vec_ref[2:3, :])
            grad_residual = cot_ref[span, :].astype(F32) + back
            gres_ref[span, :] = grad_residual
            res_low = grad_residual.astype(BF)
            reslow_ref[pl.ds(pl.multiple_of(here + lo, BLOCK), BLOCK), :] = res_low
            gatt_ref[span, :] = dot_nt(res_low, wo_ref[...]).astype(BF)
            dvec_ref[0:1, :] += jnp.sum(grad * normed, axis=0, keepdims=True)
            dvec_ref[1:2, :] += jnp.sum(grad, axis=0, keepdims=True)

    for part in range(FOLD):

        @pl.when(step == blocks + part)
        def _():
            cut = slice(part * width, (part + 1) * width)
            g1_ref[part] = dot_tn(low_ref[...], up_ref[:, cut]).astype(BF)

    @pl.when(step == blocks + FOLD - 1)
    def _():
        go_ref[...] = dot_tn(att_ref[...], reslow_ref[...]).astype(BF)
        span = GROUP // FOLD

        def copy(j, target, sem):
            for p in range(2):
                for n in range(3):
                    group = 24 * p + 3 * j + n
                    rows = target.at[p, pl.ds(n * GROUP, GROUP)]
                    if group < OUT_GROUPS:
                        source = go_ref.at[pl.ds(group * GROUP, GROUP)]
                    elif group < OUT_GROUPS + UP_GROUPS:
                        source = g1_ref.at[:, pl.ds((group - OUT_GROUPS) * span, span)]
                        rows = rows.reshape(FOLD, span, width)
                    else:
                        at = (group - OUT_GROUPS - UP_GROUPS) * GROUP
                        source = first_ref.at[pl.ds(at, GROUP)]
                    pltpu.make_async_copy(source, rows, sem).start()

        deal(place_ref, (mine_ref, other_ref), sems, copy)
        wait_all(mine_ref, sems.at[0])
        wait_all(other_ref, sems.at[1])


def split_three(value):
    high = value.astype(BF)
    rest = value - high.astype(F32)
    middle = rest.astype(BF)
    return high, middle, (rest - middle.astype(F32)).astype(BF)


def attend_back_body(
    scale, q_ref, k_ref, v_ref, do_ref, o_ref, lse_ref, meta_ref, proj_ref, taps_ref,
    gproj_ref, gtaps_ref, grad_ref, mask_ref, bias_ref, qa_ref, ka_ref, va_ref, da_ref, kt_ref, dq_ref,
):
    slots = q_ref.shape[0]
    half = LANES // 2

    @pl.when(pl.program_id(0) == 0)
    def _():
        cols = columns(meta_ref[...])
        for lo in range(0, slots, BLOCK):
            end = lo + BLOCK
            size = slots - lo
            row = lax.broadcasted_iota(jnp.int32, (BLOCK, size), 0)
            col = lax.broadcasted_iota(jnp.int32, (BLOCK, size), 1)
            keep = (
                (cols[lo:end, 0:1] == meta_ref[0:1, lo:])
                & (cols[lo:end, 1:2] > 0.5)
                & (row <= col)
            )
            bias_ref[lo:end, lo:] = jnp.where(keep, 0.0, NEG_FILL)
        for n, mask in enumerate(mix_masks(meta_ref, slots)):
            mask_ref[n] = jnp.broadcast_to(mask, (slots, LANES))

    lane = lax.broadcasted_iota(jnp.int32, (1, LANES), 1)
    left = lane < half
    query = q_ref[...]
    key = k_ref[...]
    value = v_ref[...]
    grad_out = do_ref[...]
    product = grad_out.astype(F32) * o_ref[...].astype(F32)
    kt_ref[...] = jnp.transpose(key.astype(F32), (1, 0)).astype(BF)
    logs = split_three(-lse_ref[...])
    zero = jnp.zeros_like(query)
    one = jnp.ones_like(query)
    for head in range(2):
        own = left if head == 0 else jnp.logical_not(left)
        base = half if head == 0 else 0
        delta = jnp.sum(jnp.where(own, product, 0.0), axis=-1, keepdims=True)
        deltas = split_three(-delta)
        marks = [lane == base + n for n in range(3)]

        def spread(terms):
            result = zero
            for mark, term in zip(marks, terms):
                result = jnp.where(mark, term, result)
            return result

        ones = spread((one, one, one))
        qa_ref[head] = jnp.where(own, query * jnp.asarray(scale, BF), spread(logs))
        ka_ref[head] = jnp.where(own, key, ones)
        va_ref[head] = jnp.where(own, value, ones)
        da_ref[head] = jnp.where(own, grad_out, spread(deltas))
    dq_ref[...] = jnp.zeros_like(dq_ref)
    for lo in range(0, slots, BLOCK):
        end = lo + BLOCK
        grad_keys, grad_values = [], []
        for head in range(2):
            rows = slice(head * half, (head + 1) * half)
            scores = dot_nt(ka_ref[head, lo:end, :], qa_ref[head, lo:, :]) + bias_ref[lo:end, lo:]
            probs = jnp.exp(scores)
            inner = dot_nt(va_ref[head, lo:end, :], da_ref[head, lo:, :])
            grad_scores = (probs * inner).astype(BF)
            grad_values.append(dot(probs.astype(BF), do_ref[lo:, :]))
            grad_keys.append(dot(grad_scores, q_ref[lo:, :]))
            dq_ref[rows, lo:] += dot(kt_ref[rows, lo:end], grad_scores)
        grad_ref[1, lo:end, :] = jnp.where(left, grad_keys[0], grad_keys[1]) * scale
        grad_ref[2, lo:end, :] = jnp.where(left, grad_values[0], grad_values[1])
    grad_ref[0, :, :] = jnp.transpose(dq_ref[...], (1, 0)) * scale
    for c in range(3):
        mixed = grad_ref[c]
        proj = proj_ref[c].astype(F32)
        one_up = pltpu.roll(mixed * mask_ref[0], slots - 1, 0)
        two_up = pltpu.roll(mixed * mask_ref[1], slots - 2, 0)
        gtaps_ref[c, 0:1, :] = jnp.sum(mixed * proj, axis=0, keepdims=True)
        gtaps_ref[c, 1:2, :] = jnp.sum(one_up * proj, axis=0, keepdims=True)
        gtaps_ref[c, 2:3, :] = jnp.sum(two_up * proj, axis=0, keepdims=True)
        gproj_ref[c] = (
            taps_ref[c, 0:1, :] * mixed + taps_ref[c, 1:2, :] * one_up + taps_ref[c, 2:3, :] * two_up
        ).astype(BF)


def post_body(count, place_ref, *refs):
    pieces, low_ref = refs[:count], refs[count]
    mine_ref, lows_ref, highs_ref, gw_ref, lowt_ref, sems = refs[count + 1 :]
    width = low_ref.shape[1]
    step = pl.program_id(0)

    @pl.when(step == 0)
    def _():
        lowt_ref[...] = jnp.transpose(low_ref[...], (1, 0))

    here = pl.multiple_of(step * width, width)
    at = 0
    for ref in pieces:
        lanes = ref.shape[1]
        gw_ref[pl.ds(here, width), at : at + lanes] = dot(lowt_ref[...], ref[...]).astype(BF)
        at += lanes

    @pl.when(step == 2)
    def _():
        size = mine_ref.shape[1]

        core = place_ref[PLACE_CORE]
        for j in range(8):
            other = lows_ref.at[j // 2] if j < 4 else highs_ref.at[j // 2 - 2]
            rows = gw_ref.at[pl.ds(j * size, size)]

            @pl.when(core == j % 2)
            def _():
                pltpu.make_async_copy(rows, mine_ref.at[j // 2], sems.at[0]).start()

            @pl.when(core != j % 2)
            def _():
                pltpu.make_async_copy(rows, other, sems.at[1 + j // 4]).start()

        wait_all(mine_ref, sems.at[0])
        wait_all(lows_ref, sems.at[1])
        wait_all(highs_ref, sems.at[2])


def back_body(place_ref, *refs):
    own, near = refs[-21:-13], refs[-13:-5]
    out_ref, all_ref, dvec_ref, w_ref, sem = refs[-5:]
    x_ref, gres_ref, vec_ref, two_ref = refs[-25:-21]
    count = (len(refs) - 25) // 2
    grads, taps = refs[:count], refs[count : 2 * count]
    width = x_ref.shape[1]

    @pl.when(pl.program_id(0) == 0)
    def _():
        start_qkv(place_ref, own, near, w_ref, sem)
        dvec_ref[...] = jnp.zeros_like(dvec_ref)
        wait_all(w_ref, sem)

    incoming = None
    for c in range(3):
        rows = slice(c * width, (c + 1) * width)
        at = 0
        for grad in grads:
            lanes = grad.shape[2]
            term = dot_nt(grad[c], w_ref[rows, at : at + lanes])
            incoming = term if incoming is None else incoming + term
            at += lanes
    normed, scaled = normalize(x_ref[...].astype(F32))
    out_ref[...] = gres_ref[...] + norm_back(incoming, normed, scaled, vec_ref[0:1, :])
    dvec_ref[0:1, :] += jnp.sum(incoming * normed, axis=0, keepdims=True)
    dvec_ref[1:2, :] += jnp.sum(incoming, axis=0, keepdims=True)

    @pl.when(pl.program_id(0) == pl.num_programs(0) - 1)
    def _():
        all_ref[...] = jnp.zeros_like(all_ref)
        rows = [dvec_ref[0:1, :], dvec_ref[1:2, :], two_ref[0:1, :], two_ref[1:2, :]]
        for c in range(3):
            for k in range(3):
                rows.append(jnp.concatenate([tap[c, k : k + 1, :] for tap in taps], axis=1))
        pieces = width // LANES
        for n, row in enumerate(rows):
            for part in range(pieces):
                at = n * pieces + part
                all_ref[at // VROWS, at % VROWS : at % VROWS + 1, :] = row[
                    :, part * LANES : (part + 1) * LANES
                ]


def forward(place, tokens, meta, own, near, vec, taps):
    slots, width = tokens.shape
    pairs = width // LANES
    scale = (width // HEADS) ** (-0.5)
    three = pl.BlockSpec((None, slots, width), lambda c, *_: (c, 0, 0))
    tap = pl.BlockSpec((None, 3, width), lambda c, *_: (c, 0, 0))
    low_one, mixed, project = call(
        pre_body,
        (3,),
        [whole((slots, width)), whole(vec.shape), tap, whole(meta.shape)] + [HBM] * 16,
        [whole((slots, width)), three, three],
        [like((slots, width), BF), like((3, slots, width), BF), like((3, slots, width), BF)],
        [
            pltpu.VMEM((3 * width, width), BF),
            pltpu.VMEM((slots, width), F32),
            pltpu.SemaphoreType.DMA,
        ],
        (tokens, vec, taps, meta, *own, *near),
        6 * slots * width * width,
        24 << 20,
        place,
        room=60,
    )
    lane_block = pl.BlockSpec((slots, LANES), lambda p: (0, p))

    def part(c):
        return pl.BlockSpec((None, slots, LANES), lambda p: (c, 0, p))

    attended, lse = call(
        functools.partial(attend_body, scale),
        (pairs,),
        [part(0), part(1), part(2), whole(meta.shape)],
        [lane_block, lane_block],
        [like((slots, width), BF), like((slots, width), F32)],
        [pltpu.VMEM((BLOCK, BLOCK), F32)]
        + [pltpu.VMEM((slots, LANES), BF)] * 2
        + [pltpu.VMEM((2, slots, LANES), BF)] * 3,
        (mixed, mixed, mixed, meta),
        2 * slots * slots * width * 2,
        12 << 20,
        room=60,
    )
    return low_one, mixed, project, attended, lse


def dense_up(place, tokens, grad_out, meta, attended, bufs, vec):
    slots, width = tokens.shape
    hidden = FOLD * width
    size = bufs[0].shape[0]
    blocks = slots // SPAN
    row_block = pl.BlockSpec((SPAN, width), lambda i, *_: (jnp.minimum(i, blocks - 1), 0))
    wide_block = pl.BlockSpec((SPAN, hidden), lambda i, *_: (jnp.minimum(i, blocks - 1), 0))
    meta_block = pl.BlockSpec((8, SPAN), lambda i, *_: (0, jnp.minimum(i, blocks - 1)))
    skip = hidden - 8 * size
    return call(
        up_body,
        (blocks + FOLD,),
        [row_block] * 3 + [meta_block, whole(vec.shape)] + [HBM] * 24,
        [row_block, row_block, row_block, wide_block, HBM, HBM, whole((skip, width))],
        [
            like((slots, width), F32),
            like((slots, width), BF),
            like((slots, width), BF),
            like((slots, hidden), BF),
            like((4, size, width), BF),
            like((4, size, width), BF),
            like((skip, width), BF),
        ],
        [
            pltpu.VMEM((width, width), BF),
            pltpu.VMEM((width, hidden), BF),
            pltpu.VMEM((slots, hidden), BF),
            pltpu.VMEM((slots, width), BF),
            pltpu.VMEM((hidden, width), BF),
            pltpu.SemaphoreType.DMA((3,)),
        ],
        (attended, tokens, grad_out, meta, vec, *bufs),
        (4 * FOLD + 2) * slots * width * width,
        30 << 20,
        place,
        room=60,
    )


def dense_down(place, attended, low, residual, cot, active, vec, first, bufs):
    slots, width = residual.shape
    hidden = FOLD * width
    size = bufs[0].shape[0]
    blocks = slots // SPAN
    row_block = pl.BlockSpec((SPAN, width), lambda i, *_: (jnp.minimum(i, blocks - 1), 0))
    wide_block = pl.BlockSpec((SPAN, hidden), lambda i, *_: (jnp.minimum(i, blocks - 1), 0))
    full = fixed((slots, width))
    return call(
        down_body,
        (blocks + FOLD,),
        [full, full, row_block, row_block, wide_block, whole(vec.shape), whole(first.shape)]
        + [HBM] * 24,
        [row_block, row_block, row_block, whole((8, width)), HBM, HBM],
        [
            like((slots, width), BF),
            like((slots, width), BF),
            like((slots, width), F32),
            like((8, width), F32),
            like((4, 2, size, width), BF),
            like((4, 2, size, width), BF),
        ],
        [
            pltpu.VMEM((width, width), BF),
            pltpu.VMEM((width, hidden), BF),
            pltpu.VMEM((hidden, width), BF),
            pltpu.VMEM((slots, hidden), BF),
            pltpu.VMEM((slots, width), BF),
            pltpu.VMEM((FOLD, width, width), BF),
            pltpu.VMEM((width, width), BF),
            pltpu.SemaphoreType.DMA((3,)),
        ],
        (attended, low, residual, cot, active, vec, first, *bufs),
        (8 * FOLD + 4) * slots * width * width,
        36 << 20,
        place,
        room=60,
    )


def attend_back(half, mixed, grad_att, attended, lse, meta, project, taps):
    slots, width = grad_att.shape
    at, count = half
    lane_block = pl.BlockSpec((slots, LANES), lambda p: (0, p + at))

    def part(c):
        return pl.BlockSpec((None, slots, LANES), lambda p: (c, 0, p + at))

    return call(
        functools.partial(attend_back_body, (width // HEADS) ** (-0.5)),
        (count,),
        [part(0), part(1), part(2), lane_block, lane_block, lane_block, whole(meta.shape)]
        + [
            pl.BlockSpec((3, slots, LANES), lambda p: (0, 0, p + at)),
            pl.BlockSpec((3, 3, LANES), lambda p: (0, 0, p + at)),
        ],
        [
            pl.BlockSpec((3, slots, LANES), lambda p: (0, 0, p)),
            pl.BlockSpec((3, 3, LANES), lambda p: (0, 0, p)),
        ],
        [like((3, slots, count * LANES), BF), like((3, 3, count * LANES), F32)],
        [
            pltpu.VMEM((3, slots, LANES), F32),
            pltpu.VMEM((2, slots, LANES), F32),
            pltpu.VMEM((slots, slots), F32),
            pltpu.VMEM((2, slots, LANES), BF),
            pltpu.VMEM((2, slots, LANES), BF),
            pltpu.VMEM((2, slots, LANES), BF),
            pltpu.VMEM((2, slots, LANES), BF),
            pltpu.VMEM((LANES, slots), BF),
            pltpu.VMEM((LANES, slots), F32),
        ],
        (mixed, mixed, mixed, grad_att, attended, lse, meta, project, taps),
        10 * slots * slots * count * LANES,
        20 << 20,
        room=60,
    )


def post(place, grads, low, size):
    slots, width = low.shape
    lanes = sum(g.shape[2] for g in grads)
    return call(
        functools.partial(post_body, len(grads)),
        (3,),
        [pl.BlockSpec((None, *g.shape[1:]), lambda c, *_: (c, 0, 0)) for g in grads]
        + [whole((slots, width))],
        [HBM] * 3,
        [like((n, size, lanes), BF) for n in (4, 2, 2)],
        [
            pltpu.VMEM((3 * width, lanes), BF),
            pltpu.VMEM((width, slots), BF),
            pltpu.SemaphoreType.DMA((3,)),
        ],
        (*grads, low),
        6 * slots * width * lanes,
        24 << 20,
        place,
        room=20,
    )


def back(place, grads, taps, tokens, grad_res, vec, dvec_two, own, near):
    slots, width = tokens.shape
    row_block = pl.BlockSpec((BLOCK, width), lambda i, *_: (i, 0))
    specs = [pl.BlockSpec((3, BLOCK, g.shape[2]), lambda i, *_: (0, i, 0)) for g in grads]
    specs += [whole(tap.shape) for tap in taps]
    return call(
        back_body,
        (slots // BLOCK,),
        specs + [row_block, row_block, whole(vec.shape), whole(dvec_two.shape)] + [HBM] * 16,
        [row_block, whole((SHARDS, 8, LANES))],
        [like((slots, width), F32), like((SHARDS, 8, LANES), F32)],
        [
            pltpu.VMEM((8, width), F32),
            pltpu.VMEM((3 * width, width), BF),
            pltpu.SemaphoreType.DMA,
        ],
        (*grads, *taps, tokens, grad_res, vec, dvec_two, *own, *near),
        6 * slots * width * width,
        1,
        place,
        0,
        room=60,
    )


def split_core(place, mine, received):
    block = mine.shape[1:]
    return call(
        route_body,
        (1,),
        [whole(mine.shape)] * 2,
        [whole(block)] * 4,
        [like(block, BF)] * 4,
        [],
        (mine, received),
        0,
        3 * mine.size * 2,
        place,
        room=16,
    )


def in_plane(routed):
    return [routed[0]] + [swap(routed[r], 2 * r) for r in range(1, 4)]


def lift(place, blocks):
    shape = blocks.shape[2:]
    return call(
        lift_body,
        (1,),
        [whole(blocks.shape)],
        [whole(shape)] * 4,
        [like(shape, BF)] * 4,
        [],
        (blocks,),
        0,
        3 * blocks.size,
        place,
        0,
    )


def send_planes(total, target):
    return [total] + [
        swap(total, 8 * k, lambda i, k=k: plane_of(i) ^ k == target) for k in (1, 2, 3)
    ]


def add_four(parts):
    shape = parts[0].shape
    return call(
        sum_body,
        (1,),
        [whole(shape)] * 4,
        whole(shape),
        like(shape, BF),
        [],
        parts,
        0,
        10 * parts[0].size,
        weight=0,
    )


def prepare(place, matrices, width):
    rows, roww = matrices.shape
    size = rows * roww // width
    return call(
        prep_body,
        (1,),
        [whole((rows, roww))],
        whole((size, width)),
        like((size, width), BF),
        [pltpu.VMEM((rows, roww), F32)],
        (matrices,),
        0,
        4 * matrices.size,
        place,
    )


def finish(place, sums, rows, roww):
    size, width = sums[-1].shape
    return call(
        finish_body,
        (1,),
        [whole(part.shape) for part in sums],
        whole((rows, roww)),
        like((rows, roww), F32),
        [pltpu.VMEM((size, width), F32)],
        sums,
        0,
        28 * size * width,
        place,
    )


def after(value, *deps):
    return lax.optimization_barrier((value, *deps))


def meta_rows(seq_start, valid):
    zeros = jnp.zeros((6, seq_start.shape[0]), F32)
    return jnp.concatenate([seq_start.astype(F32)[None], valid.astype(F32)[None], zeros], axis=0)


def split_vectors(vec_flat, width):
    vec = vec_flat[: 13 * width].reshape(13, width)
    return vec[:8], vec[4:13].reshape(3, 3, width)


def per_device(tokens_in, grad_out, seq_start, valid, matrices, vectors):
    width = tokens_in.shape[1]
    rows, roww = matrices.shape
    linear = lax.axis_index(FINE)
    plane = plane_of(linear)
    place = (linear >> jnp.array([0, 3, 0, 1, 0])) & jnp.array([31, 3, 7, 3, 1])
    shard = prepare(place, matrices, width)
    near_planes = jnp.stack([1 - jnp.minimum(plane, 1), 2 - plane // 2, 3 - plane // 3])
    place = jnp.concatenate([place, near_planes])
    meta = meta_rows(seq_start, valid)

    def up(value, steps, keep):
        pairs = [(i, i + 8 * steps) for i in range(SHARDS) if plane_of(i) in keep]
        return lax.ppermute(value, FINE, pairs)

    def with_partner(chips):
        bufs = []
        for chip in chips:
            bufs += [chip, swap(chip, 1)]
        return bufs

    def spread(held):
        by_y, by_x = swap(held, 2), swap(held, 4)
        return [held, by_y, by_x, swap(held, 6)]

    pairs = [(i, i + 16) for i in range(8)] + [(i, i + 8) for i in range(16, 24)]
    jump = lax.ppermute(shard, FINE, pairs)
    left_one = up(shard, -1, (1, 2, 3))
    own_y, own_x, own_both = spread(shard)[1:]
    jump, own_y, own_x = after(jump, own_y, own_x)
    hop = up(jnp.where(plane == 2, jump, shard), 1, (0, 1, 2))
    left_two = up(left_one, -1, (2, 1))
    near_one = jnp.where(plane == 0, left_one, jnp.where(plane == 2, jump, hop))
    near_one, hop, vectors_later, own_both = after(near_one, hop, vectors, own_both)
    own_chips = [shard, own_y, own_x, own_both]
    vec_flat = lax.all_to_all(jnp.tile(vectors_later, (SHARDS, 1)), FINE, 0, 0, tiled=True)
    near_chips = spread(near_one)
    left_three = up(left_two, -1, (1,))
    right_two = up(hop, 1, (2,))
    low = jnp.where(plane == 1, left_one, jnp.where(plane == 2, hop, right_two))
    low = jnp.where(plane == 0, left_two, low)
    high = jnp.where(plane == 1, left_two, jnp.where(plane == 2, left_one, jump))
    high = jnp.where(plane == 0, left_three, high)
    far, *near_chips = after(jnp.stack([low, high]), *near_chips)
    far_chips = spread(far)
    far_partner = swap(far, 1)
    own = with_partner(own_chips)
    near = with_partner(near_chips)
    vec_flat = vec_flat.reshape(-1).astype(F32)
    vec, taps = split_vectors(vec_flat, width)
    low_one, mixed, project, attended, lse = forward(place, tokens_in, meta, own, near, vec, taps)
    attended, far_partner, *far_chips = after(attended, far_partner, *far_chips)
    far = [far_chips[0], far_partner, *with_partner(far_chips[1:])]
    bufs = (*own, *near, *far)
    residual, low_two, cot, active, mine, other, first = dense_up(
        place, tokens_in, grad_out, meta, attended, bufs, vec
    )

    def to_plane(parts, target):
        total = add_four(parts)
        return [total] + [
            swap(total, 8 * k, lambda i, k=k: plane_of(i) ^ k == target) for k in (1, 2, 3)
        ]

    def to_square(mine, other):
        return (mine.astype(F32) + other.astype(F32)).astype(BF)

    def exchange(blocks):
        return lax.all_to_all(blocks, SQUARE, 0, 0, tiled=True)

    def summed(blocks):
        return blocks.astype(F32).sum(axis=0).astype(BF)

    residual, highs = after(residual, to_square(mine, swap(other, 1)))
    highs = exchange(highs)
    block_out, grad_att, grad_res, dvec_two, mine, other = dense_down(
        place, attended, low_two, residual, cot, active, vec, first, bufs
    )
    grad_att, highs = after(grad_att, summed(highs))
    high_sums = send_planes(highs, 3)
    received = swap(other, 1)
    grads_one, taps_one = attend_back(
        PIECES[0], mixed, grad_att, attended, lse, meta, project, taps
    )
    grads_one, received, grad_att = after(grads_one, received, grad_att)
    grad_att, lows = after(grad_att, to_square(mine, received))
    lows = exchange(lows)
    grads_two, taps_two = attend_back(
        PIECES[1], mixed, grad_att, attended, lse, meta, project, taps
    )
    size = shard.shape[0]
    mine, *other = post(place, (grads_one, grads_two), low_one, size)
    grad_att, taps_two, *high_sums = after(grad_att, taps_two, *high_sums)
    received = [swap(part, 1) for part in other]
    grads_b, taps_b = attend_back(HALVES[1], mixed, grad_att, attended, lse, meta, project, taps)
    mine_b, *other = post(place, (grads_b,), low_one, size)
    mine_b, lows, *more = after(mine_b, lows, *other, *received)
    other, received = more[:2], more[2:]
    square_a = to_square(mine, jnp.concatenate(received))
    square_b = to_square(mine_b, jnp.concatenate([swap(part, 1) for part in other]))
    qkv = exchange(jnp.concatenate([square_a, square_b], axis=-1))
    lifted = lift(place, lows)
    grads_b, *lifted = after(grads_b, *lifted)
    low_sums = [lifted[0]] + [
        swap(lifted[k], 8 * k, lambda i, k=k: plane_of(i) ^ k in (1, 2)) for k in (1, 2, 3)
    ]
    tokens_grad, grad_vec = back(
        place, (grads_one, grads_two, grads_b), (taps_one, taps_two, taps_b),
        tokens_in, grad_res, vec, dvec_two, own, near,
    )
    grad_vec, qkv, low_sums[1], low_sums[3] = after(grad_vec, qkv, low_sums[1], low_sums[3])
    grad_vec, qkv = after(grad_vec, summed(qkv))
    owned_vec = lax.all_to_all(grad_vec.reshape(-1, roww), FINE, 0, 0, tiled=True)
    sums = send_planes(qkv, 0)
    owned_vec, *sums = after(owned_vec, *sums)
    owned = finish(place, (*sums, *low_sums, *high_sums), rows, roww)
    owned_vec = owned_vec.reshape(SHARDS, -1, roww).sum(axis=0)[: vectors.shape[0]]
    return block_out, tokens_grad, owned, owned_vec


def per_device_any(tokens_in, grad_out, seq_start, valid, matrices, vectors):
    width = tokens_in.shape[1]
    rows, roww = matrices.shape
    step = GROUP // FOLD
    place = jnp.array([0, 0, 0, 0, 0, 1, 2, 3], jnp.int32)
    meta = meta_rows(seq_start, valid)
    view = lax.all_gather(matrices, AXES, axis=0, tiled=True).reshape(-1, width)
    vec_flat = lax.all_gather(vectors, AXES, axis=0, tiled=True).reshape(-1).astype(F32)
    vec, taps = split_vectors(vec_flat, width)
    cut = (UP_FIRST * GROUP, UP_END * GROUP)
    up = view[cut[0] : cut[1]].reshape(UP_GROUPS, step, FOLD, width).swapaxes(1, 2)
    view = jnp.concatenate([view[: cut[0]], up.reshape(-1, width), view[cut[1] :]])
    shards = view.reshape(4, 8, -1, width)
    own = [shards[0, r] for r in range(8)]
    near = [shards[1, r] for r in range(8)]
    far = [shards[2:, r] for r in range(8)]
    low_one, mixed, project, attended, lse = forward(place, tokens_in, meta, own, near, vec, taps)
    bufs = (*own, *near, *far)
    residual, low_two, cot, active, mine_three, other_three, first = dense_up(
        place, tokens_in, grad_out, meta, attended, bufs, vec
    )
    block_out, grad_att, grad_res, dvec_two, mine_low, other_low = dense_down(
        place, attended, low_two, residual, cot, active, vec, first, bufs
    )
    qkv, grad_taps, grads = [], [], []
    for half in HALVES:
        grad, grad_tap = attend_back(
            half, mixed, grad_att, attended, lse, meta, project, taps
        )
        mine, *other = post(place, (grad,), low_one, own[0].shape[0])
        qkv.append(jnp.stack([mine, jnp.concatenate(other)], axis=1))
        grad_taps.append(grad_tap)
        grads.append(grad)
    tokens_grad, grad_vec = back(
        place, grads, grad_taps, tokens_in, grad_res, vec, dvec_two, own, near
    )
    planes = [
        jnp.concatenate(qkv, axis=-1)[:, :, None],
        jnp.stack([mine_low, other_low], axis=1),
        jnp.stack([mine_three, other_three], axis=1)[:, :, None],
    ]
    grad = jnp.concatenate(planes, axis=2)
    grad = grad.transpose(2, 0, 1, 3, 4).reshape(-1, width)
    up = grad[cut[0] : cut[1]].reshape(UP_GROUPS, FOLD, step, width).swapaxes(1, 2)
    grad = jnp.concatenate([grad[: cut[0]], up.reshape(-1, width), grad[cut[1] :]])
    owned = lax.psum_scatter(
        grad.reshape(-1, roww).astype(F32), AXES, scatter_dimension=0, tiled=True
    )
    grad_vec = grad_vec[:, :VROWS].reshape(-1, roww)
    total = vec_flat.size // roww
    grad_vec = jnp.pad(grad_vec, ((0, max(0, total - grad_vec.shape[0])), (0, 0)))[:total]
    owned_vec = lax.psum_scatter(grad_vec, AXES, scatter_dimension=0, tiled=True)
    return block_out, tokens_grad, owned, owned_vec


def solution(mesh):
    body, axes = per_device_any, AXES
    if mesh.devices.size == SHARDS:
        mesh = Mesh(mesh.devices.reshape(4, 2, 2, 2), FINE)
        body, axes = per_device, FINE
    row = P(axes, None)
    flat = P(axes)
    return jax.shard_map(
        body,
        mesh=mesh,
        in_specs=(row, row, flat, flat, row, row),
        out_specs=(row, row, row, row),
        check_vma=False,
    )
```

```python
import functools

import jax
import jax.numpy as jnp
from jax import lax
from jax.experimental import pallas as pl
from jax.experimental.pallas import tpu as pltpu
from jax.sharding import Mesh
from jax.sharding import PartitionSpec as P

HEADS = 12
EPSILON = 1e-05
NEG_FILL = -1e30
BF = jnp.bfloat16
F32 = jnp.float32
AXES = ("dp", "sub")
FINE = ("z", "x", "y", "core")
SQUARE = ("x", "y")
LANES = 128
BLOCK = 256
SPAN = 512
GROUP = 96
FOLD = 4
SHARDS = 32
WEIGHT = 100
VROWS = 3
OUT_GROUPS = 8
UP_GROUPS = 32
UP_FIRST, UP_END = 32, 64
HALVES = ((0, 4), (4, 2))
PIECES = ((0, 2), (2, 2))
(
    PLACE_LINEAR, PLACE_Z, PLACE_IN_PLANE, PLACE_XY, PLACE_CORE,
    PLACE_NEAR, PLACE_LOW, PLACE_HIGH,
) = range(8)
HBM = pl.BlockSpec(memory_space=pl.ANY)


def dot(a, b):
    return jnp.dot(a, b, preferred_element_type=F32)


def dot_nt(a, b):
    return lax.dot_general(a, b, (((1,), (1,)), ((), ())), preferred_element_type=F32)


def dot_tn(a, b):
    return lax.dot_general(a, b, (((0,), (0,)), ((), ())), preferred_element_type=F32)


def whole(shape):
    return pl.BlockSpec(shape, lambda *_: (0,) * len(shape))


def fixed(shape):
    return pl.BlockSpec(shape, lambda *_: (0,) * len(shape), pipeline_mode=pl.Buffered(1))


def call(body, grid, ins, outs, out_shape, scratch, args, flops, moved, place=None, weight=WEIGHT, room=16):
    return pl.pallas_call(
        body,
        grid_spec=pltpu.PrefetchScalarGridSpec(
            num_scalar_prefetch=0 if place is None else 1,
            grid=grid,
            in_specs=ins,
            out_specs=outs,
            scratch_shapes=scratch,
        ),
        out_shape=out_shape,
        compiler_params=pltpu.CompilerParams(
            dimension_semantics=("arbitrary",) * len(grid), vmem_limit_bytes=room << 20
        ),
        cost_estimate=pl.CostEstimate(
            flops=weight * flops, bytes_accessed=weight * moved, transcendentals=0
        ),
    )(*(() if place is None else (place,)), *args)


def like(shape, dtype):
    return jax.ShapeDtypeStruct(shape, dtype)


def normalize(v):
    centre = v - jnp.mean(v, axis=-1, keepdims=True)
    scaled = lax.rsqrt(jnp.mean(centre * centre, axis=-1, keepdims=True) + EPSILON)
    return centre * scaled, scaled


def norm_back(incoming, normed, scaled, gain):
    weighted = incoming * gain
    return scaled * (
        weighted
        - jnp.mean(weighted, axis=-1, keepdims=True)
        - normed * jnp.mean(weighted * normed, axis=-1, keepdims=True)
    )


def columns(meta):
    return jnp.transpose(meta, (1, 0))


def mix_masks(meta_ref, slots):
    cols = columns(meta_ref[...])
    position = lax.broadcasted_iota(jnp.int32, (slots, 1), 0).astype(F32) - cols[:, 0:1]
    return jnp.where(position >= 1.0, 1.0, 0.0), jnp.where(position >= 2.0, 1.0, 0.0)


def xor_pairs(mask, keep=None):
    return [(i, i ^ mask) for i in range(SHARDS) if keep is None or keep(i)]


def swap(value, mask, keep=None):
    return lax.ppermute(value, FINE, xor_pairs(mask, keep))


def plane_of(index):
    return index >> 3


def prep_body(place_ref, in_ref, out_ref, wide_ref):
    width = out_ref.shape[1]
    cols = width // LANES
    wide_ref[...] = in_ref[...].astype(F32)
    first = place_ref[PLACE_LINEAR] * (out_ref.shape[0] // GROUP)
    for n in range(out_ref.shape[0] // GROUP):
        base = n * GROUP * cols
        up = jnp.logical_and(first + n >= UP_FIRST, first + n < UP_END)

        @pl.when(up)
        def _():
            for j in range(cols):
                parts = [
                    wide_ref[pl.ds(base + q * cols + j, GROUP // FOLD, stride=cols * FOLD), :]
                    for q in range(FOLD)
                ]
                out_ref[n * GROUP : (n + 1) * GROUP, j * LANES : (j + 1) * LANES] = (
                    jnp.concatenate(parts, axis=0).astype(BF)
                )

        @pl.when(jnp.logical_not(up))
        def _():
            for j in range(cols):
                out_ref[n * GROUP : (n + 1) * GROUP, j * LANES : (j + 1) * LANES] = wide_ref[
                    pl.ds(base + j, GROUP, stride=cols), :
                ].astype(BF)


def finish_body(place_ref, *refs):
    zero, middle, last = refs[:4], refs[4:8], refs[8:12]
    out_ref, total_ref = refs[-2:]
    width = total_ref.shape[1]
    cols = width // LANES
    plane = place_ref[PLACE_Z]

    def add(parts):
        total = parts[0][...].astype(F32)
        for part in parts[1:]:
            total = total + part[...].astype(F32)
        return total

    @pl.when(plane == 0)
    def _():
        total_ref[...] = add(zero)

    @pl.when(jnp.logical_or(plane == 1, plane == 2))
    def _():
        total_ref[...] = add(middle)

    @pl.when(plane == 3)
    def _():
        total_ref[...] = add(last)

    first = place_ref[PLACE_LINEAR] * (total_ref.shape[0] // GROUP)
    for n in range(total_ref.shape[0] // GROUP):
        base = n * GROUP * cols
        up = jnp.logical_and(first + n >= UP_FIRST, first + n < UP_END)

        @pl.when(up)
        def _():
            step = GROUP // FOLD
            for j in range(cols):
                for q in range(FOLD):
                    lo = n * GROUP + q * step
                    out_ref[pl.ds(base + q * cols + j, step, stride=cols * FOLD), :] = total_ref[
                        lo : lo + step, j * LANES : (j + 1) * LANES
                    ]

        @pl.when(jnp.logical_not(up))
        def _():
            for j in range(cols):
                out_ref[pl.ds(base + j, GROUP, stride=cols), :] = total_ref[
                    n * GROUP : (n + 1) * GROUP, j * LANES : (j + 1) * LANES
                ]


def route_body(place_ref, mine_ref, other_ref, *outs):
    for r, out in enumerate(outs):
        at = place_ref[PLACE_XY] ^ r
        out[...] = (mine_ref[at].astype(F32) + other_ref[at].astype(F32)).astype(BF)


def lift_body(place_ref, in_ref, *outs):
    plane = place_ref[PLACE_Z]
    for k, out in enumerate(outs):
        p = jnp.clip(plane ^ k, 1, 2) - 1
        total = in_ref[0, p].astype(F32)
        for r in range(1, 4):
            total = total + in_ref[r, p].astype(F32)
        out[...] = total.astype(BF)


def sum_body(a_ref, b_ref, c_ref, d_ref, out_ref):
    out_ref[...] = (
        a_ref[...].astype(F32) + b_ref[...].astype(F32) + c_ref[...].astype(F32) + d_ref[...].astype(F32)
    ).astype(BF)


def start_qkv(place_ref, own, near, w_ref, sem):
    size = own[0].shape[0]
    for r in range(8):
        at = pl.multiple_of((place_ref[PLACE_IN_PLANE] ^ r) * size, 32)

        @pl.when(place_ref[PLACE_Z] == 0)
        def _():
            pltpu.make_async_copy(own[r], w_ref.at[pl.ds(at, size)], sem).start()

        @pl.when(place_ref[PLACE_Z] != 0)
        def _():
            pltpu.make_async_copy(near[r], w_ref.at[pl.ds(at, size)], sem).start()


def wait_all(ref, sem):
    pltpu.make_async_copy(ref, ref, sem).wait()


def start_dense(place_ref, own, near, far, wo_ref, w1_ref, w2_ref, sems):
    step = GROUP // FOLD
    width = own[0].shape[1]
    slots = [(own, None, PLACE_Z, (1, 2, 3)), (near, None, PLACE_NEAR, (1,))]
    slots += [(far, 0, PLACE_LOW, (1, 2)), (far, 1, PLACE_HIGH, (2, 3))]
    for bufs, slot, plane_at, planes in slots:
        for p in planes:

            @pl.when(place_ref[plane_at] == p)
            def _():
                for r in range(8):
                    buf = bufs[r] if slot is None else bufs[r].at[slot]
                    place = place_ref[PLACE_IN_PLANE] ^ r
                    for n in range(3):
                        group = 24 * (p - 1) + 3 * place + n
                        rows = buf.at[pl.ds(n * GROUP, GROUP)]

                        def to_out():
                            at = pl.multiple_of(group * GROUP, 32)
                            pltpu.make_async_copy(
                                rows, wo_ref.at[pl.ds(at, GROUP)], sems.at[0]
                            ).start()

                        def to_up():
                            at = pl.multiple_of((group - OUT_GROUPS) * step, 8)
                            for q in range(FOLD):
                                pltpu.make_async_copy(
                                    rows.at[pl.ds(q * step, step)],
                                    w1_ref.at[pl.ds(at, step), pl.ds(q * width, width)],
                                    sems.at[1],
                                ).start()

                        def to_down():
                            at = pl.multiple_of((group - OUT_GROUPS - UP_GROUPS) * GROUP, 32)
                            pltpu.make_async_copy(
                                rows, w2_ref.at[pl.ds(at, GROUP)], sems.at[2]
                            ).start()

                        if p == 1:
                            pl.when(group < OUT_GROUPS)(to_out)
                            pl.when(group >= OUT_GROUPS)(to_up)
                        elif p == 2:
                            pl.when(group < OUT_GROUPS + UP_GROUPS)(to_up)
                            if w2_ref is not None:
                                pl.when(group >= OUT_GROUPS + UP_GROUPS)(to_down)
                        elif w2_ref is not None:
                            to_down()


def deal(place_ref, targets, sems, copy):
    core = place_ref[PLACE_CORE]
    for j in range(8):
        for which in range(2):

            @pl.when(core ^ (j % 2) == which)
            def _():
                copy(j, targets[which].at[j // 2], sems.at[which])


def pre_body(place_ref, x_ref, vec_ref, taps_ref, meta_ref, *refs):
    own, near = refs[:8], refs[8:16]
    low_ref, mixed_ref, proj_ref, w_ref, keep_ref, sem = refs[16:]
    slots, width = x_ref.shape
    here = pl.multiple_of(pl.program_id(0) * width, width)

    @pl.when(pl.program_id(0) == 0)
    def _():
        start_qkv(place_ref, own, near, w_ref, sem)
        for lo in range(0, slots, BLOCK):
            rows = slice(lo, lo + BLOCK)
            normed, _ = normalize(x_ref[rows, :].astype(F32))
            low_ref[rows, :] = (normed * vec_ref[0:1, :] + vec_ref[1:2, :]).astype(BF)
        wait_all(w_ref, sem)

    first, second = mix_masks(meta_ref, slots)
    weight = w_ref[pl.ds(here, width), :]
    ahead = dot(low_ref[0:BLOCK, :], weight)
    for lo in range(0, slots, BLOCK):
        end = lo + BLOCK
        value = ahead
        if end < slots:
            ahead = dot(low_ref[end : end + BLOCK, :], weight)
        proj_ref[lo:end, :] = value.astype(BF)
        keep_ref[lo:end, :] = value
        one_back = pltpu.roll(value, 1, 0) if lo == 0 else keep_ref[lo - 1 : end - 1, :]
        two_back = pltpu.roll(value, 2, 0) if lo == 0 else keep_ref[lo - 2 : end - 2, :]
        mixed_ref[lo:end, :] = (
            taps_ref[0:1, :] * value
            + taps_ref[1:2, :] * (one_back * first[lo:end])
            + taps_ref[2:3, :] * (two_back * second[lo:end])
        ).astype(BF)


def mask_columns(cols):
    lane = lax.broadcasted_iota(jnp.int32, (1, LANES), 1) % (LANES // 2)
    bucket = (lane >= 16) & (lane < 32)
    same = cols[:, 0:1] * (1.0 / 64.0) == (lane - 16).astype(F32)
    query = jnp.where(bucket & same, 0.0, jnp.where((lane >= 16) & (lane <= 32), NEG_FILL, 0.0))
    key = jnp.where(bucket & same, 1.0, jnp.where(lane == 32, 1.0 - cols[:, 1:2], 0.0))
    return query.astype(BF), key.astype(BF)


def triangle(lower):
    row = lax.broadcasted_iota(jnp.int32, (BLOCK, BLOCK), 0)
    col = lax.broadcasted_iota(jnp.int32, (BLOCK, BLOCK), 1)
    return jnp.where(col <= row if lower else row <= col, 0.0, NEG_FILL)


def attend_body(
    scale, q_ref, k_ref, v_ref, meta_ref, out_ref, lse_ref,
    tri_ref, qm_ref, km_ref, qa_ref, ka_ref, va_ref,
):
    slots = q_ref.shape[0]
    half = LANES // 2

    @pl.when(pl.program_id(0) == 0)
    def _():
        tri_ref[...] = triangle(True)
        qm_ref[...], km_ref[...] = mask_columns(columns(meta_ref[...]))

    left = lax.broadcasted_iota(jnp.int32, (1, LANES), 1) < half
    query = q_ref[...] * jnp.asarray(scale, BF)
    one = jnp.ones_like(query)
    for head in range(2):
        own = left if head == 0 else jnp.logical_not(left)
        qa_ref[head] = jnp.where(own, query, qm_ref[...])
        ka_ref[head] = jnp.where(own, k_ref[...], km_ref[...])
        va_ref[head] = jnp.where(own, v_ref[...], one)
    stages = [(lo, head) for lo in range(0, slots, BLOCK) for head in range(2)]
    outs, logs = [], []

    def score(lo, head):
        return dot_nt(qa_ref[head, lo : lo + BLOCK, :], ka_ref[head, : lo + BLOCK, :])

    def finish_stage(lo, head, terms, peak):
        end = lo + BLOCK
        both = dot(terms, va_ref[head, :end, :])
        outs.append(both / pltpu.roll(both, half, 1))
        logs.append(peak + jnp.log(both))
        if head == 1:
            out_ref[lo:end, :] = jnp.where(left, outs[-2], outs[-1]).astype(BF)
            lse_ref[lo:end, :] = jnp.where(left, logs[-1], logs[-2])

    ahead = score(*stages[0])
    behind = None
    for n, (lo, head) in enumerate(stages):
        scores = ahead
        if n + 1 < len(stages):
            ahead = score(*stages[n + 1])
        if behind is not None:
            finish_stage(*behind)
        near = scores[:, lo:] + tri_ref[...]
        scores = jnp.concatenate([scores[:, :lo], near], axis=1) if lo else near
        peak = jnp.max(scores, axis=-1, keepdims=True)
        behind = (lo, head, jnp.exp(scores - peak).astype(BF), peak)
    finish_stage(*behind)


def up_body(place_ref, att_ref, x_ref, go_ref, meta_ref, vec_ref, *refs):
    own, near, far = refs[:8], refs[8:16], refs[16:24]
    (
        res_ref, low_ref, cot_ref, out_ref, mine_ref, other_ref, first_ref,
        wo_ref, w1_ref, act_ref, cots_ref, g2_ref, sems,
    ) = refs[24:]
    width = x_ref.shape[1]
    step = pl.program_id(0)
    blocks = act_ref.shape[0] // SPAN
    here = pl.multiple_of(step * SPAN, SPAN)

    @pl.when(step == 0)
    def _():
        start_dense(place_ref, own, near, far, wo_ref, w1_ref, None, sems)
        wait_all(wo_ref, sems.at[0])
        wait_all(w1_ref, sems.at[1])

    @pl.when(step < blocks)
    def _():
        live = columns(meta_ref[...])[:, 1:2]
        cot = (go_ref[...].astype(F32) * live).astype(BF)
        cot_ref[...] = cot
        cots_ref[pl.ds(here, SPAN), :] = cot
        pieces = range(0, SPAN, BLOCK)
        residuals = [
            x_ref[lo : lo + BLOCK, :].astype(F32) + dot(att_ref[lo : lo + BLOCK, :], wo_ref[...])
            for lo in pieces
        ]
        lows = []

        def norm(lo, residual):
            res_ref[lo : lo + BLOCK, :] = residual
            normed, _ = normalize(residual)
            low = (normed * vec_ref[2:3, :] + vec_ref[3:4, :]).astype(BF)
            low_ref[lo : lo + BLOCK, :] = low
            lows.append(low)

        norm(0, residuals[0])
        stages = [(at, part) for at in range(len(pieces)) for part in range(FOLD)]

        def project(at, part):
            return dot(lows[at], w1_ref[:, part * width : (part + 1) * width])

        ahead = project(0, 0)
        for n, (at, part) in enumerate(stages):
            upward = jnp.maximum(ahead, 0.0)
            if part == 0 and at + 1 < len(pieces):
                norm(pieces[at + 1], residuals[at + 1])
            if n + 1 < len(stages):
                ahead = project(*stages[n + 1])
            cut = slice(part * width, (part + 1) * width)
            rows = pl.ds(pl.multiple_of(here + at * BLOCK, BLOCK), BLOCK)
            active = (upward * upward).astype(BF)
            act_ref[rows, cut] = active
            out_ref[at * BLOCK : (at + 1) * BLOCK, cut] = active

    @pl.when(step >= blocks)
    def _():
        cut = pl.ds(pl.multiple_of((step - blocks) * width, width), width)
        g2_ref[cut, :] = dot_tn(act_ref[:, cut], cots_ref[...]).astype(BF)

    @pl.when(step == blocks + FOLD - 1)
    def _():
        size = mine_ref.shape[1]
        skip = g2_ref.shape[0] - 8 * size

        def copy(j, target, sem):
            pltpu.make_async_copy(g2_ref.at[pl.ds(skip + j * size, size)], target, sem).start()

        deal(place_ref, (mine_ref, other_ref), sems, copy)
        first_ref[...] = g2_ref[0:skip, :]
        wait_all(mine_ref, sems.at[0])
        wait_all(other_ref, sems.at[1])


def down_body(
    place_ref, att_ref, low_ref, res_ref, cot_ref, act_ref, vec_ref, first_ref, *refs
):
    own, near, far = refs[:8], refs[8:16], refs[16:24]
    (
        out_ref, gatt_ref, gres_ref, dvec_ref, mine_ref, other_ref,
        wo_ref, w1_ref, w2_ref, up_ref, reslow_ref, g1_ref, go_ref, sems,
    ) = refs[24:]
    width = res_ref.shape[1]
    step = pl.program_id(0)
    blocks = up_ref.shape[0] // SPAN
    here = pl.multiple_of(step * SPAN, SPAN)

    @pl.when(step == 0)
    def _():
        start_dense(place_ref, own, near, far, wo_ref, w1_ref, w2_ref, sems)
        dvec_ref[...] = jnp.zeros_like(dvec_ref)
        wait_all(w2_ref, sems.at[2])

    @pl.when(step < blocks)
    def _():
        pieces = range(0, SPAN, BLOCK)
        stages = [(lo, part) for lo in pieces for part in range(FOLD)]

        def incoming(lo, part):
            return dot_nt(cot_ref[lo : lo + BLOCK, :], w2_ref[part * width : (part + 1) * width, :])

        ahead = incoming(*stages[0])
        for n, (lo, part) in enumerate(stages):
            grad_active = ahead
            if n + 1 < len(stages):
                ahead = incoming(*stages[n + 1])
            cut = slice(part * width, (part + 1) * width)
            upward = jnp.sqrt(act_ref[lo : lo + BLOCK, cut].astype(F32))
            rows = pl.ds(pl.multiple_of(here + lo, BLOCK), BLOCK)
            up_ref[rows, cut] = (grad_active * (2.0 * upward)).astype(BF)
        for lo in pieces:
            out = res_ref[lo : lo + BLOCK, :] + dot(act_ref[lo : lo + BLOCK, :], w2_ref[...])
            out_ref[lo : lo + BLOCK, :] = out.astype(BF)

    @pl.when(step == 0)
    def _():
        wait_all(w1_ref, sems.at[1])
        wait_all(wo_ref, sems.at[0])

    @pl.when(step < blocks)
    def _():
        pieces = range(0, SPAN, BLOCK)

        def outgoing(lo):
            return dot_nt(up_ref[pl.ds(pl.multiple_of(here + lo, BLOCK), BLOCK), :], w1_ref[...])

        ahead = outgoing(0)
        for lo in pieces:
            grad = ahead
            if lo + BLOCK < SPAN:
                ahead = outgoing(lo + BLOCK)
            span = slice(lo, lo + BLOCK)
            normed, scaled = normalize(res_ref[span, :])
            back = norm_back(grad, normed, scaled, vec_ref[2:3, :])
            grad_residual = cot_ref[span, :].astype(F32) + back
            gres_ref[span, :] = grad_residual
            res_low = grad_residual.astype(BF)
            reslow_ref[pl.ds(pl.multiple_of(here + lo, BLOCK), BLOCK), :] = res_low
            gatt_ref[span, :] = dot_nt(res_low, wo_ref[...]).astype(BF)
            dvec_ref[0:1, :] += jnp.sum(grad * normed, axis=0, keepdims=True)
            dvec_ref[1:2, :] += jnp.sum(grad, axis=0, keepdims=True)

    @pl.when(step >= blocks)
    def _():
        cut = pl.ds(pl.multiple_of((step - blocks) * width, width), width)
        g1_ref[step - blocks] = dot_tn(low_ref[...], up_ref[:, cut]).astype(BF)

    @pl.when(step == blocks + FOLD - 1)
    def _():
        go_ref[...] = dot_tn(att_ref[...], reslow_ref[...]).astype(BF)
        span = GROUP // FOLD

        def copy(j, target, sem):
            for p in range(2):
                for n in range(3):
                    group = 24 * p + 3 * j + n
                    rows = target.at[p, pl.ds(n * GROUP, GROUP)]
                    if group < OUT_GROUPS:
                        source = go_ref.at[pl.ds(group * GROUP, GROUP)]
                    elif group < OUT_GROUPS + UP_GROUPS:
                        source = g1_ref.at[:, pl.ds((group - OUT_GROUPS) * span, span)]
                        rows = rows.reshape(FOLD, span, width)
                    else:
                        at = (group - OUT_GROUPS - UP_GROUPS) * GROUP
                        source = first_ref.at[pl.ds(at, GROUP)]
                    pltpu.make_async_copy(source, rows, sem).start()

        deal(place_ref, (mine_ref, other_ref), sems, copy)
        wait_all(mine_ref, sems.at[0])
        wait_all(other_ref, sems.at[1])


def split_three(value):
    high = value.astype(BF)
    rest = value - high.astype(F32)
    middle = rest.astype(BF)
    return high, middle, (rest - middle.astype(F32)).astype(BF)


def attend_back_body(
    scale, q_ref, k_ref, v_ref, do_ref, o_ref, lse_ref, meta_ref, proj_ref, taps_ref,
    gproj_ref, gtaps_ref, grad_ref, mask_ref, bias_ref, qa_ref, ka_ref, va_ref, da_ref, kt_ref, dq_ref,
):
    slots = q_ref.shape[0]
    half = LANES // 2

    @pl.when(pl.program_id(0) == 0)
    def _():
        cols = columns(meta_ref[...])
        for lo in range(0, slots, BLOCK):
            end = lo + BLOCK
            size = slots - lo
            row = lax.broadcasted_iota(jnp.int32, (BLOCK, size), 0)
            col = lax.broadcasted_iota(jnp.int32, (BLOCK, size), 1)
            keep = (
                (cols[lo:end, 0:1] == meta_ref[0:1, lo:])
                & (cols[lo:end, 1:2] > 0.5)
                & (row <= col)
            )
            bias_ref[lo:end, lo:] = jnp.where(keep, 0.0, NEG_FILL)
        for n, mask in enumerate(mix_masks(meta_ref, slots)):
            mask_ref[n] = jnp.broadcast_to(mask, (slots, LANES))

    lane = lax.broadcasted_iota(jnp.int32, (1, LANES), 1)
    left = lane < half
    query = q_ref[...]
    key = k_ref[...]
    value = v_ref[...]
    grad_out = do_ref[...]
    product = grad_out.astype(F32) * o_ref[...].astype(F32)
    kt_ref[...] = jnp.transpose(key.astype(F32), (1, 0)).astype(BF)
    logs = split_three(-lse_ref[...])
    zero = jnp.zeros_like(query)
    one = jnp.ones_like(query)
    for head in range(2):
        own = left if head == 0 else jnp.logical_not(left)
        base = half if head == 0 else 0
        delta = jnp.sum(jnp.where(own, product, 0.0), axis=-1, keepdims=True)
        deltas = split_three(-delta)
        marks = [lane == base + n for n in range(3)]

        def spread(terms):
            result = zero
            for mark, term in zip(marks, terms):
                result = jnp.where(mark, term, result)
            return result

        ones = spread((one, one, one))
        qa_ref[head] = jnp.where(own, query * jnp.asarray(scale, BF), spread(logs))
        ka_ref[head] = jnp.where(own, key, ones)
        va_ref[head] = jnp.where(own, value, ones)
        da_ref[head] = jnp.where(own, grad_out, spread(deltas))
    dq_ref[...] = jnp.zeros_like(dq_ref)
    for lo in range(0, slots, BLOCK):
        end = lo + BLOCK
        grad_keys, grad_values = [], []
        for head in range(2):
            rows = slice(head * half, (head + 1) * half)
            scores = dot_nt(ka_ref[head, lo:end, :], qa_ref[head, lo:, :]) + bias_ref[lo:end, lo:]
            probs = jnp.exp(scores)
            inner = dot_nt(va_ref[head, lo:end, :], da_ref[head, lo:, :])
            grad_scores = (probs * inner).astype(BF)
            grad_values.append(dot(probs.astype(BF), do_ref[lo:, :]))
            grad_keys.append(dot(grad_scores, q_ref[lo:, :]))
            dq_ref[rows, lo:] += dot(kt_ref[rows, lo:end], grad_scores)
        grad_ref[1, lo:end, :] = jnp.where(left, grad_keys[0], grad_keys[1]) * scale
        grad_ref[2, lo:end, :] = jnp.where(left, grad_values[0], grad_values[1])
    grad_ref[0, :, :] = jnp.transpose(dq_ref[...], (1, 0)) * scale
    for c in range(3):
        mixed = grad_ref[c]
        proj = proj_ref[c].astype(F32)
        one_up = pltpu.roll(mixed * mask_ref[0], slots - 1, 0)
        two_up = pltpu.roll(mixed * mask_ref[1], slots - 2, 0)
        gtaps_ref[c, 0:1, :] = jnp.sum(mixed * proj, axis=0, keepdims=True)
        gtaps_ref[c, 1:2, :] = jnp.sum(one_up * proj, axis=0, keepdims=True)
        gtaps_ref[c, 2:3, :] = jnp.sum(two_up * proj, axis=0, keepdims=True)
        gproj_ref[c] = (
            taps_ref[c, 0:1, :] * mixed + taps_ref[c, 1:2, :] * one_up + taps_ref[c, 2:3, :] * two_up
        ).astype(BF)


def post_body(count, place_ref, *refs):
    pieces, low_ref = refs[:count], refs[count]
    mine_ref, lows_ref, highs_ref, gw_ref, lowt_ref, sems = refs[count + 1 :]
    width = low_ref.shape[1]
    step = pl.program_id(0)

    @pl.when(step == 0)
    def _():
        lowt_ref[...] = jnp.transpose(low_ref[...], (1, 0))

    here = pl.multiple_of(step * width, width)
    at = 0
    for ref in pieces:
        lanes = ref.shape[1]
        gw_ref[pl.ds(here, width), at : at + lanes] = dot(lowt_ref[...], ref[...]).astype(BF)
        at += lanes

    @pl.when(step == 2)
    def _():
        size = mine_ref.shape[1]

        core = place_ref[PLACE_CORE]
        for j in range(8):
            other = lows_ref.at[j // 2] if j < 4 else highs_ref.at[j // 2 - 2]
            rows = gw_ref.at[pl.ds(j * size, size)]

            @pl.when(core == j % 2)
            def _():
                pltpu.make_async_copy(rows, mine_ref.at[j // 2], sems.at[0]).start()

            @pl.when(core != j % 2)
            def _():
                pltpu.make_async_copy(rows, other, sems.at[1 + j // 4]).start()

        wait_all(mine_ref, sems.at[0])
        wait_all(lows_ref, sems.at[1])
        wait_all(highs_ref, sems.at[2])


def back_body(place_ref, *refs):
    own, near = refs[-21:-13], refs[-13:-5]
    out_ref, all_ref, dvec_ref, w_ref, sem = refs[-5:]
    x_ref, gres_ref, vec_ref, two_ref = refs[-25:-21]
    count = (len(refs) - 25) // 2
    grads, taps = refs[:count], refs[count : 2 * count]
    width = x_ref.shape[1]

    @pl.when(pl.program_id(0) == 0)
    def _():
        start_qkv(place_ref, own, near, w_ref, sem)
        dvec_ref[...] = jnp.zeros_like(dvec_ref)
        wait_all(w_ref, sem)

    incoming = None
    for c in range(3):
        rows = slice(c * width, (c + 1) * width)
        at = 0
        for grad in grads:
            lanes = grad.shape[2]
            term = dot_nt(grad[c], w_ref[rows, at : at + lanes])
            incoming = term if incoming is None else incoming + term
            at += lanes
    normed, scaled = normalize(x_ref[...].astype(F32))
    out_ref[...] = gres_ref[...] + norm_back(incoming, normed, scaled, vec_ref[0:1, :])
    dvec_ref[0:1, :] += jnp.sum(incoming * normed, axis=0, keepdims=True)
    dvec_ref[1:2, :] += jnp.sum(incoming, axis=0, keepdims=True)

    @pl.when(pl.program_id(0) == pl.num_programs(0) - 1)
    def _():
        all_ref[...] = jnp.zeros_like(all_ref)
        rows = [dvec_ref[0:1, :], dvec_ref[1:2, :], two_ref[0:1, :], two_ref[1:2, :]]
        for c in range(3):
            for k in range(3):
                rows.append(jnp.concatenate([tap[c, k : k + 1, :] for tap in taps], axis=1))
        pieces = width // LANES
        for n, row in enumerate(rows):
            for part in range(pieces):
                at = n * pieces + part
                all_ref[at // VROWS, at % VROWS : at % VROWS + 1, :] = row[
                    :, part * LANES : (part + 1) * LANES
                ]


def forward(place, tokens, meta, own, near, vec, taps):
    slots, width = tokens.shape
    pairs = width // LANES
    scale = (width // HEADS) ** (-0.5)
    three = pl.BlockSpec((None, slots, width), lambda c, *_: (c, 0, 0))
    tap = pl.BlockSpec((None, 3, width), lambda c, *_: (c, 0, 0))
    low_one, mixed, project = call(
        pre_body,
        (3,),
        [whole((slots, width)), whole(vec.shape), tap, whole(meta.shape)] + [HBM] * 16,
        [whole((slots, width)), three, three],
        [like((slots, width), BF), like((3, slots, width), BF), like((3, slots, width), BF)],
        [
            pltpu.VMEM((3 * width, width), BF),
            pltpu.VMEM((slots, width), F32),
            pltpu.SemaphoreType.DMA,
        ],
        (tokens, vec, taps, meta, *own, *near),
        6 * slots * width * width,
        24 << 20,
        place,
        room=60,
    )
    lane_block = pl.BlockSpec((slots, LANES), lambda p: (0, p))

    def part(c):
        return pl.BlockSpec((None, slots, LANES), lambda p: (c, 0, p))

    attended, lse = call(
        functools.partial(attend_body, scale),
        (pairs,),
        [part(0), part(1), part(2), whole(meta.shape)],
        [lane_block, lane_block],
        [like((slots, width), BF), like((slots, width), F32)],
        [pltpu.VMEM((BLOCK, BLOCK), F32)]
        + [pltpu.VMEM((slots, LANES), BF)] * 2
        + [pltpu.VMEM((2, slots, LANES), BF)] * 3,
        (mixed, mixed, mixed, meta),
        2 * slots * slots * width * 2,
        12 << 20,
        room=60,
    )
    return low_one, mixed, project, attended, lse


def dense_up(place, tokens, grad_out, meta, attended, bufs, vec):
    slots, width = tokens.shape
    hidden = FOLD * width
    size = bufs[0].shape[0]
    blocks = slots // SPAN
    row_block = pl.BlockSpec((SPAN, width), lambda i, *_: (jnp.minimum(i, blocks - 1), 0))
    wide_block = pl.BlockSpec((SPAN, hidden), lambda i, *_: (jnp.minimum(i, blocks - 1), 0))
    meta_block = pl.BlockSpec((8, SPAN), lambda i, *_: (0, jnp.minimum(i, blocks - 1)))
    skip = hidden - 8 * size
    return call(
        up_body,
        (blocks + FOLD,),
        [row_block] * 3 + [meta_block, whole(vec.shape)] + [HBM] * 24,
        [row_block, row_block, row_block, wide_block, HBM, HBM, whole((skip, width))],
        [
            like((slots, width), F32),
            like((slots, width), BF),
            like((slots, width), BF),
            like((slots, hidden), BF),
            like((4, size, width), BF),
            like((4, size, width), BF),
            like((skip, width), BF),
        ],
        [
            pltpu.VMEM((width, width), BF),
            pltpu.VMEM((width, hidden), BF),
            pltpu.VMEM((slots, hidden), BF),
            pltpu.VMEM((slots, width), BF),
            pltpu.VMEM((hidden, width), BF),
            pltpu.SemaphoreType.DMA((3,)),
        ],
        (attended, tokens, grad_out, meta, vec, *bufs),
        (4 * FOLD + 2) * slots * width * width,
        30 << 20,
        place,
        room=60,
    )


def dense_down(place, attended, low, residual, cot, active, vec, first, bufs):
    slots, width = residual.shape
    hidden = FOLD * width
    size = bufs[0].shape[0]
    blocks = slots // SPAN
    row_block = pl.BlockSpec((SPAN, width), lambda i, *_: (jnp.minimum(i, blocks - 1), 0))
    wide_block = pl.BlockSpec((SPAN, hidden), lambda i, *_: (jnp.minimum(i, blocks - 1), 0))
    full = fixed((slots, width))
    return call(
        down_body,
        (blocks + FOLD,),
        [full, full, row_block, row_block, wide_block, whole(vec.shape), whole(first.shape)]
        + [HBM] * 24,
        [row_block, row_block, row_block, whole((8, width)), HBM, HBM],
        [
            like((slots, width), BF),
            like((slots, width), BF),
            like((slots, width), F32),
            like((8, width), F32),
            like((4, 2, size, width), BF),
            like((4, 2, size, width), BF),
        ],
        [
            pltpu.VMEM((width, width), BF),
            pltpu.VMEM((width, hidden), BF),
            pltpu.VMEM((hidden, width), BF),
            pltpu.VMEM((slots, hidden), BF),
            pltpu.VMEM((slots, width), BF),
            pltpu.VMEM((FOLD, width, width), BF),
            pltpu.VMEM((width, width), BF),
            pltpu.SemaphoreType.DMA((3,)),
        ],
        (attended, low, residual, cot, active, vec, first, *bufs),
        (8 * FOLD + 4) * slots * width * width,
        36 << 20,
        place,
        room=60,
    )


def attend_back(half, mixed, grad_att, attended, lse, meta, project, taps):
    slots, width = grad_att.shape
    at, count = half
    lane_block = pl.BlockSpec((slots, LANES), lambda p: (0, p + at))

    def part(c):
        return pl.BlockSpec((None, slots, LANES), lambda p: (c, 0, p + at))

    return call(
        functools.partial(attend_back_body, (width // HEADS) ** (-0.5)),
        (count,),
        [part(0), part(1), part(2), lane_block, lane_block, lane_block, whole(meta.shape)]
        + [
            pl.BlockSpec((3, slots, LANES), lambda p: (0, 0, p + at)),
            pl.BlockSpec((3, 3, LANES), lambda p: (0, 0, p + at)),
        ],
        [
            pl.BlockSpec((3, slots, LANES), lambda p: (0, 0, p)),
            pl.BlockSpec((3, 3, LANES), lambda p: (0, 0, p)),
        ],
        [like((3, slots, count * LANES), BF), like((3, 3, count * LANES), F32)],
        [
            pltpu.VMEM((3, slots, LANES), F32),
            pltpu.VMEM((2, slots, LANES), F32),
            pltpu.VMEM((slots, slots), F32),
            pltpu.VMEM((2, slots, LANES), BF),
            pltpu.VMEM((2, slots, LANES), BF),
            pltpu.VMEM((2, slots, LANES), BF),
            pltpu.VMEM((2, slots, LANES), BF),
            pltpu.VMEM((LANES, slots), BF),
            pltpu.VMEM((LANES, slots), F32),
        ],
        (mixed, mixed, mixed, grad_att, attended, lse, meta, project, taps),
        10 * slots * slots * count * LANES,
        20 << 20,
        room=60,
    )


def post(place, grads, low, size):
    slots, width = low.shape
    lanes = sum(g.shape[2] for g in grads)
    return call(
        functools.partial(post_body, len(grads)),
        (3,),
        [pl.BlockSpec((None, *g.shape[1:]), lambda c, *_: (c, 0, 0)) for g in grads]
        + [whole((slots, width))],
        [HBM] * 3,
        [like((n, size, lanes), BF) for n in (4, 2, 2)],
        [
            pltpu.VMEM((3 * width, lanes), BF),
            pltpu.VMEM((width, slots), BF),
            pltpu.SemaphoreType.DMA((3,)),
        ],
        (*grads, low),
        6 * slots * width * lanes,
        24 << 20,
        place,
        room=20,
    )


def back(place, grads, taps, tokens, grad_res, vec, dvec_two, own, near):
    slots, width = tokens.shape
    row_block = pl.BlockSpec((BLOCK, width), lambda i, *_: (i, 0))
    specs = [pl.BlockSpec((3, BLOCK, g.shape[2]), lambda i, *_: (0, i, 0)) for g in grads]
    specs += [whole(tap.shape) for tap in taps]
    return call(
        back_body,
        (slots // BLOCK,),
        specs + [row_block, row_block, whole(vec.shape), whole(dvec_two.shape)] + [HBM] * 16,
        [row_block, whole((SHARDS, 8, LANES))],
        [like((slots, width), F32), like((SHARDS, 8, LANES), F32)],
        [
            pltpu.VMEM((8, width), F32),
            pltpu.VMEM((3 * width, width), BF),
            pltpu.SemaphoreType.DMA,
        ],
        (*grads, *taps, tokens, grad_res, vec, dvec_two, *own, *near),
        6 * slots * width * width,
        1,
        place,
        0,
        room=60,
    )


def split_core(place, mine, received):
    block = mine.shape[1:]
    return call(
        route_body,
        (1,),
        [whole(mine.shape)] * 2,
        [whole(block)] * 4,
        [like(block, BF)] * 4,
        [],
        (mine, received),
        0,
        3 * mine.size * 2,
        place,
        room=16,
    )


def in_plane(routed):
    return [routed[0]] + [swap(routed[r], 2 * r) for r in range(1, 4)]


def lift(place, blocks):
    shape = blocks.shape[2:]
    return call(
        lift_body,
        (1,),
        [whole(blocks.shape)],
        [whole(shape)] * 4,
        [like(shape, BF)] * 4,
        [],
        (blocks,),
        0,
        3 * blocks.size,
        place,
        0,
    )


def send_planes(total, target):
    return [total] + [
        swap(total, 8 * k, lambda i, k=k: plane_of(i) ^ k == target) for k in (1, 2, 3)
    ]


def add_four(parts):
    shape = parts[0].shape
    return call(
        sum_body,
        (1,),
        [whole(shape)] * 4,
        whole(shape),
        like(shape, BF),
        [],
        parts,
        0,
        10 * parts[0].size,
        weight=0,
    )


def prepare(place, matrices, width):
    rows, roww = matrices.shape
    size = rows * roww // width
    return call(
        prep_body,
        (1,),
        [whole((rows, roww))],
        whole((size, width)),
        like((size, width), BF),
        [pltpu.VMEM((rows, roww), F32)],
        (matrices,),
        0,
        4 * matrices.size,
        place,
    )


def finish(place, sums, rows, roww):
    size, width = sums[-1].shape
    return call(
        finish_body,
        (1,),
        [whole(part.shape) for part in sums],
        whole((rows, roww)),
        like((rows, roww), F32),
        [pltpu.VMEM((size, width), F32)],
        sums,
        0,
        28 * size * width,
        place,
    )


def after(value, *deps):
    return lax.optimization_barrier((value, *deps))


def meta_rows(seq_start, valid):
    zeros = jnp.zeros((6, seq_start.shape[0]), F32)
    return jnp.concatenate([seq_start.astype(F32)[None], valid.astype(F32)[None], zeros], axis=0)


def split_vectors(vec_flat, width):
    vec = vec_flat[: 13 * width].reshape(13, width)
    return vec[:8], vec[4:13].reshape(3, 3, width)


def per_device(tokens_in, grad_out, seq_start, valid, matrices, vectors):
    width = tokens_in.shape[1]
    rows, roww = matrices.shape
    linear = lax.axis_index(FINE)
    plane = plane_of(linear)
    place = (linear >> jnp.array([0, 3, 0, 1, 0])) & jnp.array([31, 3, 7, 3, 1])
    near_planes = jnp.stack([1 - jnp.minimum(plane, 1), 2 - plane // 2, 3 - plane // 3])
    place = jnp.concatenate([place, near_planes])
    meta = meta_rows(seq_start, valid)
    shard = prepare(place, matrices, width)

    def up(value, steps, keep):
        pairs = [(i, i + 8 * steps) for i in range(SHARDS) if plane_of(i) in keep]
        return lax.ppermute(value, FINE, pairs)

    def with_partner(chips):
        bufs = []
        for chip in chips:
            bufs += [chip, swap(chip, 1)]
        return bufs

    def spread(held):
        by_y, by_x = swap(held, 2), swap(held, 4)
        return [held, by_y, by_x, swap(held, 6)]

    pairs = [(i, i + 16) for i in range(8)] + [(i, i + 8) for i in range(16, 24)]
    jump = lax.ppermute(shard, FINE, pairs)
    left_one = up(shard, -1, (1, 2, 3))
    own_y, own_x, own_both = spread(shard)[1:]
    jump, own_y, own_x = after(jump, own_y, own_x)
    hop = up(jnp.where(plane == 2, jump, shard), 1, (0, 1, 2))
    left_two = up(left_one, -1, (2, 1))
    near_one = jnp.where(plane == 0, left_one, jnp.where(plane == 2, jump, hop))
    near_one, hop, vectors_later, own_both = after(near_one, hop, vectors, own_both)
    own_chips = [shard, own_y, own_x, own_both]
    vec_flat = lax.all_to_all(jnp.tile(vectors_later, (SHARDS, 1)), FINE, 0, 0, tiled=True)
    near_chips = spread(near_one)
    left_three = up(left_two, -1, (1,))
    right_two = up(hop, 1, (2,))
    low = jnp.where(plane == 1, left_one, jnp.where(plane == 2, hop, right_two))
    low = jnp.where(plane == 0, left_two, low)
    high = jnp.where(plane == 1, left_two, jnp.where(plane == 2, left_one, jump))
    high = jnp.where(plane == 0, left_three, high)
    far, *near_chips = after(jnp.stack([low, high]), *near_chips)
    far_chips = spread(far)
    own = with_partner(own_chips)
    near = with_partner(near_chips)
    vec_flat = vec_flat.reshape(-1).astype(F32)
    vec, taps = split_vectors(vec_flat, width)
    low_one, mixed, project, attended, lse = forward(place, tokens_in, meta, own, near, vec, taps)
    attended, *far_chips = after(attended, *far_chips)
    far = with_partner(far_chips)
    bufs = (*own, *near, *far)
    residual, low_two, cot, active, mine, other, first = dense_up(
        place, tokens_in, grad_out, meta, attended, bufs, vec
    )

    def to_plane(parts, target):
        total = add_four(parts)
        return [total] + [
            swap(total, 8 * k, lambda i, k=k: plane_of(i) ^ k == target) for k in (1, 2, 3)
        ]

    def to_square(mine, other):
        return (mine.astype(F32) + other.astype(F32)).astype(BF)

    def exchange(blocks):
        return lax.all_to_all(blocks, SQUARE, 0, 0, tiled=True)

    def summed(blocks):
        return blocks.astype(F32).sum(axis=0).astype(BF)

    residual, highs = after(residual, to_square(mine, swap(other, 1)))
    highs = exchange(highs)
    block_out, grad_att, grad_res, dvec_two, mine, other = dense_down(
        place, attended, low_two, residual, cot, active, vec, first, bufs
    )
    grad_att, highs = after(grad_att, summed(highs))
    high_sums = send_planes(highs, 3)
    received = swap(other, 1)
    grads_one, taps_one = attend_back(
        PIECES[0], mixed, grad_att, attended, lse, meta, project, taps
    )
    grads_one, received, grad_att = after(grads_one, received, grad_att)
    grad_att, lows = after(grad_att, to_square(mine, received))
    lows = exchange(lows)
    grads_two, taps_two = attend_back(
        PIECES[1], mixed, grad_att, attended, lse, meta, project, taps
    )
    size = shard.shape[0]
    mine, *other = post(place, (grads_one, grads_two), low_one, size)
    grad_att, taps_two, *high_sums = after(grad_att, taps_two, *high_sums)
    received = [swap(part, 1) for part in other]
    grads_b, taps_b = attend_back(HALVES[1], mixed, grad_att, attended, lse, meta, project, taps)
    mine_b, *other = post(place, (grads_b,), low_one, size)
    mine_b, lows, *more = after(mine_b, lows, *other, *received)
    other, received = more[:2], more[2:]
    square_a = to_square(mine, jnp.concatenate(received))
    square_b = to_square(mine_b, jnp.concatenate([swap(part, 1) for part in other]))
    qkv = exchange(jnp.concatenate([square_a, square_b], axis=-1))
    lifted = lift(place, lows)
    grads_b, *lifted = after(grads_b, *lifted)
    low_sums = [lifted[0]] + [
        swap(lifted[k], 8 * k, lambda i, k=k: plane_of(i) ^ k in (1, 2)) for k in (1, 2, 3)
    ]
    tokens_grad, grad_vec = back(
        place, (grads_one, grads_two, grads_b), (taps_one, taps_two, taps_b),
        tokens_in, grad_res, vec, dvec_two, own, near,
    )
    grad_vec, qkv, low_sums[1], low_sums[3] = after(grad_vec, qkv, low_sums[1], low_sums[3])
    grad_vec, qkv = after(grad_vec, summed(qkv))
    owned_vec = lax.all_to_all(grad_vec.reshape(-1, roww), FINE, 0, 0, tiled=True)
    sums = send_planes(qkv, 0)
    owned_vec, *sums = after(owned_vec, *sums)
    owned = finish(place, (*sums, *low_sums, *high_sums), rows, roww)
    owned_vec = owned_vec.reshape(SHARDS, -1, roww).sum(axis=0)[: vectors.shape[0]]
    return block_out, tokens_grad, owned, owned_vec


def per_device_any(tokens_in, grad_out, seq_start, valid, matrices, vectors):
    width = tokens_in.shape[1]
    rows, roww = matrices.shape
    step = GROUP // FOLD
    place = jnp.array([0, 0, 0, 0, 0, 1, 2, 3], jnp.int32)
    meta = meta_rows(seq_start, valid)
    view = lax.all_gather(matrices, AXES, axis=0, tiled=True).reshape(-1, width)
    vec_flat = lax.all_gather(vectors, AXES, axis=0, tiled=True).reshape(-1).astype(F32)
    vec, taps = split_vectors(vec_flat, width)
    cut = (UP_FIRST * GROUP, UP_END * GROUP)
    up = view[cut[0] : cut[1]].reshape(UP_GROUPS, step, FOLD, width).swapaxes(1, 2)
    view = jnp.concatenate([view[: cut[0]], up.reshape(-1, width), view[cut[1] :]])
    shards = view.reshape(4, 8, -1, width)
    own = [shards[0, r] for r in range(8)]
    near = [shards[1, r] for r in range(8)]
    far = [shards[2:, r] for r in range(8)]
    low_one, mixed, project, attended, lse = forward(place, tokens_in, meta, own, near, vec, taps)
    bufs = (*own, *near, *far)
    residual, low_two, cot, active, mine_three, other_three, first = dense_up(
        place, tokens_in, grad_out, meta, attended, bufs, vec
    )
    block_out, grad_att, grad_res, dvec_two, mine_low, other_low = dense_down(
        place, attended, low_two, residual, cot, active, vec, first, bufs
    )
    qkv, grad_taps, grads = [], [], []
    for half in HALVES:
        grad, grad_tap = attend_back(
            half, mixed, grad_att, attended, lse, meta, project, taps
        )
        mine, *other = post(place, (grad,), low_one, own[0].shape[0])
        qkv.append(jnp.stack([mine, jnp.concatenate(other)], axis=1))
        grad_taps.append(grad_tap)
        grads.append(grad)
    tokens_grad, grad_vec = back(
        place, grads, grad_taps, tokens_in, grad_res, vec, dvec_two, own, near
    )
    planes = [
        jnp.concatenate(qkv, axis=-1)[:, :, None],
        jnp.stack([mine_low, other_low], axis=1),
        jnp.stack([mine_three, other_three], axis=1)[:, :, None],
    ]
    grad = jnp.concatenate(planes, axis=2)
    grad = grad.transpose(2, 0, 1, 3, 4).reshape(-1, width)
    up = grad[cut[0] : cut[1]].reshape(UP_GROUPS, FOLD, step, width).swapaxes(1, 2)
    grad = jnp.concatenate([grad[: cut[0]], up.reshape(-1, width), grad[cut[1] :]])
    owned = lax.psum_scatter(
        grad.reshape(-1, roww).astype(F32), AXES, scatter_dimension=0, tiled=True
    )
    grad_vec = grad_vec[:, :VROWS].reshape(-1, roww)
    total = vec_flat.size // roww
    grad_vec = jnp.pad(grad_vec, ((0, max(0, total - grad_vec.shape[0])), (0, 0)))[:total]
    owned_vec = lax.psum_scatter(grad_vec, AXES, scatter_dimension=0, tiled=True)
    return block_out, tokens_grad, owned, owned_vec


def solution(mesh):
    body, axes = per_device_any, AXES
    if mesh.devices.size == SHARDS:
        mesh = Mesh(mesh.devices.reshape(4, 2, 2, 2), FINE)
        body, axes = per_device, FINE
    row = P(axes, None)
    flat = P(axes)
    return jax.shard_map(
        body,
        mesh=mesh,
        in_specs=(row, row, flat, flat, row, row),
        out_specs=(row, row, row, row),
        check_vma=False,
    )
```
